32 devices in a mesh: rep: 2 (over x), sp: 16 (over z, y, core).
Axes of the slice: x: 2, y: 2, z: 4, core: 2. Of those that a mesh axis runs over, the one named last changes fastest.
Arguments:
- volume: bfloat16 [128, 16, 16, 128], P(('rep', 'sp')), parts along dimension 0, may hold values from -6 to 6
- first_kernel: bfloat16 [3, 3, 3, 128, 128], replicated, may hold values from -0.15625 to 0.15625
- second_kernel: bfloat16 [3, 3, 3, 128, 256], replicated, may hold values from -0.15625 to 0.15625
- deep_kernel: bfloat16 [3, 3, 3, 256, 512], P(None, None, None, None, 'sp'), may hold values from -0.109375 to 0.109375
- deeper_kernel: bfloat16 [3, 3, 3, 512, 512], P(None, None, None, None, 'sp'), may hold values from -0.078125 to 0.078125
- rise_kernel: bfloat16 [2, 2, 2, 512, 256], replicated, may hold values from -0.375 to 0.375
- decode_kernel: bfloat16 [3, 3, 3, 512, 256], P(None, None, None, 'sp'), may hold values from -0.078125 to 0.078125
- final_kernel: bfloat16 [2, 2, 2, 256, 128], replicated, may hold values from -0.5 to 0.5
Outputs:
- segmented: bfloat16 [128, 16, 16, 128], P(('rep', 'sp')), parts along dimension 0
The draws below stay inside these ranges and needn't reach their ends.
There are 2 independent parts, one for each index of `rep`. The reference program is written for one: setup_inputs(seed, part) draws one part's arguments, and reference() takes and returns one part's arrays. A program takes and returns all parts, laid end to end along the dimension named above; an argument that names none is the same for every part. Nothing has to cross between parts.
All inputs are finite; a program needn't handle non-finite values.
Results may differ from the reference program's by a relative error of at most 0.015.
Values may be sent and summed in bfloat16 or wider, within the bound.
A program may use at most 64 MiB of HBM per device.

```python
import jax
import jax.numpy as jnp
from jax import lax

C1 = 128
C2 = 256
C3 = 512
HT = 16
WD = 16
DEPTH = 64


def draw_volume(key, part):
    fine_key = jax.random.fold_in(key, 11)
    coarse_key = jax.random.fold_in(key, 23)
    coarse_shape = (DEPTH // 4, HT // 4, WD // 4, C1)
    fine = 0.6 * jax.random.normal(fine_key, (DEPTH, HT, WD, C1), jnp.float32)
    coarse = 1.4 * jax.random.normal(coarse_key, coarse_shape, jnp.float32)
    coarse_full = jnp.repeat(jnp.repeat(jnp.repeat(coarse, 4, axis=0), 4, axis=1), 4, axis=2)
    return jnp.clip(fine + coarse_full, -6.0, 6.0).astype(jnp.bfloat16)


def shard_levels(stream_key, extent, pieces, smallest, high):
    factor_of = 1.0
    for dim, shards_of in pieces:
        draws = jax.random.uniform(jax.random.fold_in(jax.random.fold_in(stream_key, 6), dim), (shards_of,), jnp.float32, smallest / len(pieces), high / len(pieces))
        factor_of = factor_of * jnp.repeat(jnp.exp(draws), extent[dim] // shards_of).reshape((-1,) + (1,) * (len(extent) - 1 - dim))
    return factor_of


def noise(rng, shape, deviation, reach, shards=(), held_as=jnp.bfloat16):
    gain = shard_levels(rng, shape, shards, -0.22, 0.18) if shards else 1.0
    values = jax.random.normal(rng, shape, jnp.float32) * deviation * gain
    return jnp.minimum(jnp.maximum(values, -reach), reach).astype(held_as)


def setup_inputs(seed: int = 0, part: int = 0) -> dict:
    seeds = jax.random.split(jax.random.key(seed), 9)
    own_keys = jax.random.split(jax.random.fold_in(seeds[8], part), 9)
    return {
        "volume": draw_volume(jax.random.fold_in(jax.random.fold_in(seeds[8], part), 71), part),
        "first_kernel": noise(seeds[1], (3, 3, 3, C1, C1), (27 * C1 // 2) ** -0.5, 0.15625),
        "second_kernel": noise(seeds[2], (3, 3, 3, C1, C2), (27 * C1 // 2) ** -0.5, 0.15625),
        "deep_kernel": noise(seeds[3], (3, 3, 3, C2, C3), (27 * C2 // 2) ** -0.5, 0.109375, ((4, 16),)),
        "deeper_kernel": noise(seeds[4], (3, 3, 3, C3, C3), (27 * C3 // 2) ** -0.5, 0.078125, ((4, 16),)),
        "rise_kernel": noise(seeds[5], (2, 2, 2, C3, C2), (C3 // 2) ** -0.5, 0.375),
        "decode_kernel": noise(seeds[6], (3, 3, 3, 2 * C2, C2), (27 * C2) ** -0.5, 0.078125, ((3, 16),)),
        "final_kernel": noise(seeds[7], (2, 2, 2, C2, C1), (C2 // 2) ** -0.5, 0.5),
    }


def conv_cube(values, kernel):
    result = lax.conv_general_dilated(values.astype(jnp.float32)[None], kernel.astype(jnp.float32), (1, 1, 1), "SAME", dimension_numbers=("NDHWC", "DHWIO", "NDHWC"), precision=lax.Precision.HIGHEST)
    return result[0]


def pool_mean(values):
    depth, height, width, chans = values.shape
    blocks = values.astype(jnp.float32).reshape(depth // 2, 2, height // 2, 2, width // 2, 2, chans)
    return jnp.mean(blocks, axis=(1, 3, 5)).astype(jnp.bfloat16)


def up_conv(values, kernel):
    depth, height, width, chans = values.shape
    result = jnp.einsum("dhwi,abcio->dahbwco", values.astype(jnp.float32), kernel.astype(jnp.float32), precision=lax.Precision.HIGHEST)
    return result.reshape(2 * depth, 2 * height, 2 * width, kernel.shape[4])


def reference(volume, first_kernel, second_kernel, deep_kernel, deeper_kernel, rise_kernel, decode_kernel, final_kernel):
    first = jax.nn.relu(conv_cube(volume, first_kernel)).astype(jnp.bfloat16)
    pooled_one = pool_mean(first)
    skip = jax.nn.relu(conv_cube(pooled_one, second_kernel)).astype(jnp.bfloat16)
    pooled_two = pool_mean(skip)
    deep = jax.nn.relu(conv_cube(pooled_two, deep_kernel)).astype(jnp.bfloat16)
    deeper = jax.nn.relu(conv_cube(deep, deeper_kernel)).astype(jnp.bfloat16)
    risen = up_conv(deeper, rise_kernel).astype(jnp.bfloat16)
    joined = jnp.concatenate([risen, skip], axis=3)
    decoded = jax.nn.relu(conv_cube(joined, decode_kernel)).astype(jnp.bfloat16)
    return up_conv(decoded, final_kernel).astype(jnp.bfloat16)
```

```python
import functools

import jax
import jax.numpy as jnp
import numpy as np
from jax import lax
from jax.experimental import pallas as pl
from jax.experimental.pallas import tpu as pltpu
from jax.sharding import PartitionSpec as P

LANES = 128


def remote(src, dst, send_sem, recv_sem, target):
    return pltpu.make_async_remote_copy(
        src_ref=src, dst_ref=dst, send_sem=send_sem, recv_sem=recv_sem,
        device_id={"sp": target}, device_id_type=pl.DeviceIdType.MESH,
    )


def trade_edges(n, first, last, low, high, send_sem, recv_sem):
    me = lax.axis_index("sp")
    upward = remote(last, low, send_sem.at[0], recv_sem.at[0], lax.rem(me + 1, n))
    downward = remote(first, high, send_sem.at[1], recv_sem.at[1], lax.rem(me + n - 1, n))

    @pl.when(me < n - 1)
    def _():
        upward.start()

    @pl.when(me > 0)
    def _():
        downward.start()

    @pl.when(me == 0)
    def _():
        low[...] = jnp.zeros(low.shape, low.dtype)

    @pl.when(me == n - 1)
    def _():
        high[...] = jnp.zeros(high.shape, high.dtype)

    def finish():
        @pl.when(me > 0)
        def _():
            upward.wait_recv()
            downward.wait_send()

        @pl.when(me < n - 1)
        def _():
            downward.wait_recv()
            upward.wait_send()

    return finish


def greet_neighbours(n):
    me = lax.axis_index("sp")
    barrier = pltpu.get_barrier_semaphore()

    @pl.when(me > 0)
    def _():
        pl.semaphore_signal(
            barrier, inc=1, device_id={"sp": lax.rem(me + n - 1, n)},
            device_id_type=pl.DeviceIdType.MESH,
        )

    @pl.when(me < n - 1)
    def _():
        pl.semaphore_signal(
            barrier, inc=1, device_id={"sp": lax.rem(me + 1, n)},
            device_id_type=pl.DeviceIdType.MESH,
        )

    @pl.when((me > 0) & (me < n - 1))
    def _():
        pl.semaphore_wait(barrier, 2)

    @pl.when((me == 0) | (me == n - 1))
    def _():
        pl.semaphore_wait(barrier, 1)


def first_level_kernel(
    n, depth, height, width,
    volume_ref, weight_ref, out_ref,
    ends, taps, sums, send_a, recv_a, send_b, recv_b,
):
    area = height * width
    chans = volume_ref.shape[2]
    greet_neighbours(n)
    finish = trade_edges(
        n, volume_ref.at[0], volume_ref.at[depth - 1], ends.at[0], ends.at[1], send_a, recv_a
    )
    index = lax.broadcasted_iota(jnp.int32, (area, 1), 0) & (width - 1)
    blank = jnp.zeros((depth + 2, width, 3 * chans), jnp.bfloat16)
    taps[:, 0:width] = blank
    taps[:, area + width : area + 2 * width] = blank

    def spread(at, values):
        taps[at, width : area + width, chans : 2 * chans] = values
        values = values.astype(jnp.float32)
        left = jnp.where(index > 0, pltpu.roll(values, 1, 0), 0.0)
        right = jnp.where(index < width - 1, pltpu.roll(values, area - 1, 0), 0.0)
        taps[at, width : area + width, 0:chans] = left.astype(jnp.bfloat16)
        taps[at, width : area + width, 2 * chans : 3 * chans] = right.astype(jnp.bfloat16)

    for d in range(depth):
        spread(d + 1, volume_ref[d])
    finish()
    spread(0, ends[0])
    spread(depth + 1, ends[1])
    for pair in range(depth // 2):
        total = jnp.zeros((2 * area, weight_ref.shape[3]), jnp.float32)
        for a in range(3):
            for b in range(3):
                block = taps[2 * pair + a : 2 * pair + a + 2, b * width : b * width + area]
                total += jnp.dot(
                    block.reshape(2 * area, 3 * chans), weight_ref[a, b],
                    preferred_element_type=jnp.float32,
                )
        total = jnp.maximum(total, 0.0).astype(jnp.bfloat16).astype(jnp.float32)
        total = total[0:area] + total[area : 2 * area]
        total = total.reshape(height // 2, 2, width, total.shape[1]).sum(axis=1)
        sums[...] = total.reshape(area // 2, total.shape[2])
        total = sums[pl.ds(0, area // 4, 2), :] + sums[pl.ds(1, area // 4, 2), :]
        out_ref[1 + pair] = (total * 0.125).astype(jnp.bfloat16)
    halves = depth // 2
    trade_edges(
        n, out_ref.at[1], out_ref.at[halves], out_ref.at[0], out_ref.at[halves + 1],
        send_b, recv_b,
    )()


def first_level(volume, kernel):
    n = lax.axis_size("sp")
    depth, height, width, chans = volume.shape
    outs = kernel.shape[4]
    area = height * width
    vmem = pl.BlockSpec(memory_space=pltpu.VMEM)
    padded = pl.pallas_call(
        functools.partial(first_level_kernel, n, depth, height, width),
        out_shape=jax.ShapeDtypeStruct((depth // 2 + 2, area // 4, outs), jnp.bfloat16),
        in_specs=[vmem] * 2,
        out_specs=vmem,
        scratch_shapes=[
            pltpu.VMEM((2, area, chans), jnp.bfloat16),
            pltpu.VMEM((depth + 2, area + 2 * width, 3 * chans), jnp.bfloat16),
            pltpu.VMEM((area // 2, outs), jnp.float32),
        ]
        + [pltpu.SemaphoreType.DMA((2,))] * 4,
        compiler_params=pltpu.CompilerParams(
            collective_id=1, has_side_effects=True, vmem_limit_bytes=16 << 20
        ),
        name="first_level",
    )(volume.reshape(depth, area, chans), kernel.reshape(3, 3, 3 * chans, outs))
    return padded.reshape(depth // 2 + 2, height // 2, width // 2, outs)


def conv_depth(padded, kernel):
    result = lax.conv_general_dilated(
        padded[None],
        kernel,
        (1, 1, 1),
        ((0, 0), (1, 1), (1, 1)),
        dimension_numbers=("NDHWC", "DHWIO", "NDHWC"),
        preferred_element_type=jnp.float32,
    )
    return result[0]


def pool_mean(values):
    depth, height, width, chans = values.shape
    blocks = values.astype(jnp.float32).reshape(depth // 2, 2, height // 2, 2, width // 2, 2, chans)
    return jnp.mean(blocks, axis=(1, 3, 5)).astype(jnp.bfloat16)


def up_conv(values, kernel):
    depth, height, width, chans = values.shape
    result = jnp.einsum("dhwi,abcio->dahbwco", values, kernel, preferred_element_type=jnp.float32)
    return result.reshape(2 * depth, 2 * height, 2 * width, kernel.shape[4])


def conv_rows(values, weight_ref, height, width):
    rows = values.shape[0]
    index = lax.broadcasted_iota(jnp.int32, (rows, 1), 0)
    w_at = index & (width - 1)
    h_at = (index >> (width.bit_length() - 1)) & (height - 1)
    part, chans = weight_ref.shape[2:]
    blank = jnp.zeros((LANES - 3 * part, chans), weight_ref.dtype)
    total = jnp.zeros((rows, LANES), jnp.float32)
    for b in range(3):
        for c in range(3):
            shift = width * (b - 1) + (c - 1)
            moved = values if shift == 0 else pltpu.roll(values, (-shift) % rows, 0)
            h_to, w_to = h_at + (b - 1), w_at + (c - 1)
            keep = (h_to >= 0) & (h_to < height) & (w_to >= 0) & (w_to < width)
            moved = jnp.where(keep, moved, 0.0).astype(jnp.bfloat16)
            tap = 3 * b + c
            weight = jnp.concatenate([weight_ref[a, tap] for a in range(3)] + [blank], axis=0)
            total += lax.dot_general(
                moved, weight, (((1,), (1,)), ((), ())), preferred_element_type=jnp.float32
            )
    return total


def bottleneck_kernel(
    n, height, width, part,
    pooled_ref, skip_ref, deep_w_ref, deeper_w_ref, out_ref, near_ref,
    whole, deep_mine, deep_all, packed,
    send_a, recv_a, send_b, recv_b, send_c, recv_c, send_d, recv_d,
):
    me = lax.axis_index("sp")
    area = height * width
    voxels = n * area
    partner = me + 1 - 2 * (me % 2)
    half = n // 2

    barrier = pltpu.get_barrier_semaphore()

    def greet(k, carry):
        pl.semaphore_signal(
            barrier, inc=1, device_id={"sp": lax.rem(me + k, n)},
            device_id_type=pl.DeviceIdType.MESH,
        )
        return carry

    lax.fori_loop(1, n, greet, 0)
    pl.semaphore_wait(barrier, n - 1)

    def gather(mine, everyone, send_sem, recv_sem):
        def slot(source):
            return everyone.at[source]

        def direct(k):
            target = lax.rem(me + 2 * k, n)
            return remote(mine, slot(me), send_sem.at[k], recv_sem.at[me], target)

        def relay(k):
            source = lax.rem(me + 2 * (half - k), n)
            return remote(
                slot(source), slot(source), send_sem.at[half + k], recv_sem.at[source], partner
            )

        def arrival(source):
            return remote(mine, slot(source), send_sem.at[0], recv_sem.at[source], partner)

        def start_direct(k, carry):
            direct(k).start()
            return carry

        to_partner = remote(mine, slot(me), send_sem.at[0], recv_sem.at[me], partner)
        lax.fori_loop(1, half, start_direct, 0)
        to_partner.start()
        everyone[me] = mine[...]

        def pass_on(k, carry):
            arrival(lax.rem(me + 2 * (half - k), n)).wait_recv()
            relay(k).start()
            return carry

        lax.fori_loop(1, half, pass_on, 0)

        def from_partner(k, carry):
            arrival(lax.rem(partner + 2 * (half - k), n)).wait_recv()
            return carry

        lax.fori_loop(0, half, from_partner, 0)

        def finish():
            to_partner.wait_send()

            def sent(k, carry):
                direct(k).wait_send()
                relay(k).wait_send()
                return carry

            lax.fori_loop(1, half, sent, 0)

        return finish

    finish_a = gather(pooled_ref, whole, send_a, recv_a)
    depth = skip_ref.shape[0]
    finish_d = trade_edges(
        n, skip_ref.at[0], skip_ref.at[depth - 1], near_ref.at[0], near_ref.at[1], send_d, recv_d
    )
    lanes = lax.broadcasted_iota(jnp.int32, (1, voxels), 1)
    values = whole[...].astype(jnp.float32).reshape(voxels, pooled_ref.shape[1])
    deep = conv_rows(values, deep_w_ref, height, width).T
    below = jnp.where(lanes >= area, pltpu.roll(deep[0:part], area, 1), 0.0)
    above = jnp.where(
        lanes < voxels - area, pltpu.roll(deep[2 * part : 3 * part], voxels - area, 1), 0.0
    )
    deep = below + deep[part : 2 * part] + above
    deep_mine[...] = jnp.maximum(deep, 0.0).astype(jnp.bfloat16)
    finish_b = gather(deep_mine, deep_all, send_b, recv_b)

    values = deep_all[...].astype(jnp.float32).reshape(n * part, voxels).T
    deeper = conv_rows(values, deeper_w_ref, height, width)
    rows = lax.broadcasted_iota(jnp.int32, (voxels, 1), 0)

    def down(block):
        return jnp.where(rows >= area, pltpu.roll(block, area, 0), 0.0)

    def up(block):
        return jnp.where(rows < voxels - area, pltpu.roll(block, voxels - area, 0), 0.0)

    deeper = (
        down(deeper)
        + pltpu.roll(deeper, LANES - part, 1)
        + up(pltpu.roll(deeper, LANES - 2 * part, 1))
    )
    deeper = jnp.maximum(deeper, 0.0)
    lane = lax.broadcasted_iota(jnp.int32, (1, LANES), 1)
    deeper = jnp.where(
        lane < part,
        down(deeper),
        jnp.where(
            lane < 2 * part,
            pltpu.roll(deeper, part, 1),
            up(pltpu.roll(deeper, 2 * part, 1)),
        ),
    )
    packed[...] = deeper.astype(jnp.bfloat16).reshape(n, area, LANES)

    def deal(k):
        target = lax.rem(me + k, n)
        return remote(packed.at[target], out_ref.at[me], send_c.at[k], recv_c.at[me], target)

    def start_deal(k, carry):
        deal(k).start()
        return carry

    lax.fori_loop(1, n, start_deal, 0)
    out_ref[me] = packed[me]

    def receive(k, carry):
        source = lax.rem(me + k, n)
        remote(
            packed.at[source], out_ref.at[source], send_c.at[k], recv_c.at[source], source
        ).wait_recv()
        return carry

    lax.fori_loop(1, n, receive, 0)

    def sent(k, carry):
        deal(k).wait_send()
        return carry

    lax.fori_loop(1, n, sent, 0)
    finish_a()
    finish_b()
    finish_d()


def out_major(kernel):
    chans, part = kernel.shape[3], kernel.shape[4]
    return jnp.transpose(kernel, (0, 1, 2, 4, 3)).reshape(3, 9, part, chans)


def bottleneck(pooled, skip, deep_kernel, deeper_kernel):
    n = lax.axis_size("sp")
    _, height, width, chans = pooled.shape
    part = deep_kernel.shape[4]
    area = height * width
    voxels = n * area
    vmem = pl.BlockSpec(memory_space=pltpu.VMEM)
    received, near = pl.pallas_call(
        functools.partial(bottleneck_kernel, n, height, width, part),
        out_shape=(
            jax.ShapeDtypeStruct((n, area, LANES), jnp.bfloat16),
            jax.ShapeDtypeStruct((2,) + skip.shape[1:], jnp.bfloat16),
        ),
        in_specs=[vmem] * 4,
        out_specs=(vmem, vmem),
        scratch_shapes=[
            pltpu.VMEM((n, area, chans), jnp.bfloat16),
            pltpu.VMEM((part, voxels), jnp.bfloat16),
            pltpu.VMEM((n, part, voxels), jnp.bfloat16),
            pltpu.VMEM((n, area, LANES), jnp.bfloat16),
        ]
        + [pltpu.SemaphoreType.DMA((n,))] * 6
        + [pltpu.SemaphoreType.DMA((2,))] * 2,
        compiler_params=pltpu.CompilerParams(
            collective_id=0, has_side_effects=True, vmem_limit_bytes=24 << 20
        ),
        name="bottleneck",
    )(pooled.reshape(area, chans), skip, out_major(deep_kernel), out_major(deeper_kernel))
    blocks = received[:, :, : 3 * part].reshape(n, area, 3, part)
    return jnp.transpose(blocks, (2, 1, 0, 3)).reshape(3, height, width, n * part), near


def body(
    volume,
    first_kernel,
    second_kernel,
    deep_kernel,
    deeper_kernel,
    rise_kernel,
    decode_kernel,
    final_kernel,
):
    padded_pool = first_level(volume, first_kernel)
    skip = jax.nn.relu(conv_depth(padded_pool, second_kernel)).astype(jnp.bfloat16)
    pooled_two = pool_mean(skip)
    deeper_near, skip_near = bottleneck(pooled_two, skip, deep_kernel, deeper_kernel)
    padded_skip = jnp.concatenate([skip_near[:1], skip, skip_near[1:]], axis=0)
    risen = up_conv(deeper_near, rise_kernel)[1:-1].astype(jnp.bfloat16)
    padded_joined = jnp.concatenate([risen, padded_skip], axis=3)
    whole_decode_kernel = lax.all_gather(decode_kernel, "sp", axis=3, tiled=True)
    decoded = jax.nn.relu(conv_depth(padded_joined, whole_decode_kernel)).astype(jnp.bfloat16)
    return up_conv(decoded, final_kernel).astype(jnp.bfloat16)


def spread_matrix():
    out = np.zeros((6, 6, 4, 4, 16, 16), np.float32)
    for eh in range(6):
        for ew in range(6):
            for hc in range(4):
                for wc in range(4):
                    h, w = 4 * hc + eh - 1, 4 * wc + ew - 1
                    if 0 <= h < 16 and 0 <= w < 16:
                        out[eh, ew, hc, wc, h, w] = 1.0
    return out.reshape(36 * 16, 256)


def spread_matrix_two():
    out = np.zeros((4, 4, 4, 4, 2, 2, 4, 4), np.float32)
    for eh in range(4):
        for ew in range(4):
            for hc in range(4):
                for wc in range(4):
                    h, w = 2 * hc + eh - 1, 2 * wc + ew - 1
                    if 0 <= h < 8 and 0 <= w < 8:
                        out[eh, ew, hc, wc, h % 2, w % 2, h // 2, w // 2] = 1.0
    return out.reshape(16 * 16, 64)


def gather_matrix():
    out = np.zeros((16, 16, 4, 4, 4, 4), np.float32)
    for h in range(16):
        for w in range(16):
            out[h, w, h % 4, w % 4, h // 4, w // 4] = 1.0
    return out.reshape(256, 256)


def block_transpose(pieces, width):
    pieces = list(pieces)
    count = len(pieces)
    block = lax.broadcasted_iota(jnp.int32, pieces[0].shape, 1) // width
    step = 1
    while step < count:
        low = (block & step) == 0
        for i in range(count):
            if i & step:
                continue
            a, b = pieces[i], pieces[i + step]
            pieces[i] = jnp.where(low, a, pltpu.roll(b, width * step, 1))
            pieces[i + step] = jnp.where(low, pltpu.roll(a, 128 - width * step, 1), b)
        step *= 2
    return pieces


def moved(values, by, keep):
    lanes = values.shape[1]
    return jnp.where(keep, pltpu.roll(values, by % lanes, 1), 0.0)


class Lanes:
    def __init__(self, count):
        lane = lax.broadcasted_iota(jnp.int32, (1, count), 1)
        wc, hc, d = lane & 3, (lane >> 2) & 3, lane >> 4
        top = count // 16 - 1
        self.after = {1: wc > 0, 4: hc > 0, 16: d > 0}
        self.before = {1: wc < 3, 4: hc < 3, 16: d < top}

    def back(self, values, by):
        return moved(values, by, self.after[by])

    def ahead(self, values, by):
        return moved(values, -by, self.before[by])


def add_taps(lanes, y, outs):
    def row(a, b, c):
        at = (9 * a + 3 * b + c) * outs
        return y[at : at + outs]

    def tall(c):
        return jnp.concatenate([row(a, b, c) for b in range(3) for a in range(3)], axis=0)

    y = tall(1) + lanes.back(tall(0), 1) + lanes.ahead(tall(2), 1)
    y = [y[i * 3 * outs : (i + 1) * 3 * outs] for i in range(3)]
    y = y[1] + lanes.back(y[0], 4) + lanes.ahead(y[2], 4)
    y = [y[i * outs : (i + 1) * outs] for i in range(3)]
    return y[1] + lanes.back(y[0], 16) + lanes.ahead(y[2], 16)


def add_fine_taps(lanes, load, outs):
    def pair(zero, one, by):
        even = zero[1] + one[2] + lanes.back(one[0], by)
        odd = one[1] + zero[0] + lanes.ahead(zero[2], by)
        return even, odd

    planes = {}
    for pd in range(2):
        rows = {}
        for ph in range(2):
            def taps(pw):
                p = 4 * pd + 2 * ph + pw
                return [
                    jnp.concatenate(
                        [load(p, 9 * a + 3 * b + c) for b in range(3) for a in range(3)], axis=0
                    )
                    for c in range(3)
                ]

            rows[ph] = pair(taps(0), taps(1), 1)
        for qw in range(2):
            def cut(ph):
                return [rows[ph][qw][i * 3 * outs : (i + 1) * 3 * outs] for i in range(3)]

            planes[pd, qw] = pair(cut(0), cut(1), 4)
    result = [None] * 8
    for qw in range(2):
        for qh in range(2):
            def cut(pd):
                return [planes[pd, qw][qh][i * outs : (i + 1) * outs] for i in range(3)]

            low, high = pair(cut(0), cut(1), 16)
            result[2 * qh + qw] = low
            result[4 + 2 * qh + qw] = high
    return result


class Gather:
    def __init__(self, n, slots, send_sem, recv_sem):
        self.n, self.slots, self.send_sem, self.recv_sem = n, slots, send_sem, recv_sem
        self.me = lax.axis_index("sp")
        self.sent = []
        self.others = list(range(n - 2, 0, -2))

    def send(self, source, target):
        slot = self.slots.at[self.me ^ source]
        copy = remote(
            slot, slot, self.send_sem.at[len(self.sent)], self.recv_sem.at[source ^ target],
            self.me ^ target,
        )
        copy.start()
        self.sent.append(copy)

    def wait(self, source):
        slot = self.slots.at[self.me ^ source]
        remote(slot, slot, self.send_sem.at[0], self.recv_sem.at[source], self.me ^ 1).wait_recv()

    def start(self):
        for k in self.others:
            self.send(0, k)
        self.send(0, 1)

    def relay(self):
        for k in reversed(self.others):
            self.wait(k)
            self.send(k, 1)

    def finish(self):
        for k in range(1, self.n, 2):
            self.wait(k)

    def drain(self):
        for copy in self.sent:
            copy.wait_send()


def net_kernel(
    n,
    volume_hbm, first_hbm, second_hbm, deep_hbm, deeper_hbm, rise_hbm, decode_hbm,
    spread_hbm, spread_two_hbm,
    out_ref,
    vol, vhalo, pp, pp2, wpair, w2, wd, wdd, rw, kloc,
    ex, pool, ex2, pooled_all, deep_all, deeper_all, skip_all,
    wsend, wall, wt, ys, dsend,
    load_sem, send_v, recv_v, send_p, recv_p,
    send_a, recv_a, send_b, recv_b, send_c, recv_c, send_s, recv_s,
    send_w, recv_w, send_d, recv_d,
):
    me = lax.axis_index("sp")
    bf = jnp.bfloat16
    f32 = jnp.float32
    depth = vol.shape[0]
    k1 = first_hbm.shape[1]
    part = wd.shape[0] // 27
    outs = 256 // n
    coarse = 16 * n

    loads = []

    def load(src, dst):
        copy = pltpu.make_async_copy(src, dst, load_sem.at[len(loads)])
        copy.start()
        loads.append(copy)
        return copy

    get_vol = load(volume_hbm, vol)
    get_pp = load(spread_hbm, pp)
    get_k = load(decode_hbm, kloc)
    get_w1 = [
        load(first_hbm.at[1], wpair.at[0:k1, 0:128]),
        load(first_hbm.at[0], wpair.at[0:k1, 128:256]),
        load(first_hbm.at[2], wpair.at[k1 : 2 * k1, 0:128]),
        load(first_hbm.at[1], wpair.at[k1 : 2 * k1, 128:256]),
    ]
    get_pp2 = load(spread_two_hbm, pp2)
    get_w2 = load(second_hbm, w2)
    get_wd = load(deep_hbm, wd)
    get_wdd = load(deeper_hbm, wdd)
    get_rw = load(rise_hbm, rw)

    barrier = pltpu.get_barrier_semaphore()
    for k in range(n - 1, 0, -1):
        pl.semaphore_signal(
            barrier, inc=1, device_id={"sp": me ^ k}, device_id_type=pl.DeviceIdType.MESH
        )

    def spread(planes, to):
        get = jnp.concatenate(planes, axis=1)
        result = jnp.dot(pp[...], get, preferred_element_type=f32).astype(bf)
        for i, at in enumerate(to):
            ex[at] = result[:, 128 * i : 128 * (i + 1)]

    get_vol.wait()
    get_pp.wait()
    for d in range(0, depth, 2):
        spread([vol[d], vol[d + 1]], [d + 1, d + 2])

    get_k.wait()
    per = 128 // outs
    for half in range(256 // 128):
        for group in range(wsend.shape[2] // 128):
            taps = []
            for i in range(per):
                tap = per * group + i
                if tap < 27:
                    taps.append(kloc[tap, :, 128 * half : 128 * (half + 1)].astype(f32))
                else:
                    taps.append(jnp.zeros((kloc.shape[1], 128), f32))
            for j, piece in enumerate(block_transpose(taps, outs)):
                wsend[per * half + j, :, 128 * group : 128 * (group + 1)] = piece.astype(bf)

    pl.semaphore_wait(barrier, n - 1)
    finish_v = trade_edges(
        n, vol.at[0], vol.at[depth - 1], vhalo.at[0], vhalo.at[1], send_v, recv_v
    )
    w_copies = []
    for k in range(n - 1, 0, -1):
        copy = remote(wsend.at[me ^ k], wall.at[me], send_w.at[k], recv_w.at[k], me ^ k)
        copy.start()
        w_copies.append(copy)
    wall[me] = wsend[me]

    def taken(at, b):
        columns = []
        for c in range(3):
            columns.append(
                jnp.concatenate(
                    [ex[at, pl.ds(((b + hm) * 6 + c) * 16, 64), :] for hm in range(4)], axis=0
                )
            )
        return columns

    def rows_of(at):
        return jnp.concatenate(sum([taken(at, b) for b in range(3)], []), axis=1)

    for copy in get_w1:
        copy.wait()

    def both(at):
        left = jnp.concatenate([rows_of(at), rows_of(at + 1)], axis=1)
        return jnp.dot(left, wpair[...], preferred_element_type=f32)

    pairs = [both(1), both(3)]
    own_low = jnp.dot(rows_of(2), wpair[0:k1, 128:256], preferred_element_type=f32)
    own_high = jnp.dot(rows_of(3), wpair[k1 : 2 * k1, 0:128], preferred_element_type=f32)
    finish_v()
    spread([vhalo[0], vhalo[1]], [0, depth + 1])
    far_low = jnp.dot(rows_of(0), wpair[0:k1, 128:256], preferred_element_type=f32)
    far_high = jnp.dot(rows_of(5), wpair[k1 : 2 * k1, 0:128], preferred_element_type=f32)
    planes = [
        pairs[0][:, 0:128] + far_low,
        pairs[0][:, 128:256] + own_high,
        pairs[1][:, 0:128] + own_low,
        pairs[1][:, 128:256] + far_high,
    ]
    planes = [jnp.maximum(t, 0.0).astype(bf).astype(f32) for t in planes]
    for i in range(2):
        total = planes[2 * i] + planes[2 * i + 1]
        for ph in range(2):
            for pw in range(2):
                slabs = [
                    total[((2 * ph + y) * 4 + 2 * pw + x) * 16 :][:16]
                    for y in range(2) for x in range(2)
                ]
                slab = (slabs[0] + slabs[1]) + (slabs[2] + slabs[3])
                pool[1 + i, pl.ds((2 * ph + pw) * 16, 16), :] = (slab * 0.125).astype(bf)

    finish_p = trade_edges(n, pool.at[1], pool.at[2], pool.at[0], pool.at[3], send_p, recv_p)
    get_pp2.wait()
    get_w2.wait()

    def spread_two(at):
        ex2[at] = jnp.dot(pp2[...], pool[at], preferred_element_type=f32).astype(bf)

    def rows_two(a):
        columns = []
        for b in range(3):
            for c in range(3):
                columns.append(
                    jnp.concatenate(
                        [
                            ex2[a + i, pl.ds(((b + ph) * 4 + c) * 16, 32), :]
                            for i in range(2) for ph in range(2)
                        ],
                        axis=0,
                    )
                )
        return jnp.concatenate(columns, axis=1)

    spread_two(1)
    spread_two(2)
    skip = jnp.dot(rows_two(1), w2[1], preferred_element_type=f32)
    finish_p()
    spread_two(0)
    spread_two(3)
    skip += jnp.dot(rows_two(0), w2[0], preferred_element_type=f32)
    skip += jnp.dot(rows_two(2), w2[2], preferred_element_type=f32)
    skip = jnp.maximum(skip, 0.0).astype(bf)
    skip_all[me] = skip.reshape(skip_all.shape[1:])
    skip = skip.astype(f32)
    slabs = [skip[16 * i : 16 * (i + 1)] for i in range(8)]
    while len(slabs) > 1:
        slabs = [slabs[i] + slabs[i + 1] for i in range(0, len(slabs), 2)]
    pooled_all[me] = (slabs[0] * 0.125).astype(bf)

    gather_a = Gather(n, pooled_all, send_a, recv_a)
    gather_b = Gather(n, deep_all, send_b, recv_b)
    gather_c = Gather(n, deeper_all, send_c, recv_c)
    gather_s = Gather(n, skip_all, send_s, recv_s)
    gather_a.start()
    gather_s.start()
    lanes = Lanes(coarse)
    get_wd.wait()
    get_wdd.wait()
    get_rw.wait()
    gather_a.relay()
    gather_a.finish()
    y = lax.dot_general(
        wd[...], pooled_all[...].reshape(coarse, pooled_all.shape[2]),
        (((1,), (1,)), ((), ())), preferred_element_type=f32,
    )
    deep_all[me] = jnp.maximum(add_taps(lanes, y, part), 0.0).astype(bf)
    gather_b.start()
    for k in range(1, n):
        remote(wsend.at[me ^ k], wall.at[me ^ k], send_w.at[k], recv_w.at[k], me ^ k).wait_recv()
    for at in range(0, wt.shape[1], 128):
        block = wall[pl.ds(at // part, 128 // part)].reshape(128, wall.shape[2])
        wt[:, at : at + 128] = block.astype(f32).T.astype(bf)[0 : wt.shape[0]]
    gather_b.relay()
    gather_b.finish()
    y = jnp.dot(
        wdd[...], deep_all[...].reshape(n * part, coarse), preferred_element_type=f32
    )
    deeper_all[me] = jnp.maximum(add_taps(lanes, y, part), 0.0).astype(bf)
    gather_c.start()
    gather_s.relay()
    gather_s.finish()

    def fine(p, values, inner):
        ys[p] = lax.dot_general(
            wt[:, inner], values, (((1,), (1,)), ((), ())), preferred_element_type=f32
        )

    def tap_of(p, tap):
        return ys[p, outs * tap : outs * (tap + 1), :]

    for p in range(8):
        fine(p, skip_all[:, p].reshape(coarse, skip_all.shape[3]), slice(256, 512))
    from_skip = add_fine_taps(lanes, tap_of, outs)
    gather_c.relay()
    gather_c.finish()
    deeper = deeper_all[...].reshape(n * part, coarse).astype(f32).T.astype(bf)
    for p in range(8):
        risen = jnp.dot(deeper, rw[p], preferred_element_type=f32).astype(bf)
        fine(p, risen, slice(0, 256))
    from_risen = add_fine_taps(lanes, tap_of, outs)
    decoded = [jnp.maximum(s + r, 0.0) for s, r in zip(from_skip, from_risen)]
    for half in range(coarse // 128):
        cut = [t[:, 128 * half : 128 * (half + 1)] for t in decoded]
        for j, piece in enumerate(block_transpose(cut, 16)):
            dsend[8 * half + j] = piece.astype(bf)
    d_copies = []
    for k in range(n - 1, 0, -1):
        copy = remote(dsend.at[me ^ k], out_ref.at[me], send_d.at[k], recv_d.at[k], me ^ k)
        copy.start()
        d_copies.append(copy)
    out_ref[me] = dsend[me]
    for k in range(1, n):
        remote(dsend.at[me ^ k], out_ref.at[me ^ k], send_d.at[k], recv_d.at[k], me ^ k).wait_recv()
    for copy in w_copies + d_copies:
        copy.wait_send()
    for gather in (gather_a, gather_b, gather_c, gather_s):
        gather.drain()


def net(volume, first_kernel, second_kernel, deep_kernel, deeper_kernel, rise_kernel, decode_kernel):
    n = lax.axis_size("sp")
    depth, height, width, chans = volume.shape
    mid = second_kernel.shape[4]
    low = rise_kernel.shape[3]
    part = deep_kernel.shape[4]
    block = decode_kernel.shape[3]
    outs = mid // n
    coarse = 16 * n
    area = height * width
    taps = 27 * outs
    wide = -(-taps // LANES) * LANES
    bf = jnp.bfloat16
    vmem = pltpu.VMEM
    dma = pltpu.SemaphoreType.DMA
    any_spec = pl.BlockSpec(memory_space=pl.ANY)

    def tap_rows(kernel):
        return jnp.transpose(kernel, (0, 1, 2, 4, 3)).reshape(27 * part, kernel.shape[3])

    return pl.pallas_call(
        functools.partial(net_kernel, n),
        out_shape=jax.ShapeDtypeStruct((n, outs, 128), bf),
        in_specs=[any_spec] * 9,
        out_specs=pl.BlockSpec(memory_space=pltpu.VMEM),
        scratch_shapes=[
            vmem((depth, area, chans), bf),
            vmem((2, area, chans), bf),
            vmem((36 * 16, area), bf),
            vmem((16 * 16, area // 4), bf),
            vmem((18 * chans, 2 * chans), bf),
            vmem((3, 9 * chans, mid), bf),
            vmem((27 * part, mid), bf),
            vmem((27 * part, low), bf),
            vmem((8, low, mid), bf),
            vmem((27, block, mid), bf),
            vmem((depth + 2, 36 * 16, chans), bf),
            vmem((depth // 2 + 2, area // 4, chans), bf),
            vmem((depth // 2 + 2, 16 * 16, chans), bf),
            vmem((n, 16, mid), bf),
            vmem((n, part, coarse), bf),
            vmem((n, part, coarse), bf),
            vmem((n, 8, 16, mid), bf),
            vmem((n, block, wide), bf),
            vmem((n, block, wide), bf),
            vmem((taps, 2 * mid), bf),
            vmem((8, taps, coarse), jnp.float32),
            vmem((n, outs, 128), bf),
            dma((16,)),
            dma((2,)), dma((2,)), dma((2,)), dma((2,)),
            dma((2 * n,)), dma((n,)), dma((2 * n,)), dma((n,)),
            dma((2 * n,)), dma((n,)), dma((2 * n,)), dma((n,)),
            dma((n,)), dma((n,)), dma((n,)), dma((n,)),
        ],
        compiler_params=pltpu.CompilerParams(
            collective_id=2, has_side_effects=True, vmem_limit_bytes=44 << 20
        ),
        name="net",
    )(
        volume.reshape(depth, area, chans),
        first_kernel.reshape(3, 9 * chans, chans),
        second_kernel.reshape(3, 9 * chans, mid),
        tap_rows(deep_kernel),
        tap_rows(deeper_kernel),
        rise_kernel.reshape(8, low, mid),
        decode_kernel.reshape(27, block, mid),
        jnp.asarray(spread_matrix(), bf),
        jnp.asarray(spread_matrix_two(), bf),
    )


def last_kernel(decoded_ref, weight_ref, order_ref, out_ref):
    f32, bf = jnp.float32, jnp.bfloat16
    decoded = decoded_ref[...].astype(f32).T.astype(bf)
    slabs = {}
    for a in range(2):
        for b in range(2):
            for c in range(2):
                t = jnp.dot(
                    decoded, weight_ref[4 * a + 2 * b + c], preferred_element_type=f32
                ).astype(bf)
                for p in range(8):
                    at = (2 * (p // 4) + a, 2 * (p // 2 % 2) + b, 2 * (p % 2) + c)
                    slabs[at] = t[16 * p : 16 * (p + 1)]
    for d in range(0, 4, 2):
        plane = jnp.concatenate(
            [
                jnp.concatenate([slabs[d + i, y, x] for y in range(4) for x in range(4)], axis=0)
                for i in range(2)
            ],
            axis=1,
        )
        plane = jnp.dot(order_ref[...], plane, preferred_element_type=f32).astype(bf)
        out_ref[d] = plane[:, 0:128]
        out_ref[d + 1] = plane[:, 128:256]


def last(decoded, final_kernel):
    mid, chans = final_kernel.shape[3:]
    return pl.pallas_call(
        last_kernel,
        out_shape=jax.ShapeDtypeStruct((4, 256, chans), jnp.bfloat16),
        in_specs=[pl.BlockSpec(memory_space=pltpu.VMEM)] * 3,
        out_specs=pl.BlockSpec(memory_space=pltpu.VMEM),
        name="last",
    )(
        decoded.reshape(mid, 128),
        final_kernel.reshape(8, mid, chans),
        jnp.asarray(gather_matrix(), jnp.bfloat16),
    ).reshape(4, 16, 16, chans)


def split_body(
    volume, first_kernel, second_kernel, deep_kernel, deeper_kernel,
    rise_kernel, decode_kernel, final_kernel,
):
    n = lax.axis_size("sp")
    if n & (n - 1) or decode_kernel.shape[4] % (16 * n) or decode_kernel.shape[3] % 16:
        return body(
            volume, first_kernel, second_kernel, deep_kernel, deeper_kernel,
            rise_kernel, decode_kernel, final_kernel,
        )
    decoded = net(
        volume, first_kernel, second_kernel, deep_kernel, deeper_kernel, rise_kernel, decode_kernel
    )
    return last(decoded, final_kernel)


def solution(mesh):
    return jax.shard_map(
        split_body,
        mesh=mesh,
        in_specs=(
            P(("rep", "sp"), None, None, None),
            P(),
            P(),
            P(None, None, None, None, "sp"),
            P(None, None, None, None, "sp"),
            P(),
            P(None, None, None, "sp", None),
            P(),
        ),
        out_specs=P(("rep", "sp"), None, None, None),
        check_vma=False,
    )
```

```python
import functools

import jax
import jax.numpy as jnp
import numpy as np
from jax import lax
from jax.experimental import pallas as pl
from jax.experimental.pallas import tpu as pltpu
from jax.sharding import PartitionSpec as P

LANES = 128


def remote(src, dst, send_sem, recv_sem, target):
    return pltpu.make_async_remote_copy(
        src_ref=src, dst_ref=dst, send_sem=send_sem, recv_sem=recv_sem,
        device_id={"sp": target}, device_id_type=pl.DeviceIdType.MESH,
    )


def trade_edges(n, first, last, low, high, send_sem, recv_sem):
    me = lax.axis_index("sp")
    upward = remote(last, low, send_sem.at[0], recv_sem.at[0], lax.rem(me + 1, n))
    downward = remote(first, high, send_sem.at[1], recv_sem.at[1], lax.rem(me + n - 1, n))

    @pl.when(me < n - 1)
    def _():
        upward.start()

    @pl.when(me > 0)
    def _():
        downward.start()

    @pl.when(me == 0)
    def _():
        low[...] = jnp.zeros(low.shape, low.dtype)

    @pl.when(me == n - 1)
    def _():
        high[...] = jnp.zeros(high.shape, high.dtype)

    def finish():
        @pl.when(me > 0)
        def _():
            upward.wait_recv()
            downward.wait_send()

        @pl.when(me < n - 1)
        def _():
            downward.wait_recv()
            upward.wait_send()

    return finish


def greet_neighbours(n):
    me = lax.axis_index("sp")
    barrier = pltpu.get_barrier_semaphore()

    @pl.when(me > 0)
    def _():
        pl.semaphore_signal(
            barrier, inc=1, device_id={"sp": lax.rem(me + n - 1, n)},
            device_id_type=pl.DeviceIdType.MESH,
        )

    @pl.when(me < n - 1)
    def _():
        pl.semaphore_signal(
            barrier, inc=1, device_id={"sp": lax.rem(me + 1, n)},
            device_id_type=pl.DeviceIdType.MESH,
        )

    @pl.when((me > 0) & (me < n - 1))
    def _():
        pl.semaphore_wait(barrier, 2)

    @pl.when((me == 0) | (me == n - 1))
    def _():
        pl.semaphore_wait(barrier, 1)


def first_level_kernel(
    n, depth, height, width,
    volume_ref, weight_ref, out_ref,
    ends, taps, sums, send_a, recv_a, send_b, recv_b,
):
    area = height * width
    chans = volume_ref.shape[2]
    greet_neighbours(n)
    finish = trade_edges(
        n, volume_ref.at[0], volume_ref.at[depth - 1], ends.at[0], ends.at[1], send_a, recv_a
    )
    index = lax.broadcasted_iota(jnp.int32, (area, 1), 0) & (width - 1)
    blank = jnp.zeros((depth + 2, width, 3 * chans), jnp.bfloat16)
    taps[:, 0:width] = blank
    taps[:, area + width : area + 2 * width] = blank

    def spread(at, values):
        taps[at, width : area + width, chans : 2 * chans] = values
        values = values.astype(jnp.float32)
        left = jnp.where(index > 0, pltpu.roll(values, 1, 0), 0.0)
        right = jnp.where(index < width - 1, pltpu.roll(values, area - 1, 0), 0.0)
        taps[at, width : area + width, 0:chans] = left.astype(jnp.bfloat16)
        taps[at, width : area + width, 2 * chans : 3 * chans] = right.astype(jnp.bfloat16)

    for d in range(depth):
        spread(d + 1, volume_ref[d])
    finish()
    spread(0, ends[0])
    spread(depth + 1, ends[1])
    for pair in range(depth // 2):
        total = jnp.zeros((2 * area, weight_ref.shape[3]), jnp.float32)
        for a in range(3):
            for b in range(3):
                block = taps[2 * pair + a : 2 * pair + a + 2, b * width : b * width + area]
                total += jnp.dot(
                    block.reshape(2 * area, 3 * chans), weight_ref[a, b],
                    preferred_element_type=jnp.float32,
                )
        total = jnp.maximum(total, 0.0).astype(jnp.bfloat16).astype(jnp.float32)
        total = total[0:area] + total[area : 2 * area]
        total = total.reshape(height // 2, 2, width, total.shape[1]).sum(axis=1)
        sums[...] = total.reshape(area // 2, total.shape[2])
        total = sums[pl.ds(0, area // 4, 2), :] + sums[pl.ds(1, area // 4, 2), :]
        out_ref[1 + pair] = (total * 0.125).astype(jnp.bfloat16)
    halves = depth // 2
    trade_edges(
        n, out_ref.at[1], out_ref.at[halves], out_ref.at[0], out_ref.at[halves + 1],
        send_b, recv_b,
    )()


def first_level(volume, kernel):
    n = lax.axis_size("sp")
    depth, height, width, chans = volume.shape
    outs = kernel.shape[4]
    area = height * width
    vmem = pl.BlockSpec(memory_space=pltpu.VMEM)
    padded = pl.pallas_call(
        functools.partial(first_level_kernel, n, depth, height, width),
        out_shape=jax.ShapeDtypeStruct((depth // 2 + 2, area // 4, outs), jnp.bfloat16),
        in_specs=[vmem] * 2,
        out_specs=vmem,
        scratch_shapes=[
            pltpu.VMEM((2, area, chans), jnp.bfloat16),
            pltpu.VMEM((depth + 2, area + 2 * width, 3 * chans), jnp.bfloat16),
            pltpu.VMEM((area // 2, outs), jnp.float32),
        ]
        + [pltpu.SemaphoreType.DMA((2,))] * 4,
        compiler_params=pltpu.CompilerParams(
            collective_id=1, has_side_effects=True, vmem_limit_bytes=16 << 20
        ),
        name="first_level",
    )(volume.reshape(depth, area, chans), kernel.reshape(3, 3, 3 * chans, outs))
    return padded.reshape(depth // 2 + 2, height // 2, width // 2, outs)


def conv_depth(padded, kernel):
    result = lax.conv_general_dilated(
        padded[None],
        kernel,
        (1, 1, 1),
        ((0, 0), (1, 1), (1, 1)),
        dimension_numbers=("NDHWC", "DHWIO", "NDHWC"),
        preferred_element_type=jnp.float32,
    )
    return result[0]


def pool_mean(values):
    depth, height, width, chans = values.shape
    blocks = values.astype(jnp.float32).reshape(depth // 2, 2, height // 2, 2, width // 2, 2, chans)
    return jnp.mean(blocks, axis=(1, 3, 5)).astype(jnp.bfloat16)


def up_conv(values, kernel):
    depth, height, width, chans = values.shape
    result = jnp.einsum("dhwi,abcio->dahbwco", values, kernel, preferred_element_type=jnp.float32)
    return result.reshape(2 * depth, 2 * height, 2 * width, kernel.shape[4])


def conv_rows(values, weight_ref, height, width):
    rows = values.shape[0]
    index = lax.broadcasted_iota(jnp.int32, (rows, 1), 0)
    w_at = index & (width - 1)
    h_at = (index >> (width.bit_length() - 1)) & (height - 1)
    part, chans = weight_ref.shape[2:]
    blank = jnp.zeros((LANES - 3 * part, chans), weight_ref.dtype)
    total = jnp.zeros((rows, LANES), jnp.float32)
    for b in range(3):
        for c in range(3):
            shift = width * (b - 1) + (c - 1)
            moved = values if shift == 0 else pltpu.roll(values, (-shift) % rows, 0)
            h_to, w_to = h_at + (b - 1), w_at + (c - 1)
            keep = (h_to >= 0) & (h_to < height) & (w_to >= 0) & (w_to < width)
            moved = jnp.where(keep, moved, 0.0).astype(jnp.bfloat16)
            tap = 3 * b + c
            weight = jnp.concatenate([weight_ref[a, tap] for a in range(3)] + [blank], axis=0)
            total += lax.dot_general(
                moved, weight, (((1,), (1,)), ((), ())), preferred_element_type=jnp.float32
            )
    return total


def bottleneck_kernel(
    n, height, width, part,
    pooled_ref, skip_ref, deep_w_ref, deeper_w_ref, out_ref, near_ref,
    whole, deep_mine, deep_all, packed,
    send_a, recv_a, send_b, recv_b, send_c, recv_c, send_d, recv_d,
):
    me = lax.axis_index("sp")
    area = height * width
    voxels = n * area
    partner = me + 1 - 2 * (me % 2)
    half = n // 2

    barrier = pltpu.get_barrier_semaphore()

    def greet(k, carry):
        pl.semaphore_signal(
            barrier, inc=1, device_id={"sp": lax.rem(me + k, n)},
            device_id_type=pl.DeviceIdType.MESH,
        )
        return carry

    lax.fori_loop(1, n, greet, 0)
    pl.semaphore_wait(barrier, n - 1)

    def gather(mine, everyone, send_sem, recv_sem):
        def slot(source):
            return everyone.at[source]

        def direct(k):
            target = lax.rem(me + 2 * k, n)
            return remote(mine, slot(me), send_sem.at[k], recv_sem.at[me], target)

        def relay(k):
            source = lax.rem(me + 2 * (half - k), n)
            return remote(
                slot(source), slot(source), send_sem.at[half + k], recv_sem.at[source], partner
            )

        def arrival(source):
            return remote(mine, slot(source), send_sem.at[0], recv_sem.at[source], partner)

        def start_direct(k, carry):
            direct(k).start()
            return carry

        to_partner = remote(mine, slot(me), send_sem.at[0], recv_sem.at[me], partner)
        lax.fori_loop(1, half, start_direct, 0)
        to_partner.start()
        everyone[me] = mine[...]

        def pass_on(k, carry):
            arrival(lax.rem(me + 2 * (half - k), n)).wait_recv()
            relay(k).start()
            return carry

        lax.fori_loop(1, half, pass_on, 0)

        def from_partner(k, carry):
            arrival(lax.rem(partner + 2 * (half - k), n)).wait_recv()
            return carry

        lax.fori_loop(0, half, from_partner, 0)

        def finish():
            to_partner.wait_send()

            def sent(k, carry):
                direct(k).wait_send()
                relay(k).wait_send()
                return carry

            lax.fori_loop(1, half, sent, 0)

        return finish

    finish_a = gather(pooled_ref, whole, send_a, recv_a)
    depth = skip_ref.shape[0]
    finish_d = trade_edges(
        n, skip_ref.at[0], skip_ref.at[depth - 1], near_ref.at[0], near_ref.at[1], send_d, recv_d
    )
    lanes = lax.broadcasted_iota(jnp.int32, (1, voxels), 1)
    values = whole[...].astype(jnp.float32).reshape(voxels, pooled_ref.shape[1])
    deep = conv_rows(values, deep_w_ref, height, width).T
    below = jnp.where(lanes >= area, pltpu.roll(deep[0:part], area, 1), 0.0)
    above = jnp.where(
        lanes < voxels - area, pltpu.roll(deep[2 * part : 3 * part], voxels - area, 1), 0.0
    )
    deep = below + deep[part : 2 * part] + above
    deep_mine[...] = jnp.maximum(deep, 0.0).astype(jnp.bfloat16)
    finish_b = gather(deep_mine, deep_all, send_b, recv_b)

    values = deep_all[...].astype(jnp.float32).reshape(n * part, voxels).T
    deeper = conv_rows(values, deeper_w_ref, height, width)
    rows = lax.broadcasted_iota(jnp.int32, (voxels, 1), 0)

    def down(block):
        return jnp.where(rows >= area, pltpu.roll(block, area, 0), 0.0)

    def up(block):
        return jnp.where(rows < voxels - area, pltpu.roll(block, voxels - area, 0), 0.0)

    deeper = (
        down(deeper)
        + pltpu.roll(deeper, LANES - part, 1)
        + up(pltpu.roll(deeper, LANES - 2 * part, 1))
    )
    deeper = jnp.maximum(deeper, 0.0)
    lane = lax.broadcasted_iota(jnp.int32, (1, LANES), 1)
    deeper = jnp.where(
        lane < part,
        down(deeper),
        jnp.where(
            lane < 2 * part,
            pltpu.roll(deeper, part, 1),
            up(pltpu.roll(deeper, 2 * part, 1)),
        ),
    )
    packed[...] = deeper.astype(jnp.bfloat16).reshape(n, area, LANES)

    def deal(k):
        target = lax.rem(me + k, n)
        return remote(packed.at[target], out_ref.at[me], send_c.at[k], recv_c.at[me], target)

    def start_deal(k, carry):
        deal(k).start()
        return carry

    lax.fori_loop(1, n, start_deal, 0)
    out_ref[me] = packed[me]

    def receive(k, carry):
        source = lax.rem(me + k, n)
        remote(
            packed.at[source], out_ref.at[source], send_c.at[k], recv_c.at[source], source
        ).wait_recv()
        return carry

    lax.fori_loop(1, n, receive, 0)

    def sent(k, carry):
        deal(k).wait_send()
        return carry

    lax.fori_loop(1, n, sent, 0)
    finish_a()
    finish_b()
    finish_d()


def out_major(kernel):
    chans, part = kernel.shape[3], kernel.shape[4]
    return jnp.transpose(kernel, (0, 1, 2, 4, 3)).reshape(3, 9, part, chans)


def bottleneck(pooled, skip, deep_kernel, deeper_kernel):
    n = lax.axis_size("sp")
    _, height, width, chans = pooled.shape
    part = deep_kernel.shape[4]
    area = height * width
    voxels = n * area
    vmem = pl.BlockSpec(memory_space=pltpu.VMEM)
    received, near = pl.pallas_call(
        functools.partial(bottleneck_kernel, n, height, width, part),
        out_shape=(
            jax.ShapeDtypeStruct((n, area, LANES), jnp.bfloat16),
            jax.ShapeDtypeStruct((2,) + skip.shape[1:], jnp.bfloat16),
        ),
        in_specs=[vmem] * 4,
        out_specs=(vmem, vmem),
        scratch_shapes=[
            pltpu.VMEM((n, area, chans), jnp.bfloat16),
            pltpu.VMEM((part, voxels), jnp.bfloat16),
            pltpu.VMEM((n, part, voxels), jnp.bfloat16),
            pltpu.VMEM((n, area, LANES), jnp.bfloat16),
        ]
        + [pltpu.SemaphoreType.DMA((n,))] * 6
        + [pltpu.SemaphoreType.DMA((2,))] * 2,
        compiler_params=pltpu.CompilerParams(
            collective_id=0, has_side_effects=True, vmem_limit_bytes=24 << 20
        ),
        name="bottleneck",
    )(pooled.reshape(area, chans), skip, out_major(deep_kernel), out_major(deeper_kernel))
    blocks = received[:, :, : 3 * part].reshape(n, area, 3, part)
    return jnp.transpose(blocks, (2, 1, 0, 3)).reshape(3, height, width, n * part), near


def body(
    volume,
    first_kernel,
    second_kernel,
    deep_kernel,
    deeper_kernel,
    rise_kernel,
    decode_kernel,
    final_kernel,
):
    padded_pool = first_level(volume, first_kernel)
    skip = jax.nn.relu(conv_depth(padded_pool, second_kernel)).astype(jnp.bfloat16)
    pooled_two = pool_mean(skip)
    deeper_near, skip_near = bottleneck(pooled_two, skip, deep_kernel, deeper_kernel)
    padded_skip = jnp.concatenate([skip_near[:1], skip, skip_near[1:]], axis=0)
    risen = up_conv(deeper_near, rise_kernel)[1:-1].astype(jnp.bfloat16)
    padded_joined = jnp.concatenate([risen, padded_skip], axis=3)
    whole_decode_kernel = lax.all_gather(decode_kernel, "sp", axis=3, tiled=True)
    decoded = jax.nn.relu(conv_depth(padded_joined, whole_decode_kernel)).astype(jnp.bfloat16)
    return up_conv(decoded, final_kernel).astype(jnp.bfloat16)


def spread_matrix():
    out = np.zeros((6, 6, 4, 4, 16, 16), np.float32)
    for eh in range(6):
        for ew in range(6):
            for hc in range(4):
                for wc in range(4):
                    h, w = 4 * hc + eh - 1, 4 * wc + ew - 1
                    if 0 <= h < 16 and 0 <= w < 16:
                        out[eh, ew, hc, wc, h, w] = 1.0
    return out.reshape(36 * 16, 256)


def spread_matrix_two():
    out = np.zeros((4, 4, 4, 4, 2, 2, 4, 4), np.float32)
    for eh in range(4):
        for ew in range(4):
            for hc in range(4):
                for wc in range(4):
                    h, w = 2 * hc + eh - 1, 2 * wc + ew - 1
                    if 0 <= h < 8 and 0 <= w < 8:
                        out[eh, ew, hc, wc, h % 2, w % 2, h // 2, w // 2] = 1.0
    return out.reshape(16 * 16, 64)


def gather_matrix():
    out = np.zeros((16, 16, 4, 4, 4, 4), np.float32)
    for h in range(16):
        for w in range(16):
            out[h, w, h % 4, w % 4, h // 4, w // 4] = 1.0
    return out.reshape(256, 256)


def block_transpose(pieces, width):
    pieces = list(pieces)
    count = len(pieces)
    block = lax.broadcasted_iota(jnp.int32, pieces[0].shape, 1) // width
    step = 1
    while step < count:
        low = (block & step) == 0
        for i in range(count):
            if i & step:
                continue
            a, b = pieces[i], pieces[i + step]
            pieces[i] = jnp.where(low, a, pltpu.roll(b, width * step, 1))
            pieces[i + step] = jnp.where(low, pltpu.roll(a, 128 - width * step, 1), b)
        step *= 2
    return pieces


def moved(values, by, keep):
    lanes = values.shape[1]
    return jnp.where(keep, pltpu.roll(values, by % lanes, 1), 0.0)


class Lanes:
    def __init__(self, count):
        lane = lax.broadcasted_iota(jnp.int32, (1, count), 1)
        wc, hc, d = lane & 3, (lane >> 2) & 3, lane >> 4
        top = count // 16 - 1
        self.after = {1: wc > 0, 4: hc > 0, 16: d > 0}
        self.before = {1: wc < 3, 4: hc < 3, 16: d < top}

    def back(self, values, by):
        return moved(values, by, self.after[by])

    def ahead(self, values, by):
        return moved(values, -by, self.before[by])


def add_taps(lanes, y, outs):
    def row(a, b, c):
        at = (9 * a + 3 * b + c) * outs
        return y[at : at + outs]

    def tall(c):
        return jnp.concatenate([row(a, b, c) for b in range(3) for a in range(3)], axis=0)

    y = tall(1) + lanes.back(tall(0), 1) + lanes.ahead(tall(2), 1)
    y = [y[i * 3 * outs : (i + 1) * 3 * outs] for i in range(3)]
    y = y[1] + lanes.back(y[0], 4) + lanes.ahead(y[2], 4)
    y = [y[i * outs : (i + 1) * outs] for i in range(3)]
    return y[1] + lanes.back(y[0], 16) + lanes.ahead(y[2], 16)


def add_fine_taps(lanes, load, outs):
    def pair(zero, one, by):
        even = zero[1] + one[2] + lanes.back(one[0], by)
        odd = one[1] + zero[0] + lanes.ahead(zero[2], by)
        return even, odd

    planes = {}
    for pd in range(2):
        rows = {}
        for ph in range(2):
            def taps(pw):
                p = 4 * pd + 2 * ph + pw
                return [
                    jnp.concatenate(
                        [load(p, 9 * a + 3 * b + c) for b in range(3) for a in range(3)], axis=0
                    )
                    for c in range(3)
                ]

            rows[ph] = pair(taps(0), taps(1), 1)
        for qw in range(2):
            def cut(ph):
                return [rows[ph][qw][i * 3 * outs : (i + 1) * 3 * outs] for i in range(3)]

            planes[pd, qw] = pair(cut(0), cut(1), 4)
    result = [None] * 8
    for qw in range(2):
        for qh in range(2):
            def cut(pd):
                return [planes[pd, qw][qh][i * outs : (i + 1) * outs] for i in range(3)]

            low, high = pair(cut(0), cut(1), 16)
            result[2 * qh + qw] = low
            result[4 + 2 * qh + qw] = high
    return result


class Gather:
    def __init__(self, n, slots, send_sem, recv_sem):
        self.n, self.slots, self.send_sem, self.recv_sem = n, slots, send_sem, recv_sem
        self.me = lax.axis_index("sp")
        self.sent = []
        self.others = list(range(n - 2, 0, -2))

    def send(self, source, target):
        slot = self.slots.at[self.me ^ source]
        copy = remote(
            slot, slot, self.send_sem.at[len(self.sent)], self.recv_sem.at[source ^ target],
            self.me ^ target,
        )
        copy.start()
        self.sent.append(copy)

    def wait(self, source):
        slot = self.slots.at[self.me ^ source]
        remote(slot, slot, self.send_sem.at[0], self.recv_sem.at[source], self.me ^ 1).wait_recv()

    def start(self):
        for k in self.others:
            self.send(0, k)
        self.send(0, 1)

    def relay(self):
        for k in reversed(self.others):
            self.wait(k)
            self.send(k, 1)

    def finish(self):
        for k in range(1, self.n, 2):
            self.wait(k)

    def pass_on(self, source, *targets):
        self.wait(source)
        for target in targets:
            self.send(source, target)

    def drain(self):
        for copy in self.sent:
            copy.wait_send()


class Doubling(Gather):
    def steps(self):
        bits = [1 << i for i in range(self.n.bit_length() - 1)]
        known = [[0]]
        for _ in bits:
            known.append([k | bit for k in known[-1] for bit in bits if bit < (k & -k or self.n)])
        return bits, known

    def start(self):
        bits, _ = self.steps()
        for bit in reversed(bits):
            self.send(0, bit)

    def hop(self, step):
        bits, known = self.steps()
        for k in known[step]:
            self.pass_on(k, *[bit for bit in reversed(bits) if bit < (k & -k)])


def net_kernel(
    n,
    volume_hbm, first_hbm, second_hbm, deep_hbm, deeper_hbm, rise_hbm, decode_hbm,
    spread_hbm, spread_two_hbm,
    out_ref,
    vol, vhalo, pp, pp2, wpair, w2, wd, wdd, rw, kloc,
    ex, pool, ex2, pooled_all, deep_all, deeper_all, skip_all,
    wsend, wall, wt, ys, dsend,
    load_sem, send_v, recv_v, send_p, recv_p,
    send_a, recv_a, send_b, recv_b, send_c, recv_c, send_s, recv_s,
    send_w, recv_w, send_f, recv_f, send_d, recv_d,
):
    me = lax.axis_index("sp")
    bf = jnp.bfloat16
    f32 = jnp.float32
    depth = vol.shape[0]
    k1 = first_hbm.shape[1]
    part = wd.shape[0] // 27
    outs = 256 // n
    coarse = 16 * n

    loads = []

    def load(src, dst):
        copy = pltpu.make_async_copy(src, dst, load_sem.at[len(loads)])
        copy.start()
        loads.append(copy)
        return copy

    get_vol = load(volume_hbm, vol)
    get_pp = load(spread_hbm, pp)
    get_k = load(decode_hbm, kloc)
    get_w1 = [
        load(first_hbm.at[1], wpair.at[0:k1, 0:128]),
        load(first_hbm.at[0], wpair.at[0:k1, 128:256]),
        load(first_hbm.at[2], wpair.at[k1 : 2 * k1, 0:128]),
        load(first_hbm.at[1], wpair.at[k1 : 2 * k1, 128:256]),
    ]
    get_pp2 = load(spread_two_hbm, pp2)
    get_w2 = load(second_hbm, w2)
    get_wd = load(deep_hbm, wd)
    get_wdd = load(deeper_hbm, wdd)
    get_rw = load(rise_hbm, rw)

    barrier = pltpu.get_barrier_semaphore()
    for k in range(n - 1, 0, -1):
        pl.semaphore_signal(
            barrier, inc=1, device_id={"sp": me ^ k}, device_id_type=pl.DeviceIdType.MESH
        )

    twin = lax.axis_index("rep")
    pl.semaphore_signal(
        barrier, inc=1, device_id={"rep": 1 - twin, "sp": me},
        device_id_type=pl.DeviceIdType.MESH,
    )

    def spread(planes, to):
        get = jnp.concatenate(planes, axis=1)
        result = jnp.dot(pp[...], get, preferred_element_type=f32).astype(bf)
        for i, at in enumerate(to):
            ex[at] = result[:, 128 * i : 128 * (i + 1)]

    get_vol.wait()
    get_pp.wait()
    for d in range(0, depth, 2):
        spread([vol[d], vol[d + 1]], [d + 1, d + 2])

    get_k.wait()
    per = 128 // outs
    for half in range(256 // 128):
        for group in range(wsend.shape[2] // 128):
            taps = []
            for i in range(per):
                tap = per * group + i
                if tap < 27:
                    taps.append(kloc[tap, :, 128 * half : 128 * (half + 1)].astype(f32))
                else:
                    taps.append(jnp.zeros((kloc.shape[1], 128), f32))
            for j, piece in enumerate(block_transpose(taps, outs)):
                wsend[per * half + j, :, 128 * group : 128 * (group + 1)] = piece.astype(bf)

    pl.semaphore_wait(barrier, n)
    finish_v = trade_edges(
        n, vol.at[0], vol.at[depth - 1], vhalo.at[0], vhalo.at[1], send_v, recv_v
    )
    w_copies = []

    def w_piece(k):
        return remote(wsend.at[me ^ k], wall.at[me], send_w.at[k], recv_w.at[k], me ^ k)

    def w_arrived(k):
        slot = wall.at[me ^ k]
        remote(slot, slot, send_w.at[k], recv_w.at[k], me ^ 1).wait_recv()

    def w_start(*steps):
        for k in [2 * i + twin for i in steps] if steps else [1]:
            copy = w_piece(k)
            copy.start()
            w_copies.append(copy)

    def w_forward():
        for i in range(1, n // 2):
            k = 2 * i + twin
            w_arrived(k)
            slot = wall.at[me ^ k]
            copy = pltpu.make_async_remote_copy(
                src_ref=slot, dst_ref=slot, send_sem=send_f.at[i], recv_sem=recv_f.at[i],
                device_id={"rep": 1 - twin, "sp": me}, device_id_type=pl.DeviceIdType.MESH,
            )
            copy.start()
            w_copies.append(copy)

    def w_finish():
        w_arrived(1)
        for i in range(1, n // 2):
            slot = wall.at[me ^ (2 * i + 1 - twin)]
            pltpu.make_async_remote_copy(
                src_ref=slot, dst_ref=slot, send_sem=send_f.at[i], recv_sem=recv_f.at[i],
                device_id={"rep": 1 - twin, "sp": me}, device_id_type=pl.DeviceIdType.MESH,
            ).wait_recv()

    w_start()
    steps = list(range(n // 2 - 1, 0, -1))
    w_start(*steps[0::2])
    wall[me] = wsend[me]

    def taken(at, b):
        columns = []
        for c in range(3):
            columns.append(
                jnp.concatenate(
                    [ex[at, pl.ds(((b + hm) * 6 + c) * 16, 64), :] for hm in range(4)], axis=0
                )
            )
        return columns

    def rows_of(at):
        return jnp.concatenate(sum([taken(at, b) for b in range(3)], []), axis=1)

    for copy in get_w1:
        copy.wait()

    def both(at):
        left = jnp.concatenate([rows_of(at), rows_of(at + 1)], axis=1)
        return jnp.dot(left, wpair[...], preferred_element_type=f32)

    pairs = [both(1), both(3)]
    own_low = jnp.dot(rows_of(2), wpair[0:k1, 128:256], preferred_element_type=f32)
    own_high = jnp.dot(rows_of(3), wpair[k1 : 2 * k1, 0:128], preferred_element_type=f32)
    finish_v()
    spread([vhalo[0], vhalo[1]], [0, depth + 1])
    far_low = jnp.dot(rows_of(0), wpair[0:k1, 128:256], preferred_element_type=f32)
    far_high = jnp.dot(rows_of(5), wpair[k1 : 2 * k1, 0:128], preferred_element_type=f32)
    planes = [
        pairs[0][:, 0:128] + far_low,
        pairs[0][:, 128:256] + own_high,
        pairs[1][:, 0:128] + own_low,
        pairs[1][:, 128:256] + far_high,
    ]
    planes = [jnp.maximum(t, 0.0).astype(bf).astype(f32) for t in planes]
    for i in range(2):
        total = planes[2 * i] + planes[2 * i + 1]
        for ph in range(2):
            for pw in range(2):
                slabs = [
                    total[((2 * ph + y) * 4 + 2 * pw + x) * 16 :][:16]
                    for y in range(2) for x in range(2)
                ]
                slab = (slabs[0] + slabs[1]) + (slabs[2] + slabs[3])
                pool[1 + i, pl.ds((2 * ph + pw) * 16, 16), :] = (slab * 0.125).astype(bf)

    finish_p = trade_edges(n, pool.at[1], pool.at[2], pool.at[0], pool.at[3], send_p, recv_p)
    if steps[1::2]:
        w_start(*steps[1::2])
    get_pp2.wait()
    get_w2.wait()

    def spread_two(at):
        ex2[at] = jnp.dot(pp2[...], pool[at], preferred_element_type=f32).astype(bf)

    def rows_two(a):
        columns = []
        for b in range(3):
            for c in range(3):
                columns.append(
                    jnp.concatenate(
                        [
                            ex2[a + i, pl.ds(((b + ph) * 4 + c) * 16, 32), :]
                            for i in range(2) for ph in range(2)
                        ],
                        axis=0,
                    )
                )
        return jnp.concatenate(columns, axis=1)

    spread_two(1)
    spread_two(2)
    skip = jnp.dot(rows_two(1), w2[1], preferred_element_type=f32)
    finish_p()
    spread_two(0)
    spread_two(3)
    skip += jnp.dot(rows_two(0), w2[0], preferred_element_type=f32)
    skip += jnp.dot(rows_two(2), w2[2], preferred_element_type=f32)
    skip = jnp.maximum(skip, 0.0).astype(bf)
    skip_all[me] = skip.reshape(skip_all.shape[1:])
    skip = skip.astype(f32)
    slabs = [skip[16 * i : 16 * (i + 1)] for i in range(8)]
    while len(slabs) > 1:
        slabs = [slabs[i] + slabs[i + 1] for i in range(0, len(slabs), 2)]
    pooled_all[me] = (slabs[0] * 0.125).astype(bf)

    gather_a = Gather(n, pooled_all, send_a, recv_a)
    gather_b = Gather(n, deep_all, send_b, recv_b)
    gather_c = Gather(n, deeper_all, send_c, recv_c)
    gather_s = Doubling(n, skip_all, send_s, recv_s)
    gather_a.start()
    gather_s.start()
    lanes = Lanes(coarse)
    get_wd.wait()
    get_wdd.wait()
    get_rw.wait()
    gather_a.relay()
    w_forward()
    gather_a.finish()
    y = lax.dot_general(
        wd[...], pooled_all[...].reshape(coarse, pooled_all.shape[2]),
        (((1,), (1,)), ((), ())), preferred_element_type=f32,
    )
    deep_all[me] = jnp.maximum(add_taps(lanes, y, part), 0.0).astype(bf)
    gather_b.start()
    gather_s.hop(1)
    gather_b.relay()
    gather_b.finish()
    y = jnp.dot(
        wdd[...], deep_all[...].reshape(n * part, coarse), preferred_element_type=f32
    )
    deeper_all[me] = jnp.maximum(add_taps(lanes, y, part), 0.0).astype(bf)
    gather_c.start()
    gather_s.hop(2)
    w_finish()
    for at in range(0, wt.shape[1], 128):
        block = wall[pl.ds(at // part, 128 // part)].reshape(128, wall.shape[2])
        wt[:, at : at + 128] = block.astype(f32).T.astype(bf)[0 : wt.shape[0]]
    gather_s.hop(3)
    gather_s.hop(4)

    def fine(p, values, inner):
        ys[p] = lax.dot_general(
            wt[:, inner], values, (((1,), (1,)), ((), ())), preferred_element_type=f32
        )

    def tap_of(p, tap):
        return ys[p, outs * tap : outs * (tap + 1), :]

    for p in range(8):
        fine(p, skip_all[:, p].reshape(coarse, skip_all.shape[3]), slice(256, 512))
    from_skip = add_fine_taps(lanes, tap_of, outs)
    gather_c.relay()
    gather_c.finish()
    deeper = deeper_all[...].reshape(n * part, coarse).astype(f32).T.astype(bf)
    for p in range(8):
        risen = jnp.dot(deeper, rw[p], preferred_element_type=f32).astype(bf)
        fine(p, risen, slice(0, 256))
    from_risen = add_fine_taps(lanes, tap_of, outs)
    decoded = [jnp.maximum(s + r, 0.0) for s, r in zip(from_skip, from_risen)]
    for half in range(coarse // 128):
        cut = [t[:, 128 * half : 128 * (half + 1)] for t in decoded]
        for j, piece in enumerate(block_transpose(cut, 16)):
            dsend[8 * half + j] = piece.astype(bf)
    d_copies = []
    for k in range(n - 1, 0, -1):
        copy = remote(dsend.at[me ^ k], out_ref.at[me], send_d.at[k], recv_d.at[k], me ^ k)
        copy.start()
        d_copies.append(copy)
    out_ref[me] = dsend[me]
    for k in range(1, n):
        remote(dsend.at[me ^ k], out_ref.at[me ^ k], send_d.at[k], recv_d.at[k], me ^ k).wait_recv()
    for copy in w_copies + d_copies:
        copy.wait_send()
    for gather in (gather_a, gather_b, gather_c, gather_s):
        gather.drain()


def net(volume, first_kernel, second_kernel, deep_kernel, deeper_kernel, rise_kernel, decode_kernel):
    n = lax.axis_size("sp")
    depth, height, width, chans = volume.shape
    mid = second_kernel.shape[4]
    low = rise_kernel.shape[3]
    part = deep_kernel.shape[4]
    block = decode_kernel.shape[3]
    outs = mid // n
    coarse = 16 * n
    area = height * width
    taps = 27 * outs
    wide = -(-taps // LANES) * LANES
    bf = jnp.bfloat16
    vmem = pltpu.VMEM
    dma = pltpu.SemaphoreType.DMA
    hbm = pl.BlockSpec(memory_space=pltpu.HBM)

    def tap_rows(kernel):
        return jnp.transpose(kernel, (0, 1, 2, 4, 3)).reshape(27 * part, kernel.shape[3])

    return pl.pallas_call(
        functools.partial(net_kernel, n),
        out_shape=jax.ShapeDtypeStruct((n, outs, 128), bf),
        in_specs=[hbm] * 9,
        out_specs=pl.BlockSpec(memory_space=pltpu.VMEM),
        scratch_shapes=[
            vmem((depth, area, chans), bf),
            vmem((2, area, chans), bf),
            vmem((36 * 16, area), bf),
            vmem((16 * 16, area // 4), bf),
            vmem((18 * chans, 2 * chans), bf),
            vmem((3, 9 * chans, mid), bf),
            vmem((27 * part, mid), bf),
            vmem((27 * part, low), bf),
            vmem((8, low, mid), bf),
            vmem((27, block, mid), bf),
            vmem((depth + 2, 36 * 16, chans), bf),
            vmem((depth // 2 + 2, area // 4, chans), bf),
            vmem((depth // 2 + 2, 16 * 16, chans), bf),
            vmem((n, 16, mid), bf),
            vmem((n, part, coarse), bf),
            vmem((n, part, coarse), bf),
            vmem((n, 8, 16, mid), bf),
            vmem((n, block, wide), bf),
            vmem((n, block, wide), bf),
            vmem((taps, 2 * mid), bf),
            vmem((8, taps, coarse), jnp.float32),
            vmem((n, outs, 128), bf),
            dma((16,)),
            dma((2,)), dma((2,)), dma((2,)), dma((2,)),
            dma((2 * n,)), dma((n,)), dma((2 * n,)), dma((n,)),
            dma((2 * n,)), dma((n,)), dma((2 * n,)), dma((n,)),
            dma((n,)), dma((n,)), dma((n,)), dma((n,)), dma((n,)), dma((n,)),
        ],
        compiler_params=pltpu.CompilerParams(
            collective_id=2, has_side_effects=True, vmem_limit_bytes=60 << 20
        ),
        name="net",
    )(
        volume.reshape(depth, area, chans),
        first_kernel.reshape(3, 9 * chans, chans),
        second_kernel.reshape(3, 9 * chans, mid),
        tap_rows(deep_kernel),
        tap_rows(deeper_kernel),
        rise_kernel.reshape(8, low, mid),
        decode_kernel.reshape(27, block, mid),
        jnp.asarray(spread_matrix(), bf),
        jnp.asarray(spread_matrix_two(), bf),
    )


def last_kernel(decoded_ref, weight_ref, order_ref, out_ref):
    f32, bf = jnp.float32, jnp.bfloat16
    decoded = decoded_ref[...].astype(f32).T.astype(bf)
    slabs = {}
    for a in range(2):
        for b in range(2):
            for c in range(2):
                t = jnp.dot(
                    decoded, weight_ref[4 * a + 2 * b + c], preferred_element_type=f32
                ).astype(bf)
                for p in range(8):
                    at = (2 * (p // 4) + a, 2 * (p // 2 % 2) + b, 2 * (p % 2) + c)
                    slabs[at] = t[16 * p : 16 * (p + 1)]
    for d in range(0, 4, 2):
        plane = jnp.concatenate(
            [
                jnp.concatenate([slabs[d + i, y, x] for y in range(4) for x in range(4)], axis=0)
                for i in range(2)
            ],
            axis=1,
        )
        plane = jnp.dot(order_ref[...], plane, preferred_element_type=f32).astype(bf)
        out_ref[d] = plane[:, 0:128]
        out_ref[d + 1] = plane[:, 128:256]


def last(decoded, final_kernel):
    mid, chans = final_kernel.shape[3:]
    return pl.pallas_call(
        last_kernel,
        out_shape=jax.ShapeDtypeStruct((4, 256, chans), jnp.bfloat16),
        in_specs=[pl.BlockSpec(memory_space=pltpu.VMEM)] * 3,
        out_specs=pl.BlockSpec(memory_space=pltpu.VMEM),
        name="last",
    )(
        decoded.reshape(mid, 128),
        final_kernel.reshape(8, mid, chans),
        jnp.asarray(gather_matrix(), jnp.bfloat16),
    ).reshape(4, 16, 16, chans)


def split_body(
    volume, first_kernel, second_kernel, deep_kernel, deeper_kernel,
    rise_kernel, decode_kernel, final_kernel,
):
    n = lax.axis_size("sp")
    if n & (n - 1) or lax.axis_size("rep") != 2 or decode_kernel.shape[4] % (16 * n) or decode_kernel.shape[3] % 16:
        return body(
            volume, first_kernel, second_kernel, deep_kernel, deeper_kernel,
            rise_kernel, decode_kernel, final_kernel,
        )
    decoded = net(
        volume, first_kernel, second_kernel, deep_kernel, deeper_kernel, rise_kernel, decode_kernel
    )
    return last(decoded, final_kernel)


def solution(mesh):
    return jax.shard_map(
        split_body,
        mesh=mesh,
        in_specs=(
            P(("rep", "sp"), None, None, None),
            P(),
            P(),
            P(None, None, None, None, "sp"),
            P(None, None, None, None, "sp"),
            P(),
            P(None, None, None, "sp", None),
            P(),
        ),
        out_specs=P(("rep", "sp"), None, None, None),
        check_vma=False,
    )
```

```python
import functools

import jax
import jax.numpy as jnp
from jax import lax
from jax.experimental import pallas as pl
from jax.experimental.pallas import tpu as pltpu
from jax.sharding import PartitionSpec as P

LANES = 128


def remote(src, dst, send_sem, recv_sem, target):
    return pltpu.make_async_remote_copy(
        src_ref=src, dst_ref=dst, send_sem=send_sem, recv_sem=recv_sem,
        device_id={"sp": target}, device_id_type=pl.DeviceIdType.MESH,
    )


def trade_edges(n, first, last, low, high, send_sem, recv_sem):
    me = lax.axis_index("sp")
    upward = remote(last, low, send_sem.at[0], recv_sem.at[0], lax.rem(me + 1, n))
    downward = remote(first, high, send_sem.at[1], recv_sem.at[1], lax.rem(me + n - 1, n))

    @pl.when(me < n - 1)
    def _():
        upward.start()

    @pl.when(me > 0)
    def _():
        downward.start()

    @pl.when(me == 0)
    def _():
        low[...] = jnp.zeros(low.shape, low.dtype)

    @pl.when(me == n - 1)
    def _():
        high[...] = jnp.zeros(high.shape, high.dtype)

    def finish():
        @pl.when(me > 0)
        def _():
            upward.wait_recv()
            downward.wait_send()

        @pl.when(me < n - 1)
        def _():
            downward.wait_recv()
            upward.wait_send()

    return finish


def greet_neighbours(n):
    me = lax.axis_index("sp")
    barrier = pltpu.get_barrier_semaphore()

    @pl.when(me > 0)
    def _():
        pl.semaphore_signal(
            barrier, inc=1, device_id={"sp": lax.rem(me + n - 1, n)},
            device_id_type=pl.DeviceIdType.MESH,
        )

    @pl.when(me < n - 1)
    def _():
        pl.semaphore_signal(
            barrier, inc=1, device_id={"sp": lax.rem(me + 1, n)},
            device_id_type=pl.DeviceIdType.MESH,
        )

    @pl.when((me > 0) & (me < n - 1))
    def _():
        pl.semaphore_wait(barrier, 2)

    @pl.when((me == 0) | (me == n - 1))
    def _():
        pl.semaphore_wait(barrier, 1)


def first_level_kernel(
    n, depth, height, width,
    volume_ref, weight_ref, out_ref,
    ends, taps, sums, send_a, recv_a, send_b, recv_b,
):
    area = height * width
    chans = volume_ref.shape[2]
    greet_neighbours(n)
    finish = trade_edges(
        n, volume_ref.at[0], volume_ref.at[depth - 1], ends.at[0], ends.at[1], send_a, recv_a
    )
    index = lax.broadcasted_iota(jnp.int32, (area, 1), 0) & (width - 1)
    blank = jnp.zeros((depth + 2, width, 3 * chans), jnp.bfloat16)
    taps[:, 0:width] = blank
    taps[:, area + width : area + 2 * width] = blank

    def spread(at, values):
        taps[at, width : area + width, chans : 2 * chans] = values
        values = values.astype(jnp.float32)
        left = jnp.where(index > 0, pltpu.roll(values, 1, 0), 0.0)
        right = jnp.where(index < width - 1, pltpu.roll(values, area - 1, 0), 0.0)
        taps[at, width : area + width, 0:chans] = left.astype(jnp.bfloat16)
        taps[at, width : area + width, 2 * chans : 3 * chans] = right.astype(jnp.bfloat16)

    for d in range(depth):
        spread(d + 1, volume_ref[d])
    finish()
    spread(0, ends[0])
    spread(depth + 1, ends[1])
    for pair in range(depth // 2):
        total = jnp.zeros((2 * area, weight_ref.shape[3]), jnp.float32)
        for a in range(3):
            for b in range(3):
                block = taps[2 * pair + a : 2 * pair + a + 2, b * width : b * width + area]
                total += jnp.dot(
                    block.reshape(2 * area, 3 * chans), weight_ref[a, b],
                    preferred_element_type=jnp.float32,
                )
        total = jnp.maximum(total, 0.0).astype(jnp.bfloat16).astype(jnp.float32)
        total = total[0:area] + total[area : 2 * area]
        total = total.reshape(height // 2, 2, width, total.shape[1]).sum(axis=1)
        sums[...] = total.reshape(area // 2, total.shape[2])
        total = sums[pl.ds(0, area // 4, 2), :] + sums[pl.ds(1, area // 4, 2), :]
        out_ref[1 + pair] = (total * 0.125).astype(jnp.bfloat16)
    halves = depth // 2
    trade_edges(
        n, out_ref.at[1], out_ref.at[halves], out_ref.at[0], out_ref.at[halves + 1],
        send_b, recv_b,
    )()


def first_level(volume, kernel):
    n = lax.axis_size("sp")
    depth, height, width, chans = volume.shape
    outs = kernel.shape[4]
    area = height * width
    vmem = pl.BlockSpec(memory_space=pltpu.VMEM)
    padded = pl.pallas_call(
        functools.partial(first_level_kernel, n, depth, height, width),
        out_shape=jax.ShapeDtypeStruct((depth // 2 + 2, area // 4, outs), jnp.bfloat16),
        in_specs=[vmem] * 2,
        out_specs=vmem,
        scratch_shapes=[
            pltpu.VMEM((2, area, chans), jnp.bfloat16),
            pltpu.VMEM((depth + 2, area + 2 * width, 3 * chans), jnp.bfloat16),
            pltpu.VMEM((area // 2, outs), jnp.float32),
        ]
        + [pltpu.SemaphoreType.DMA((2,))] * 4,
        compiler_params=pltpu.CompilerParams(
            collective_id=1, has_side_effects=True, vmem_limit_bytes=16 << 20
        ),
        name="first_level",
    )(volume.reshape(depth, area, chans), kernel.reshape(3, 3, 3 * chans, outs))
    return padded.reshape(depth // 2 + 2, height // 2, width // 2, outs)


def conv_depth(padded, kernel):
    result = lax.conv_general_dilated(
        padded[None],
        kernel,
        (1, 1, 1),
        ((0, 0), (1, 1), (1, 1)),
        dimension_numbers=("NDHWC", "DHWIO", "NDHWC"),
        preferred_element_type=jnp.float32,
    )
    return result[0]


def pool_mean(values):
    depth, height, width, chans = values.shape
    blocks = values.astype(jnp.float32).reshape(depth // 2, 2, height // 2, 2, width // 2, 2, chans)
    return jnp.mean(blocks, axis=(1, 3, 5)).astype(jnp.bfloat16)


def up_conv(values, kernel):
    depth, height, width, chans = values.shape
    result = jnp.einsum("dhwi,abcio->dahbwco", values, kernel, preferred_element_type=jnp.float32)
    return result.reshape(2 * depth, 2 * height, 2 * width, kernel.shape[4])


def conv_rows(values, weight_ref, height, width):
    rows = values.shape[0]
    index = lax.broadcasted_iota(jnp.int32, (rows, 1), 0)
    w_at = index & (width - 1)
    h_at = (index >> (width.bit_length() - 1)) & (height - 1)
    part, chans = weight_ref.shape[2:]
    blank = jnp.zeros((LANES - 3 * part, chans), weight_ref.dtype)
    total = jnp.zeros((rows, LANES), jnp.float32)
    for b in range(3):
        for c in range(3):
            shift = width * (b - 1) + (c - 1)
            moved = values if shift == 0 else pltpu.roll(values, (-shift) % rows, 0)
            h_to, w_to = h_at + (b - 1), w_at + (c - 1)
            keep = (h_to >= 0) & (h_to < height) & (w_to >= 0) & (w_to < width)
            moved = jnp.where(keep, moved, 0.0).astype(jnp.bfloat16)
            tap = 3 * b + c
            weight = jnp.concatenate([weight_ref[a, tap] for a in range(3)] + [blank], axis=0)
            total += lax.dot_general(
                moved, weight, (((1,), (1,)), ((), ())), preferred_element_type=jnp.float32
            )
    return total


def bottleneck_kernel(
    n, height, width, part,
    pooled_ref, skip_ref, deep_w_ref, deeper_w_ref, out_ref, near_ref,
    whole, deep_mine, deep_all, packed,
    send_a, recv_a, send_b, recv_b, send_c, recv_c, send_d, recv_d,
):
    me = lax.axis_index("sp")
    area = height * width
    voxels = n * area
    partner = me + 1 - 2 * (me % 2)
    half = n // 2

    barrier = pltpu.get_barrier_semaphore()

    def greet(k, carry):
        pl.semaphore_signal(
            barrier, inc=1, device_id={"sp": lax.rem(me + k, n)},
            device_id_type=pl.DeviceIdType.MESH,
        )
        return carry

    lax.fori_loop(1, n, greet, 0)
    pl.semaphore_wait(barrier, n - 1)

    def gather(mine, everyone, send_sem, recv_sem):
        def slot(source):
            return everyone.at[source]

        def direct(k):
            target = lax.rem(me + 2 * k, n)
            return remote(mine, slot(me), send_sem.at[k], recv_sem.at[me], target)

        def relay(k):
            source = lax.rem(me + 2 * (half - k), n)
            return remote(
                slot(source), slot(source), send_sem.at[half + k], recv_sem.at[source], partner
            )

        def arrival(source):
            return remote(mine, slot(source), send_sem.at[0], recv_sem.at[source], partner)

        def start_direct(k, carry):
            direct(k).start()
            return carry

        to_partner = remote(mine, slot(me), send_sem.at[0], recv_sem.at[me], partner)
        lax.fori_loop(1, half, start_direct, 0)
        to_partner.start()
        everyone[me] = mine[...]

        def pass_on(k, carry):
            arrival(lax.rem(me + 2 * (half - k), n)).wait_recv()
            relay(k).start()
            return carry

        lax.fori_loop(1, half, pass_on, 0)

        def from_partner(k, carry):
            arrival(lax.rem(partner + 2 * (half - k), n)).wait_recv()
            return carry

        lax.fori_loop(0, half, from_partner, 0)

        def finish():
            to_partner.wait_send()

            def sent(k, carry):
                direct(k).wait_send()
                relay(k).wait_send()
                return carry

            lax.fori_loop(1, half, sent, 0)

        return finish

    finish_a = gather(pooled_ref, whole, send_a, recv_a)
    depth = skip_ref.shape[0]
    finish_d = trade_edges(
        n, skip_ref.at[0], skip_ref.at[depth - 1], near_ref.at[0], near_ref.at[1], send_d, recv_d
    )
    lanes = lax.broadcasted_iota(jnp.int32, (1, voxels), 1)
    values = whole[...].astype(jnp.float32).reshape(voxels, pooled_ref.shape[1])
    deep = conv_rows(values, deep_w_ref, height, width).T
    below = jnp.where(lanes >= area, pltpu.roll(deep[0:part], area, 1), 0.0)
    above = jnp.where(
        lanes < voxels - area, pltpu.roll(deep[2 * part : 3 * part], voxels - area, 1), 0.0
    )
    deep = below + deep[part : 2 * part] + above
    deep_mine[...] = jnp.maximum(deep, 0.0).astype(jnp.bfloat16)
    finish_b = gather(deep_mine, deep_all, send_b, recv_b)

    values = deep_all[...].astype(jnp.float32).reshape(n * part, voxels).T
    deeper = conv_rows(values, deeper_w_ref, height, width)
    rows = lax.broadcasted_iota(jnp.int32, (voxels, 1), 0)

    def down(block):
        return jnp.where(rows >= area, pltpu.roll(block, area, 0), 0.0)

    def up(block):
        return jnp.where(rows < voxels - area, pltpu.roll(block, voxels - area, 0), 0.0)

    deeper = (
        down(deeper)
        + pltpu.roll(deeper, LANES - part, 1)
        + up(pltpu.roll(deeper, LANES - 2 * part, 1))
    )
    deeper = jnp.maximum(deeper, 0.0)
    lane = lax.broadcasted_iota(jnp.int32, (1, LANES), 1)
    deeper = jnp.where(
        lane < part,
        down(deeper),
        jnp.where(
            lane < 2 * part,
            pltpu.roll(deeper, part, 1),
            up(pltpu.roll(deeper, 2 * part, 1)),
        ),
    )
    packed[...] = deeper.astype(jnp.bfloat16).reshape(n, area, LANES)

    def deal(k):
        target = lax.rem(me + k, n)
        return remote(packed.at[target], out_ref.at[me], send_c.at[k], recv_c.at[me], target)

    def start_deal(k, carry):
        deal(k).start()
        return carry

    lax.fori_loop(1, n, start_deal, 0)
    out_ref[me] = packed[me]

    def receive(k, carry):
        source = lax.rem(me + k, n)
        remote(
            packed.at[source], out_ref.at[source], send_c.at[k], recv_c.at[source], source
        ).wait_recv()
        return carry

    lax.fori_loop(1, n, receive, 0)

    def sent(k, carry):
        deal(k).wait_send()
        return carry

    lax.fori_loop(1, n, sent, 0)
    finish_a()
    finish_b()
    finish_d()


def out_major(kernel):
    chans, part = kernel.shape[3], kernel.shape[4]
    return jnp.transpose(kernel, (0, 1, 2, 4, 3)).reshape(3, 9, part, chans)


def bottleneck(pooled, skip, deep_kernel, deeper_kernel):
    n = lax.axis_size("sp")
    _, height, width, chans = pooled.shape
    part = deep_kernel.shape[4]
    area = height * width
    voxels = n * area
    vmem = pl.BlockSpec(memory_space=pltpu.VMEM)
    received, near = pl.pallas_call(
        functools.partial(bottleneck_kernel, n, height, width, part),
        out_shape=(
            jax.ShapeDtypeStruct((n, area, LANES), jnp.bfloat16),
            jax.ShapeDtypeStruct((2,) + skip.shape[1:], jnp.bfloat16),
        ),
        in_specs=[vmem] * 4,
        out_specs=(vmem, vmem),
        scratch_shapes=[
            pltpu.VMEM((n, area, chans), jnp.bfloat16),
            pltpu.VMEM((part, voxels), jnp.bfloat16),
            pltpu.VMEM((n, part, voxels), jnp.bfloat16),
            pltpu.VMEM((n, area, LANES), jnp.bfloat16),
        ]
        + [pltpu.SemaphoreType.DMA((n,))] * 6
        + [pltpu.SemaphoreType.DMA((2,))] * 2,
        compiler_params=pltpu.CompilerParams(
            collective_id=0, has_side_effects=True, vmem_limit_bytes=24 << 20
        ),
        name="bottleneck",
    )(pooled.reshape(area, chans), skip, out_major(deep_kernel), out_major(deeper_kernel))
    blocks = received[:, :, : 3 * part].reshape(n, area, 3, part)
    return jnp.transpose(blocks, (2, 1, 0, 3)).reshape(3, height, width, n * part), near


def body(
    volume,
    first_kernel,
    second_kernel,
    deep_kernel,
    deeper_kernel,
    rise_kernel,
    decode_kernel,
    final_kernel,
):
    padded_pool = first_level(volume, first_kernel)
    skip = jax.nn.relu(conv_depth(padded_pool, second_kernel)).astype(jnp.bfloat16)
    pooled_two = pool_mean(skip)
    deeper_near, skip_near = bottleneck(pooled_two, skip, deep_kernel, deeper_kernel)
    padded_skip = jnp.concatenate([skip_near[:1], skip, skip_near[1:]], axis=0)
    risen = up_conv(deeper_near, rise_kernel)[1:-1].astype(jnp.bfloat16)
    padded_joined = jnp.concatenate([risen, padded_skip], axis=3)
    whole_decode_kernel = lax.all_gather(decode_kernel, "sp", axis=3, tiled=True)
    decoded = jax.nn.relu(conv_depth(padded_joined, whole_decode_kernel)).astype(jnp.bfloat16)
    return up_conv(decoded, final_kernel).astype(jnp.bfloat16)


def picks(index, columns):
    lane = lax.broadcasted_iota(jnp.int32, (index.shape[0], columns), 1)
    return jnp.where(lane == index, 1.0, 0.0).astype(jnp.bfloat16)


def spread_matrix():
    row = lax.broadcasted_iota(jnp.int32, (36 * 16, 1), 0)
    slab = row >> 4
    eh = (slab * 43) >> 8
    h = ((row >> 2) & 3) * 4 + eh - 1
    w = (row & 3) * 4 + (slab - 6 * eh) - 1
    inside = (h >= 0) & (h < 16) & (w >= 0) & (w < 16)
    return picks(jnp.where(inside, h * 16 + w, -1), 256)


def spread_matrix_two():
    row = lax.broadcasted_iota(jnp.int32, (16 * 16, 1), 0)
    h = ((row >> 2) & 3) * 2 + (row >> 6) - 1
    w = (row & 3) * 2 + ((row >> 4) & 3) - 1
    inside = (h >= 0) & (h < 8) & (w >= 0) & (w < 8)
    at = (h & 1) * 32 + (w & 1) * 16 + (h >> 1) * 4 + (w >> 1)
    return picks(jnp.where(inside, at, -1), 64)


def gather_matrix():
    row = lax.broadcasted_iota(jnp.int32, (256, 1), 0)
    h, w = row >> 4, row & 15
    return picks((h & 3) * 64 + (w & 3) * 16 + (h >> 2) * 4 + (w >> 2), 256)


def block_transpose(pieces, width):
    pieces = list(pieces)
    count = len(pieces)
    block = lax.broadcasted_iota(jnp.int32, pieces[0].shape, 1) // width
    step = 1
    while step < count:
        low = (block & step) == 0
        for i in range(count):
            if i & step:
                continue
            a, b = pieces[i], pieces[i + step]
            pieces[i] = jnp.where(low, a, pltpu.roll(b, width * step, 1))
            pieces[i + step] = jnp.where(low, pltpu.roll(a, 128 - width * step, 1), b)
        step *= 2
    return pieces


def moved(values, by, keep):
    lanes = values.shape[1]
    return jnp.where(keep, pltpu.roll(values, by % lanes, 1), 0.0)


class Lanes:
    def __init__(self, count):
        lane = lax.broadcasted_iota(jnp.int32, (1, count), 1)
        wc, hc, d = lane & 3, (lane >> 2) & 3, lane >> 4
        top = count // 16 - 1
        self.after = {1: wc > 0, 4: hc > 0, 16: d > 0}
        self.before = {1: wc < 3, 4: hc < 3, 16: d < top}

    def back(self, values, by):
        return moved(values, by, self.after[by])

    def ahead(self, values, by):
        return moved(values, -by, self.before[by])


def add_taps(lanes, y, outs):
    def row(a, b, c):
        at = (9 * a + 3 * b + c) * outs
        return y[at : at + outs]

    def tall(c):
        return jnp.concatenate([row(a, b, c) for b in range(3) for a in range(3)], axis=0)

    y = tall(1) + lanes.back(tall(0), 1) + lanes.ahead(tall(2), 1)
    y = [y[i * 3 * outs : (i + 1) * 3 * outs] for i in range(3)]
    y = y[1] + lanes.back(y[0], 4) + lanes.ahead(y[2], 4)
    y = [y[i * outs : (i + 1) * outs] for i in range(3)]
    return y[1] + lanes.back(y[0], 16) + lanes.ahead(y[2], 16)


def add_fine_taps(lanes, load, outs):
    def pair(zero, one, by):
        even = zero[1] + one[2] + lanes.back(one[0], by)
        odd = one[1] + zero[0] + lanes.ahead(zero[2], by)
        return even, odd

    planes = {}
    for pd in range(2):
        rows = {}
        for ph in range(2):
            def taps(pw):
                p = 4 * pd + 2 * ph + pw
                return [
                    jnp.concatenate(
                        [load(p, 9 * a + 3 * b + c) for b in range(3) for a in range(3)], axis=0
                    )
                    for c in range(3)
                ]

            rows[ph] = pair(taps(0), taps(1), 1)
        for qw in range(2):
            def cut(ph):
                return [rows[ph][qw][i * 3 * outs : (i + 1) * 3 * outs] for i in range(3)]

            planes[pd, qw] = pair(cut(0), cut(1), 4)
    result = [None] * 8
    for qw in range(2):
        for qh in range(2):
            def cut(pd):
                return [planes[pd, qw][qh][i * outs : (i + 1) * outs] for i in range(3)]

            low, high = pair(cut(0), cut(1), 16)
            result[2 * qh + qw] = low
            result[4 + 2 * qh + qw] = high
    return result


class Gather:
    def __init__(self, n, slots, send_sem, recv_sem):
        self.n, self.slots, self.send_sem, self.recv_sem = n, slots, send_sem, recv_sem
        self.me = lax.axis_index("sp")
        self.sent = []
        self.others = list(range(n - 2, 0, -2))

    def send(self, source, target):
        slot = self.slots.at[self.me ^ source]
        copy = remote(
            slot, slot, self.send_sem.at[len(self.sent)], self.recv_sem.at[source ^ target],
            self.me ^ target,
        )
        copy.start()
        self.sent.append(copy)

    def wait(self, source):
        slot = self.slots.at[self.me ^ source]
        remote(slot, slot, self.send_sem.at[0], self.recv_sem.at[source], self.me ^ 1).wait_recv()

    def start(self):
        for k in self.others:
            self.send(0, k)
        self.send(0, 1)

    def relay(self):
        for k in reversed(self.others):
            self.wait(k)
            self.send(k, 1)

    def finish(self):
        for k in range(1, self.n, 2):
            self.wait(k)

    def pass_on(self, source, *targets):
        self.wait(source)
        for target in targets:
            self.send(source, target)

    def drain(self):
        for copy in self.sent:
            copy.wait_send()


class Doubling(Gather):
    def steps(self):
        bits = [1 << i for i in range(self.n.bit_length() - 1)]
        known = [[0]]
        for _ in bits:
            known.append([k | bit for k in known[-1] for bit in bits if bit < (k & -k or self.n)])
        return bits, known

    def start(self):
        bits, _ = self.steps()
        for bit in reversed(bits):
            self.send(0, bit)

    def hop(self, step):
        bits, known = self.steps()
        for k in known[step]:
            self.pass_on(k, *[bit for bit in reversed(bits) if bit < (k & -k)])


def net_kernel(
    n,
    volume_hbm, first_hbm, second_hbm, deep_hbm, deeper_hbm, rise_hbm, decode_hbm, final_hbm,
    out_ref,
    vol, vhalo, pp, pp2, order, wpair, w2, wd, wdd, rw, kloc, wf,
    ex, pool, ex2, pooled_all, deep_all, deeper_all, skip_all,
    wsend, wall, wt, ys, dsend, decoded_all,
    load_sem, send_v, recv_v, send_p, recv_p,
    send_a, recv_a, send_b, recv_b, send_c, recv_c, send_s, recv_s,
    send_w, recv_w, send_f, recv_f, send_d, recv_d,
):
    me = lax.axis_index("sp")
    bf = jnp.bfloat16
    f32 = jnp.float32
    depth = vol.shape[0]
    k1 = first_hbm.shape[1]
    part = wd.shape[0] // 27
    outs = 256 // n
    coarse = 16 * n

    loads = []

    def load(src, dst):
        copy = pltpu.make_async_copy(src, dst, load_sem.at[len(loads)])
        copy.start()
        loads.append(copy)
        return copy

    get_vol = load(volume_hbm, vol)
    get_k = load(decode_hbm, kloc)
    get_w1 = [
        load(first_hbm.at[1], wpair.at[0:k1, 0:128]),
        load(first_hbm.at[0], wpair.at[0:k1, 128:256]),
        load(first_hbm.at[2], wpair.at[k1 : 2 * k1, 0:128]),
        load(first_hbm.at[1], wpair.at[k1 : 2 * k1, 128:256]),
    ]
    get_w2 = load(second_hbm, w2)
    get_wd = load(deep_hbm, wd)
    get_wdd = load(deeper_hbm, wdd)
    get_rw = load(rise_hbm, rw)
    chans = final_hbm.shape[2]
    get_wf = [load(final_hbm.at[i], wf.at[:, chans * i : chans * (i + 1)]) for i in range(8)]

    barrier = pltpu.get_barrier_semaphore()
    for k in range(n - 1, 0, -1):
        pl.semaphore_signal(
            barrier, inc=1, device_id={"sp": me ^ k}, device_id_type=pl.DeviceIdType.MESH
        )

    twin = lax.axis_index("rep")
    pl.semaphore_signal(
        barrier, inc=1, device_id={"rep": 1 - twin, "sp": me},
        device_id_type=pl.DeviceIdType.MESH,
    )

    def spread(planes, to):
        get = jnp.concatenate(planes, axis=1)
        result = jnp.dot(pp[...], get, preferred_element_type=f32).astype(bf)
        for i, at in enumerate(to):
            ex[at] = result[:, 128 * i : 128 * (i + 1)]

    pp[...] = spread_matrix()
    get_vol.wait()
    for d in range(0, depth, 2):
        spread([vol[d], vol[d + 1]], [d + 1, d + 2])

    pp2[...] = spread_matrix_two()
    order[...] = gather_matrix()

    get_k.wait()
    per = 128 // outs
    for half in range(256 // 128):
        for group in range(wsend.shape[2] // 128):
            taps = []
            for i in range(per):
                tap = per * group + i
                if tap < 27:
                    taps.append(kloc[tap, :, 128 * half : 128 * (half + 1)].astype(f32))
                else:
                    taps.append(jnp.zeros((kloc.shape[1], 128), f32))
            for j, piece in enumerate(block_transpose(taps, outs)):
                wsend[per * half + j, :, 128 * group : 128 * (group + 1)] = piece.astype(bf)

    pl.semaphore_wait(barrier, n)
    finish_v = trade_edges(
        n, vol.at[0], vol.at[depth - 1], vhalo.at[0], vhalo.at[1], send_v, recv_v
    )
    w_copies = []

    def w_piece(k):
        return remote(wsend.at[me ^ k], wall.at[me], send_w.at[k], recv_w.at[k], me ^ k)

    def w_arrived(k):
        slot = wall.at[me ^ k]
        remote(slot, slot, send_w.at[k], recv_w.at[k], me ^ 1).wait_recv()

    def w_start(*steps):
        for k in [2 * i + twin for i in steps] if steps else [1]:
            copy = w_piece(k)
            copy.start()
            w_copies.append(copy)

    def w_forward():
        for i in range(1, n // 2):
            k = 2 * i + twin
            w_arrived(k)
            slot = wall.at[me ^ k]
            copy = pltpu.make_async_remote_copy(
                src_ref=slot, dst_ref=slot, send_sem=send_f.at[i], recv_sem=recv_f.at[i],
                device_id={"rep": 1 - twin, "sp": me}, device_id_type=pl.DeviceIdType.MESH,
            )
            copy.start()
            w_copies.append(copy)

    def w_finish():
        w_arrived(1)
        for i in range(1, n // 2):
            slot = wall.at[me ^ (2 * i + 1 - twin)]
            pltpu.make_async_remote_copy(
                src_ref=slot, dst_ref=slot, send_sem=send_f.at[i], recv_sem=recv_f.at[i],
                device_id={"rep": 1 - twin, "sp": me}, device_id_type=pl.DeviceIdType.MESH,
            ).wait_recv()

    steps = list(range(n // 2 - 1, 0, -1))
    w_start()
    wall[me] = wsend[me]

    def taken(at, b):
        columns = []
        for c in range(3):
            columns.append(
                jnp.concatenate(
                    [ex[at, pl.ds(((b + hm) * 6 + c) * 16, 64), :] for hm in range(4)], axis=0
                )
            )
        return columns

    def rows_of(at):
        return jnp.concatenate(sum([taken(at, b) for b in range(3)], []), axis=1)

    for copy in get_w1:
        copy.wait()

    def both(at):
        left = jnp.concatenate([rows_of(at), rows_of(at + 1)], axis=1)
        return jnp.dot(left, wpair[...], preferred_element_type=f32)

    pairs = [both(1), both(3)]
    own_low = jnp.dot(rows_of(2), wpair[0:k1, 128:256], preferred_element_type=f32)
    own_high = jnp.dot(rows_of(3), wpair[k1 : 2 * k1, 0:128], preferred_element_type=f32)
    w_start(*steps[0::3])
    finish_v()
    spread([vhalo[0], vhalo[1]], [0, depth + 1])
    far_low = jnp.dot(rows_of(0), wpair[0:k1, 128:256], preferred_element_type=f32)
    far_high = jnp.dot(rows_of(5), wpair[k1 : 2 * k1, 0:128], preferred_element_type=f32)
    planes = [
        pairs[0][:, 0:128] + far_low,
        pairs[0][:, 128:256] + own_high,
        pairs[1][:, 0:128] + own_low,
        pairs[1][:, 128:256] + far_high,
    ]
    planes = [jnp.maximum(t, 0.0).astype(bf).astype(f32) for t in planes]
    for i in range(2):
        total = planes[2 * i] + planes[2 * i + 1]
        for ph in range(2):
            for pw in range(2):
                slabs = [
                    total[((2 * ph + y) * 4 + 2 * pw + x) * 16 :][:16]
                    for y in range(2) for x in range(2)
                ]
                slab = (slabs[0] + slabs[1]) + (slabs[2] + slabs[3])
                pool[1 + i, pl.ds((2 * ph + pw) * 16, 16), :] = (slab * 0.125).astype(bf)

    finish_p = trade_edges(n, pool.at[1], pool.at[2], pool.at[0], pool.at[3], send_p, recv_p)
    w_start(*steps[1::3])
    get_w2.wait()

    def spread_two(at):
        ex2[at] = jnp.dot(pp2[...], pool[at], preferred_element_type=f32).astype(bf)

    def rows_two(a):
        columns = []
        for b in range(3):
            for c in range(3):
                columns.append(
                    jnp.concatenate(
                        [
                            ex2[a + i, pl.ds(((b + ph) * 4 + c) * 16, 32), :]
                            for i in range(2) for ph in range(2)
                        ],
                        axis=0,
                    )
                )
        return jnp.concatenate(columns, axis=1)

    spread_two(1)
    spread_two(2)
    skip = jnp.dot(rows_two(1), w2[1], preferred_element_type=f32)
    finish_p()
    spread_two(0)
    spread_two(3)
    skip += jnp.dot(rows_two(0), w2[0], preferred_element_type=f32)
    skip += jnp.dot(rows_two(2), w2[2], preferred_element_type=f32)
    skip = jnp.maximum(skip, 0.0).astype(bf)
    skip_all[me] = skip.reshape(skip_all.shape[1:])
    skip = skip.astype(f32)
    slabs = [skip[16 * i : 16 * (i + 1)] for i in range(8)]
    while len(slabs) > 1:
        slabs = [slabs[i] + slabs[i + 1] for i in range(0, len(slabs), 2)]
    pooled_all[me] = (slabs[0] * 0.125).astype(bf)

    gather_a = Gather(n, pooled_all, send_a, recv_a)
    gather_b = Gather(n, deep_all, send_b, recv_b)
    gather_c = Gather(n, deeper_all, send_c, recv_c)
    gather_s = Doubling(n, skip_all, send_s, recv_s)
    gather_a.start()
    gather_s.start()
    w_start(*steps[2::3])
    lanes = Lanes(coarse)
    get_wd.wait()
    get_wdd.wait()
    get_rw.wait()
    gather_a.relay()
    gather_a.finish()
    y = lax.dot_general(
        wd[...], pooled_all[...].reshape(coarse, pooled_all.shape[2]),
        (((1,), (1,)), ((), ())), preferred_element_type=f32,
    )
    deep_all[me] = jnp.maximum(add_taps(lanes, y, part), 0.0).astype(bf)
    gather_b.start()
    gather_s.hop(1)
    w_forward()
    gather_b.relay()
    gather_s.hop(2)
    gather_b.finish()
    y = jnp.dot(
        wdd[...], deep_all[...].reshape(n * part, coarse), preferred_element_type=f32
    )
    deeper_all[me] = jnp.maximum(add_taps(lanes, y, part), 0.0).astype(bf)
    gather_c.start()
    gather_s.hop(3)
    w_finish()
    for at in range(0, wt.shape[1], 128):
        block = wall[pl.ds(at // part, 128 // part)].reshape(128, wall.shape[2])
        wt[:, at : at + 128] = block.astype(f32).T.astype(bf)[0 : wt.shape[0]]
    gather_s.hop(4)

    def fine(p, values, inner):
        ys[p] = lax.dot_general(
            wt[:, inner], values, (((1,), (1,)), ((), ())), preferred_element_type=f32
        )

    def tap_of(p, tap):
        return ys[p, outs * tap : outs * (tap + 1), :]

    for p in range(8):
        fine(p, skip_all[:, p].reshape(coarse, skip_all.shape[3]), slice(256, 512))
    from_skip = add_fine_taps(lanes, tap_of, outs)
    gather_c.relay()
    gather_c.finish()
    deeper = deeper_all[...].reshape(n * part, coarse).astype(f32).T.astype(bf)
    for p in range(8):
        risen = jnp.dot(deeper, rw[p], preferred_element_type=f32).astype(bf)
        fine(p, risen, slice(0, 256))
    from_risen = add_fine_taps(lanes, tap_of, outs)
    decoded = [jnp.maximum(s + r, 0.0) for s, r in zip(from_skip, from_risen)]
    for half in range(coarse // 128):
        cut = [t[:, 128 * half : 128 * (half + 1)] for t in decoded]
        for j, piece in enumerate(block_transpose(cut, 16)):
            dsend[8 * half + j] = piece.astype(bf)
    d_copies = []
    for k in range(n - 1, 0, -1):
        copy = remote(dsend.at[me ^ k], decoded_all.at[me], send_d.at[k], recv_d.at[k], me ^ k)
        copy.start()
        d_copies.append(copy)
    decoded_all[me] = dsend[me]
    for copy in get_wf:
        copy.wait()
    for k in range(1, n):
        slot = decoded_all.at[me ^ k]
        remote(slot, slot, send_d.at[k], recv_d.at[k], me ^ 1).wait_recv()
    decoded = decoded_all[...].reshape(n * outs, 128).astype(f32).T.astype(bf)
    fine_rows = jnp.dot(decoded, wf[...], preferred_element_type=f32).astype(bf)

    def slab(d, y, x):
        p = 4 * (d // 2) + 2 * (y // 2) + x // 2
        tap = 4 * (d % 2) + 2 * (y % 2) + x % 2
        return fine_rows[16 * p : 16 * (p + 1), chans * tap : chans * (tap + 1)]

    def slabs_of(d):
        return jnp.concatenate([slab(d, y, x) for y in range(4) for x in range(4)], axis=0)

    for d in range(0, depth, 2):
        plane = jnp.concatenate([slabs_of(d), slabs_of(d + 1)], axis=1)
        plane = jnp.dot(order[...], plane, preferred_element_type=f32).astype(bf)
        out_ref[d] = plane[:, 0:chans]
        out_ref[d + 1] = plane[:, chans : 2 * chans]
    for copy in w_copies + d_copies:
        copy.wait_send()
    for gather in (gather_a, gather_b, gather_c, gather_s):
        gather.drain()


def net(
    volume, first_kernel, second_kernel, deep_kernel, deeper_kernel,
    rise_kernel, decode_kernel, final_kernel,
):
    n = lax.axis_size("sp")
    depth, height, width, chans = volume.shape
    mid = second_kernel.shape[4]
    low = rise_kernel.shape[3]
    part = deep_kernel.shape[4]
    block = decode_kernel.shape[3]
    outs = mid // n
    coarse = 16 * n
    area = height * width
    taps = 27 * outs
    wide = -(-taps // LANES) * LANES
    bf = jnp.bfloat16
    vmem = pltpu.VMEM
    dma = pltpu.SemaphoreType.DMA
    hbm = pl.BlockSpec(memory_space=pltpu.HBM)

    def tap_rows(kernel):
        return jnp.transpose(kernel, (0, 1, 2, 4, 3)).reshape(27 * part, kernel.shape[3])

    return pl.pallas_call(
        functools.partial(net_kernel, n),
        out_shape=jax.ShapeDtypeStruct((depth, area, chans), bf),
        in_specs=[hbm] * 8,
        out_specs=pl.BlockSpec(memory_space=pltpu.VMEM),
        scratch_shapes=[
            vmem((depth, area, chans), bf),
            vmem((2, area, chans), bf),
            vmem((36 * 16, area), bf),
            vmem((16 * 16, area // 4), bf),
            vmem((area, area), bf),
            vmem((18 * chans, 2 * chans), bf),
            vmem((3, 9 * chans, mid), bf),
            vmem((27 * part, mid), bf),
            vmem((27 * part, low), bf),
            vmem((8, low, mid), bf),
            vmem((27, block, mid), bf),
            vmem((mid, 8 * chans), bf),
            vmem((depth + 2, 36 * 16, chans), bf),
            vmem((depth // 2 + 2, area // 4, chans), bf),
            vmem((depth // 2 + 2, 16 * 16, chans), bf),
            vmem((n, 16, mid), bf),
            vmem((n, part, coarse), bf),
            vmem((n, part, coarse), bf),
            vmem((n, 8, 16, mid), bf),
            vmem((n, block, wide), bf),
            vmem((n, block, wide), bf),
            vmem((taps, 2 * mid), bf),
            vmem((8, taps, coarse), jnp.float32),
            vmem((n, outs, 128), bf),
            vmem((n, outs, 128), bf),
            dma((24,)),
            dma((2,)), dma((2,)), dma((2,)), dma((2,)),
            dma((2 * n,)), dma((n,)), dma((2 * n,)), dma((n,)),
            dma((2 * n,)), dma((n,)), dma((2 * n,)), dma((n,)),
            dma((n,)), dma((n,)), dma((n,)), dma((n,)), dma((n,)), dma((n,)),
        ],
        compiler_params=pltpu.CompilerParams(
            collective_id=2, has_side_effects=True, vmem_limit_bytes=107 << 19
        ),
        name="net",
    )(
        volume.reshape(depth, area, chans),
        first_kernel.reshape(3, 9 * chans, chans),
        second_kernel.reshape(3, 9 * chans, mid),
        tap_rows(deep_kernel),
        tap_rows(deeper_kernel),
        rise_kernel.reshape(8, low, mid),
        decode_kernel.reshape(27, block, mid),
        final_kernel.reshape(8, mid, chans),
    ).reshape(volume.shape)


def split_body(
    volume, first_kernel, second_kernel, deep_kernel, deeper_kernel,
    rise_kernel, decode_kernel, final_kernel,
):
    n = lax.axis_size("sp")
    if n & (n - 1) or lax.axis_size("rep") != 2 or decode_kernel.shape[4] % (16 * n) or decode_kernel.shape[3] % 16:
        return body(
            volume, first_kernel, second_kernel, deep_kernel, deeper_kernel,
            rise_kernel, decode_kernel, final_kernel,
        )
    return net(
        volume, first_kernel, second_kernel, deep_kernel, deeper_kernel,
        rise_kernel, decode_kernel, final_kernel,
    )


def solution(mesh):
    return jax.shard_map(
        split_body,
        mesh=mesh,
        in_specs=(
            P(("rep", "sp"), None, None, None),
            P(),
            P(),
            P(None, None, None, None, "sp"),
            P(None, None, None, None, "sp"),
            P(),
            P(None, None, None, "sp", None),
            P(),
        ),
        out_specs=P(("rep", "sp"), None, None, None),
        check_vma=False,
    )
```

```python
import functools

import jax
import jax.numpy as jnp
from jax import lax
from jax.experimental import pallas as pl
from jax.experimental.pallas import tpu as pltpu
from jax.sharding import PartitionSpec as P

LANES = 128


def remote(src, dst, send_sem, recv_sem, target):
    return pltpu.make_async_remote_copy(
        src_ref=src, dst_ref=dst, send_sem=send_sem, recv_sem=recv_sem,
        device_id={"sp": target}, device_id_type=pl.DeviceIdType.MESH,
    )


def trade_edges(n, first, last, low, high, send_sem, recv_sem):
    me = lax.axis_index("sp")
    upward = remote(last, low, send_sem.at[0], recv_sem.at[0], lax.rem(me + 1, n))
    downward = remote(first, high, send_sem.at[1], recv_sem.at[1], lax.rem(me + n - 1, n))

    @pl.when(me < n - 1)
    def _():
        upward.start()

    @pl.when(me > 0)
    def _():
        downward.start()

    @pl.when(me == 0)
    def _():
        low[...] = jnp.zeros(low.shape, low.dtype)

    @pl.when(me == n - 1)
    def _():
        high[...] = jnp.zeros(high.shape, high.dtype)

    def finish():
        @pl.when(me > 0)
        def _():
            upward.wait_recv()
            downward.wait_send()

        @pl.when(me < n - 1)
        def _():
            downward.wait_recv()
            upward.wait_send()

    return finish


def greet_neighbours(n):
    me = lax.axis_index("sp")
    barrier = pltpu.get_barrier_semaphore()

    @pl.when(me > 0)
    def _():
        pl.semaphore_signal(
            barrier, inc=1, device_id={"sp": lax.rem(me + n - 1, n)},
            device_id_type=pl.DeviceIdType.MESH,
        )

    @pl.when(me < n - 1)
    def _():
        pl.semaphore_signal(
            barrier, inc=1, device_id={"sp": lax.rem(me + 1, n)},
            device_id_type=pl.DeviceIdType.MESH,
        )

    @pl.when((me > 0) & (me < n - 1))
    def _():
        pl.semaphore_wait(barrier, 2)

    @pl.when((me == 0) | (me == n - 1))
    def _():
        pl.semaphore_wait(barrier, 1)


def first_level_kernel(
    n, depth, height, width,
    volume_ref, weight_ref, out_ref,
    ends, taps, sums, send_a, recv_a, send_b, recv_b,
):
    area = height * width
    chans = volume_ref.shape[2]
    greet_neighbours(n)
    finish = trade_edges(
        n, volume_ref.at[0], volume_ref.at[depth - 1], ends.at[0], ends.at[1], send_a, recv_a
    )
    index = lax.broadcasted_iota(jnp.int32, (area, 1), 0) & (width - 1)
    blank = jnp.zeros((depth + 2, width, 3 * chans), jnp.bfloat16)
    taps[:, 0:width] = blank
    taps[:, area + width : area + 2 * width] = blank

    def spread(at, values):
        taps[at, width : area + width, chans : 2 * chans] = values
        values = values.astype(jnp.float32)
        left = jnp.where(index > 0, pltpu.roll(values, 1, 0), 0.0)
        right = jnp.where(index < width - 1, pltpu.roll(values, area - 1, 0), 0.0)
        taps[at, width : area + width, 0:chans] = left.astype(jnp.bfloat16)
        taps[at, width : area + width, 2 * chans : 3 * chans] = right.astype(jnp.bfloat16)

    for d in range(depth):
        spread(d + 1, volume_ref[d])
    finish()
    spread(0, ends[0])
    spread(depth + 1, ends[1])
    for pair in range(depth // 2):
        total = jnp.zeros((2 * area, weight_ref.shape[3]), jnp.float32)
        for a in range(3):
            for b in range(3):
                block = taps[2 * pair + a : 2 * pair + a + 2, b * width : b * width + area]
                total += jnp.dot(
                    block.reshape(2 * area, 3 * chans), weight_ref[a, b],
                    preferred_element_type=jnp.float32,
                )
        total = jnp.maximum(total, 0.0).astype(jnp.bfloat16).astype(jnp.float32)
        total = total[0:area] + total[area : 2 * area]
        total = total.reshape(height // 2, 2, width, total.shape[1]).sum(axis=1)
        sums[...] = total.reshape(area // 2, total.shape[2])
        total = sums[pl.ds(0, area // 4, 2), :] + sums[pl.ds(1, area // 4, 2), :]
        out_ref[1 + pair] = (total * 0.125).astype(jnp.bfloat16)
    halves = depth // 2
    trade_edges(
        n, out_ref.at[1], out_ref.at[halves], out_ref.at[0], out_ref.at[halves + 1],
        send_b, recv_b,
    )()


def first_level(volume, kernel):
    n = lax.axis_size("sp")
    depth, height, width, chans = volume.shape
    outs = kernel.shape[4]
    area = height * width
    vmem = pl.BlockSpec(memory_space=pltpu.VMEM)
    padded = pl.pallas_call(
        functools.partial(first_level_kernel, n, depth, height, width),
        out_shape=jax.ShapeDtypeStruct((depth // 2 + 2, area // 4, outs), jnp.bfloat16),
        in_specs=[vmem] * 2,
        out_specs=vmem,
        scratch_shapes=[
            pltpu.VMEM((2, area, chans), jnp.bfloat16),
            pltpu.VMEM((depth + 2, area + 2 * width, 3 * chans), jnp.bfloat16),
            pltpu.VMEM((area // 2, outs), jnp.float32),
        ]
        + [pltpu.SemaphoreType.DMA((2,))] * 4,
        compiler_params=pltpu.CompilerParams(
            collective_id=1, has_side_effects=True, vmem_limit_bytes=16 << 20
        ),
        name="first_level",
    )(volume.reshape(depth, area, chans), kernel.reshape(3, 3, 3 * chans, outs))
    return padded.reshape(depth // 2 + 2, height // 2, width // 2, outs)


def conv_depth(padded, kernel):
    result = lax.conv_general_dilated(
        padded[None],
        kernel,
        (1, 1, 1),
        ((0, 0), (1, 1), (1, 1)),
        dimension_numbers=("NDHWC", "DHWIO", "NDHWC"),
        preferred_element_type=jnp.float32,
    )
    return result[0]


def pool_mean(values):
    depth, height, width, chans = values.shape
    blocks = values.astype(jnp.float32).reshape(depth // 2, 2, height // 2, 2, width // 2, 2, chans)
    return jnp.mean(blocks, axis=(1, 3, 5)).astype(jnp.bfloat16)


def up_conv(values, kernel):
    depth, height, width, chans = values.shape
    result = jnp.einsum("dhwi,abcio->dahbwco", values, kernel, preferred_element_type=jnp.float32)
    return result.reshape(2 * depth, 2 * height, 2 * width, kernel.shape[4])


def conv_rows(values, weight_ref, height, width):
    rows = values.shape[0]
    index = lax.broadcasted_iota(jnp.int32, (rows, 1), 0)
    w_at = index & (width - 1)
    h_at = (index >> (width.bit_length() - 1)) & (height - 1)
    part, chans = weight_ref.shape[2:]
    blank = jnp.zeros((LANES - 3 * part, chans), weight_ref.dtype)
    total = jnp.zeros((rows, LANES), jnp.float32)
    for b in range(3):
        for c in range(3):
            shift = width * (b - 1) + (c - 1)
            moved = values if shift == 0 else pltpu.roll(values, (-shift) % rows, 0)
            h_to, w_to = h_at + (b - 1), w_at + (c - 1)
            keep = (h_to >= 0) & (h_to < height) & (w_to >= 0) & (w_to < width)
            moved = jnp.where(keep, moved, 0.0).astype(jnp.bfloat16)
            tap = 3 * b + c
            weight = jnp.concatenate([weight_ref[a, tap] for a in range(3)] + [blank], axis=0)
            total += lax.dot_general(
                moved, weight, (((1,), (1,)), ((), ())), preferred_element_type=jnp.float32
            )
    return total


def bottleneck_kernel(
    n, height, width, part,
    pooled_ref, skip_ref, deep_w_ref, deeper_w_ref, out_ref, near_ref,
    whole, deep_mine, deep_all, packed,
    send_a, recv_a, send_b, recv_b, send_c, recv_c, send_d, recv_d,
):
    me = lax.axis_index("sp")
    area = height * width
    voxels = n * area
    partner = me + 1 - 2 * (me % 2)
    half = n // 2

    barrier = pltpu.get_barrier_semaphore()

    def greet(k, carry):
        pl.semaphore_signal(
            barrier, inc=1, device_id={"sp": lax.rem(me + k, n)},
            device_id_type=pl.DeviceIdType.MESH,
        )
        return carry

    lax.fori_loop(1, n, greet, 0)
    pl.semaphore_wait(barrier, n - 1)

    def gather(mine, everyone, send_sem, recv_sem):
        def slot(source):
            return everyone.at[source]

        def direct(k):
            target = lax.rem(me + 2 * k, n)
            return remote(mine, slot(me), send_sem.at[k], recv_sem.at[me], target)

        def relay(k):
            source = lax.rem(me + 2 * (half - k), n)
            return remote(
                slot(source), slot(source), send_sem.at[half + k], recv_sem.at[source], partner
            )

        def arrival(source):
            return remote(mine, slot(source), send_sem.at[0], recv_sem.at[source], partner)

        def start_direct(k, carry):
            direct(k).start()
            return carry

        to_partner = remote(mine, slot(me), send_sem.at[0], recv_sem.at[me], partner)
        lax.fori_loop(1, half, start_direct, 0)
        to_partner.start()
        everyone[me] = mine[...]

        def pass_on(k, carry):
            arrival(lax.rem(me + 2 * (half - k), n)).wait_recv()
            relay(k).start()
            return carry

        lax.fori_loop(1, half, pass_on, 0)

        def from_partner(k, carry):
            arrival(lax.rem(partner + 2 * (half - k), n)).wait_recv()
            return carry

        lax.fori_loop(0, half, from_partner, 0)

        def finish():
            to_partner.wait_send()

            def sent(k, carry):
                direct(k).wait_send()
                relay(k).wait_send()
                return carry

            lax.fori_loop(1, half, sent, 0)

        return finish

    finish_a = gather(pooled_ref, whole, send_a, recv_a)
    depth = skip_ref.shape[0]
    finish_d = trade_edges(
        n, skip_ref.at[0], skip_ref.at[depth - 1], near_ref.at[0], near_ref.at[1], send_d, recv_d
    )
    lanes = lax.broadcasted_iota(jnp.int32, (1, voxels), 1)
    values = whole[...].astype(jnp.float32).reshape(voxels, pooled_ref.shape[1])
    deep = conv_rows(values, deep_w_ref, height, width).T
    below = jnp.where(lanes >= area, pltpu.roll(deep[0:part], area, 1), 0.0)
    above = jnp.where(
        lanes < voxels - area, pltpu.roll(deep[2 * part : 3 * part], voxels - area, 1), 0.0
    )
    deep = below + deep[part : 2 * part] + above
    deep_mine[...] = jnp.maximum(deep, 0.0).astype(jnp.bfloat16)
    finish_b = gather(deep_mine, deep_all, send_b, recv_b)

    values = deep_all[...].astype(jnp.float32).reshape(n * part, voxels).T
    deeper = conv_rows(values, deeper_w_ref, height, width)
    rows = lax.broadcasted_iota(jnp.int32, (voxels, 1), 0)

    def down(block):
        return jnp.where(rows >= area, pltpu.roll(block, area, 0), 0.0)

    def up(block):
        return jnp.where(rows < voxels - area, pltpu.roll(block, voxels - area, 0), 0.0)

    deeper = (
        down(deeper)
        + pltpu.roll(deeper, LANES - part, 1)
        + up(pltpu.roll(deeper, LANES - 2 * part, 1))
    )
    deeper = jnp.maximum(deeper, 0.0)
    lane = lax.broadcasted_iota(jnp.int32, (1, LANES), 1)
    deeper = jnp.where(
        lane < part,
        down(deeper),
        jnp.where(
            lane < 2 * part,
            pltpu.roll(deeper, part, 1),
            up(pltpu.roll(deeper, 2 * part, 1)),
        ),
    )
    packed[...] = deeper.astype(jnp.bfloat16).reshape(n, area, LANES)

    def deal(k):
        target = lax.rem(me + k, n)
        return remote(packed.at[target], out_ref.at[me], send_c.at[k], recv_c.at[me], target)

    def start_deal(k, carry):
        deal(k).start()
        return carry

    lax.fori_loop(1, n, start_deal, 0)
    out_ref[me] = packed[me]

    def receive(k, carry):
        source = lax.rem(me + k, n)
        remote(
            packed.at[source], out_ref.at[source], send_c.at[k], recv_c.at[source], source
        ).wait_recv()
        return carry

    lax.fori_loop(1, n, receive, 0)

    def sent(k, carry):
        deal(k).wait_send()
        return carry

    lax.fori_loop(1, n, sent, 0)
    finish_a()
    finish_b()
    finish_d()


def out_major(kernel):
    chans, part = kernel.shape[3], kernel.shape[4]
    return jnp.transpose(kernel, (0, 1, 2, 4, 3)).reshape(3, 9, part, chans)


def bottleneck(pooled, skip, deep_kernel, deeper_kernel):
    n = lax.axis_size("sp")
    _, height, width, chans = pooled.shape
    part = deep_kernel.shape[4]
    area = height * width
    voxels = n * area
    vmem = pl.BlockSpec(memory_space=pltpu.VMEM)
    received, near = pl.pallas_call(
        functools.partial(bottleneck_kernel, n, height, width, part),
        out_shape=(
            jax.ShapeDtypeStruct((n, area, LANES), jnp.bfloat16),
            jax.ShapeDtypeStruct((2,) + skip.shape[1:], jnp.bfloat16),
        ),
        in_specs=[vmem] * 4,
        out_specs=(vmem, vmem),
        scratch_shapes=[
            pltpu.VMEM((n, area, chans), jnp.bfloat16),
            pltpu.VMEM((part, voxels), jnp.bfloat16),
            pltpu.VMEM((n, part, voxels), jnp.bfloat16),
            pltpu.VMEM((n, area, LANES), jnp.bfloat16),
        ]
        + [pltpu.SemaphoreType.DMA((n,))] * 6
        + [pltpu.SemaphoreType.DMA((2,))] * 2,
        compiler_params=pltpu.CompilerParams(
            collective_id=0, has_side_effects=True, vmem_limit_bytes=24 << 20
        ),
        name="bottleneck",
    )(pooled.reshape(area, chans), skip, out_major(deep_kernel), out_major(deeper_kernel))
    blocks = received[:, :, : 3 * part].reshape(n, area, 3, part)
    return jnp.transpose(blocks, (2, 1, 0, 3)).reshape(3, height, width, n * part), near


def body(
    volume,
    first_kernel,
    second_kernel,
    deep_kernel,
    deeper_kernel,
    rise_kernel,
    decode_kernel,
    final_kernel,
):
    padded_pool = first_level(volume, first_kernel)
    skip = jax.nn.relu(conv_depth(padded_pool, second_kernel)).astype(jnp.bfloat16)
    pooled_two = pool_mean(skip)
    deeper_near, skip_near = bottleneck(pooled_two, skip, deep_kernel, deeper_kernel)
    padded_skip = jnp.concatenate([skip_near[:1], skip, skip_near[1:]], axis=0)
    risen = up_conv(deeper_near, rise_kernel)[1:-1].astype(jnp.bfloat16)
    padded_joined = jnp.concatenate([risen, padded_skip], axis=3)
    whole_decode_kernel = lax.all_gather(decode_kernel, "sp", axis=3, tiled=True)
    decoded = jax.nn.relu(conv_depth(padded_joined, whole_decode_kernel)).astype(jnp.bfloat16)
    return up_conv(decoded, final_kernel).astype(jnp.bfloat16)


def picks(index, columns):
    lane = lax.broadcasted_iota(jnp.int32, (index.shape[0], columns), 1)
    return jnp.where(lane == index, 1.0, 0.0).astype(jnp.bfloat16)


def spread_matrix():
    row = lax.broadcasted_iota(jnp.int32, (36 * 16, 1), 0)
    slab = row >> 4
    eh = (slab * 43) >> 8
    h = ((row >> 2) & 3) * 4 + eh - 1
    w = (row & 3) * 4 + (slab - 6 * eh) - 1
    inside = (h >= 0) & (h < 16) & (w >= 0) & (w < 16)
    return picks(jnp.where(inside, h * 16 + w, -1), 256)


def spread_matrix_two():
    row = lax.broadcasted_iota(jnp.int32, (16 * 16, 1), 0)
    h = ((row >> 2) & 3) * 2 + (row >> 6) - 1
    w = (row & 3) * 2 + ((row >> 4) & 3) - 1
    inside = (h >= 0) & (h < 8) & (w >= 0) & (w < 8)
    at = (h & 1) * 32 + (w & 1) * 16 + (h >> 1) * 4 + (w >> 1)
    return picks(jnp.where(inside, at, -1), 64)


def gather_matrix():
    row = lax.broadcasted_iota(jnp.int32, (256, 1), 0)
    h, w = row >> 4, row & 15
    return picks((h & 3) * 64 + (w & 3) * 16 + (h >> 2) * 4 + (w >> 2), 256)


def block_transpose(pieces, width):
    pieces = list(pieces)
    count = len(pieces)
    block = lax.broadcasted_iota(jnp.int32, pieces[0].shape, 1) // width
    step = 1
    while step < count:
        low = (block & step) == 0
        for i in range(count):
            if i & step:
                continue
            a, b = pieces[i], pieces[i + step]
            pieces[i] = jnp.where(low, a, pltpu.roll(b, width * step, 1))
            pieces[i + step] = jnp.where(low, pltpu.roll(a, 128 - width * step, 1), b)
        step *= 2
    return pieces


def moved(values, by, keep):
    lanes = values.shape[1]
    return jnp.where(keep, pltpu.roll(values, by % lanes, 1), 0.0)


class Lanes:
    def __init__(self, count):
        lane = lax.broadcasted_iota(jnp.int32, (1, count), 1)
        wc, hc, d = lane & 3, (lane >> 2) & 3, lane >> 4
        top = count // 16 - 1
        self.after = {1: wc > 0, 4: hc > 0, 16: d > 0}
        self.before = {1: wc < 3, 4: hc < 3, 16: d < top}

    def back(self, values, by):
        return moved(values, by, self.after[by])

    def ahead(self, values, by):
        return moved(values, -by, self.before[by])


def add_taps(lanes, y, outs):
    def row(a, b, c):
        at = (9 * a + 3 * b + c) * outs
        return y[at : at + outs]

    def tall(c):
        return jnp.concatenate([row(a, b, c) for b in range(3) for a in range(3)], axis=0)

    y = tall(1) + lanes.back(tall(0), 1) + lanes.ahead(tall(2), 1)
    y = [y[i * 3 * outs : (i + 1) * 3 * outs] for i in range(3)]
    y = y[1] + lanes.back(y[0], 4) + lanes.ahead(y[2], 4)
    y = [y[i * outs : (i + 1) * outs] for i in range(3)]
    return y[1] + lanes.back(y[0], 16) + lanes.ahead(y[2], 16)


def add_fine_taps(lanes, load, outs):
    def pair(zero, one, by):
        even = zero[1] + one[2] + lanes.back(one[0], by)
        odd = one[1] + zero[0] + lanes.ahead(zero[2], by)
        return even, odd

    planes = {}
    for pd in range(2):
        rows = {}
        for ph in range(2):
            def taps(pw):
                p = 4 * pd + 2 * ph + pw
                return [
                    jnp.concatenate(
                        [load(p, 9 * a + 3 * b + c) for b in range(3) for a in range(3)], axis=0
                    )
                    for c in range(3)
                ]

            rows[ph] = pair(taps(0), taps(1), 1)
        for qw in range(2):
            def cut(ph):
                return [rows[ph][qw][i * 3 * outs : (i + 1) * 3 * outs] for i in range(3)]

            planes[pd, qw] = pair(cut(0), cut(1), 4)
    result = [None] * 8
    for qw in range(2):
        for qh in range(2):
            def cut(pd):
                return [planes[pd, qw][qh][i * outs : (i + 1) * outs] for i in range(3)]

            low, high = pair(cut(0), cut(1), 16)
            result[2 * qh + qw] = low
            result[4 + 2 * qh + qw] = high
    return result


class Gather:
    def __init__(self, n, slots, send_sem, recv_sem):
        self.n, self.slots, self.send_sem, self.recv_sem = n, slots, send_sem, recv_sem
        self.me = lax.axis_index("sp")
        self.sent = []
        self.others = list(range(n - 2, 0, -2))

    def send(self, source, target):
        slot = self.slots.at[self.me ^ source]
        copy = remote(
            slot, slot, self.send_sem.at[len(self.sent)], self.recv_sem.at[source ^ target],
            self.me ^ target,
        )
        copy.start()
        self.sent.append(copy)

    def wait(self, source):
        slot = self.slots.at[self.me ^ source]
        remote(slot, slot, self.send_sem.at[0], self.recv_sem.at[source], self.me ^ 1).wait_recv()

    def start(self):
        for k in self.others:
            self.send(0, k)
        self.send(0, 1)

    def relay(self):
        for k in reversed(self.others):
            self.wait(k)
            self.send(k, 1)

    def finish(self):
        for k in range(1, self.n, 2):
            self.wait(k)

    def pass_on(self, source, *targets):
        self.wait(source)
        for target in targets:
            self.send(source, target)

    def drain(self):
        for copy in self.sent:
            copy.wait_send()


class Doubling(Gather):
    def steps(self):
        bits = [1 << i for i in range(self.n.bit_length() - 1)]
        known = [[0]]
        for _ in bits:
            known.append([k | bit for k in known[-1] for bit in bits if bit < (k & -k or self.n)])
        return bits, known

    def start(self):
        bits, _ = self.steps()
        for bit in reversed(bits):
            self.send(0, bit)

    def hop(self, step):
        bits, known = self.steps()
        for k in known[step]:
            self.pass_on(k, *[bit for bit in reversed(bits) if bit < (k & -k)])


def net_kernel(
    n,
    volume_hbm, first_hbm, second_hbm, deep_hbm, deeper_hbm, rise_hbm, decode_hbm, final_hbm,
    out_ref,
    vol, vhalo, pp, pp2, order, wpair, w2, wd, wdd, rw, kloc, wf,
    ex, pool, ex2, pooled_all, deep_all, deeper_all, skip_all,
    wsend, wall, wt, ys, dsend, decoded_all,
    load_sem, send_v, recv_v, send_p, recv_p,
    send_a, recv_a, send_b, recv_b, send_c, recv_c, send_s, recv_s,
    send_w, recv_w, send_f, recv_f, send_d, recv_d, ready,
):
    me = lax.axis_index("sp")
    bf = jnp.bfloat16
    f32 = jnp.float32
    depth = vol.shape[0]
    k1 = first_hbm.shape[1]
    part = wd.shape[0] // 27
    outs = 256 // n
    coarse = 16 * n

    loads = []

    def load(src, dst):
        copy = pltpu.make_async_copy(src, dst, load_sem.at[len(loads)])
        copy.start()
        loads.append(copy)
        return copy

    get_vol = load(volume_hbm, vol)
    get_k = load(decode_hbm, kloc)
    get_w1 = [
        load(first_hbm.at[1], wpair.at[0:k1, 0:128]),
        load(first_hbm.at[0], wpair.at[0:k1, 128:256]),
        load(first_hbm.at[2], wpair.at[k1 : 2 * k1, 0:128]),
        load(first_hbm.at[1], wpair.at[k1 : 2 * k1, 128:256]),
    ]
    get_w2 = load(second_hbm, w2)
    get_wd = load(deep_hbm, wd)
    get_wdd = load(deeper_hbm, wdd)
    get_rw = load(rise_hbm, rw)
    chans = final_hbm.shape[2]
    get_wf = [load(final_hbm.at[i], wf.at[:, chans * i : chans * (i + 1)]) for i in range(8)]

    twin = lax.axis_index("rep")
    barrier = pltpu.get_barrier_semaphore()
    plane, columns = (1, 2, 3), (4, 8)

    def say(sem, target):
        pl.semaphore_signal(
            sem, inc=1, device_id={"sp": target}, device_id_type=pl.DeviceIdType.MESH
        )

    corner = ((me % 4 == 0) & (me > 0)) | ((me % 4 == 3) & (me < n - 1))
    beyond = jnp.where(me % 4 == 0, me + n - 1, me + 1) % n
    pl.when(corner)(lambda: say(barrier, beyond))
    for k in columns[::-1] + plane:
        say(barrier, me ^ k)
    pl.semaphore_signal(
        barrier, inc=1, device_id={"rep": 1 - twin, "sp": me},
        device_id_type=pl.DeviceIdType.MESH,
    )

    def meet_near():
        near = len(plane) + len(columns) + 1

        @pl.when(corner)
        def _():
            pl.semaphore_wait(barrier, near + 1)

        @pl.when(jnp.logical_not(corner))
        def _():
            pl.semaphore_wait(barrier, near)

        for k in plane:
            say(ready.at[0], me ^ k)

    def meet_planes():
        pl.semaphore_wait(ready.at[0], len(plane))
        for k in columns:
            say(ready.at[1], me ^ k)

    def meet_all():
        pl.semaphore_wait(ready.at[1], len(columns))

    def spread(planes, to):
        get = jnp.concatenate(planes, axis=1)
        result = jnp.dot(pp[...], get, preferred_element_type=f32).astype(bf)
        for i, at in enumerate(to):
            ex[at] = result[:, 128 * i : 128 * (i + 1)]

    pp[...] = spread_matrix()
    get_vol.wait()
    for d in range(0, depth, 2):
        spread([vol[d], vol[d + 1]], [d + 1, d + 2])

    meet_near()
    finish_v = trade_edges(
        n, vol.at[0], vol.at[depth - 1], vhalo.at[0], vhalo.at[1], send_v, recv_v
    )
    pp2[...] = spread_matrix_two()
    order[...] = gather_matrix()

    get_k.wait()
    per = 128 // outs
    for half in range(256 // 128):
        for group in range(wsend.shape[2] // 128):
            taps = []
            for i in range(per):
                tap = per * group + i
                if tap < 27:
                    taps.append(kloc[tap, :, 128 * half : 128 * (half + 1)].astype(f32))
                else:
                    taps.append(jnp.zeros((kloc.shape[1], 128), f32))
            for j, piece in enumerate(block_transpose(taps, outs)):
                wsend[per * half + j, :, 128 * group : 128 * (group + 1)] = piece.astype(bf)

    w_copies = []

    def w_piece(k):
        return remote(wsend.at[me ^ k], wall.at[me], send_w.at[k], recv_w.at[k], me ^ k)

    def w_arrived(k):
        slot = wall.at[me ^ k]
        remote(slot, slot, send_w.at[k], recv_w.at[k], me ^ 1).wait_recv()

    def w_start(batch):
        for k in [2 * i + twin for i in batch] if batch else [1]:
            copy = w_piece(k)
            copy.start()
            w_copies.append(copy)

    def w_forward():
        for i in range(1, n // 2):
            k = 2 * i + twin
            w_arrived(k)
            slot = wall.at[me ^ k]
            copy = pltpu.make_async_remote_copy(
                src_ref=slot, dst_ref=slot, send_sem=send_f.at[i], recv_sem=recv_f.at[i],
                device_id={"rep": 1 - twin, "sp": me}, device_id_type=pl.DeviceIdType.MESH,
            )
            copy.start()
            w_copies.append(copy)

    def w_finish():
        w_arrived(1)
        for i in range(1, n // 2):
            slot = wall.at[me ^ (2 * i + 1 - twin)]
            pltpu.make_async_remote_copy(
                src_ref=slot, dst_ref=slot, send_sem=send_f.at[i], recv_sem=recv_f.at[i],
                device_id={"rep": 1 - twin, "sp": me}, device_id_type=pl.DeviceIdType.MESH,
            ).wait_recv()

    batches = [[5, 3], [4, 2], [7, 6, 1]]
    w_start([])
    wall[me] = wsend[me]

    def taken(at, b):
        columns = []
        for c in range(3):
            columns.append(
                jnp.concatenate(
                    [ex[at, pl.ds(((b + hm) * 6 + c) * 16, 64), :] for hm in range(4)], axis=0
                )
            )
        return columns

    def rows_of(at):
        return jnp.concatenate(sum([taken(at, b) for b in range(3)], []), axis=1)

    for copy in get_w1:
        copy.wait()

    def both(at):
        left = jnp.concatenate([rows_of(at), rows_of(at + 1)], axis=1)
        return jnp.dot(left, wpair[...], preferred_element_type=f32)

    pairs = [both(1), both(3)]
    own_low = jnp.dot(rows_of(2), wpair[0:k1, 128:256], preferred_element_type=f32)
    own_high = jnp.dot(rows_of(3), wpair[k1 : 2 * k1, 0:128], preferred_element_type=f32)
    def turn_w():
        for at in range(0, wt.shape[1], 128):
            block = wall[pl.ds(at // part, 128 // part)].reshape(128, wall.shape[2])
            wt[:, at : at + 128] = block.astype(f32).T.astype(bf)[0 : wt.shape[0]]

    meet_planes()
    w_start(batches[0])
    finish_v()
    spread([vhalo[0], vhalo[1]], [0, depth + 1])
    far_low = jnp.dot(rows_of(0), wpair[0:k1, 128:256], preferred_element_type=f32)
    far_high = jnp.dot(rows_of(5), wpair[k1 : 2 * k1, 0:128], preferred_element_type=f32)
    planes = [
        pairs[0][:, 0:128] + far_low,
        pairs[0][:, 128:256] + own_high,
        pairs[1][:, 0:128] + own_low,
        pairs[1][:, 128:256] + far_high,
    ]
    planes = [jnp.maximum(t, 0.0).astype(bf).astype(f32) for t in planes]
    for i in range(2):
        total = planes[2 * i] + planes[2 * i + 1]
        for ph in range(2):
            for pw in range(2):
                slabs = [
                    total[((2 * ph + y) * 4 + 2 * pw + x) * 16 :][:16]
                    for y in range(2) for x in range(2)
                ]
                slab = (slabs[0] + slabs[1]) + (slabs[2] + slabs[3])
                pool[1 + i, pl.ds((2 * ph + pw) * 16, 16), :] = (slab * 0.125).astype(bf)

    finish_p = trade_edges(n, pool.at[1], pool.at[2], pool.at[0], pool.at[3], send_p, recv_p)
    w_start(batches[1])
    get_w2.wait()

    def spread_two(at):
        ex2[at] = jnp.dot(pp2[...], pool[at], preferred_element_type=f32).astype(bf)

    def rows_two(a):
        columns = []
        for b in range(3):
            for c in range(3):
                columns.append(
                    jnp.concatenate(
                        [
                            ex2[a + i, pl.ds(((b + ph) * 4 + c) * 16, 32), :]
                            for i in range(2) for ph in range(2)
                        ],
                        axis=0,
                    )
                )
        return jnp.concatenate(columns, axis=1)

    spread_two(1)
    spread_two(2)
    skip = jnp.dot(rows_two(1), w2[1], preferred_element_type=f32)
    finish_p()
    spread_two(0)
    spread_two(3)
    skip += jnp.dot(rows_two(0), w2[0], preferred_element_type=f32)
    skip += jnp.dot(rows_two(2), w2[2], preferred_element_type=f32)
    skip = jnp.maximum(skip, 0.0).astype(bf)
    skip_all[me] = skip.reshape(skip_all.shape[1:])
    skip = skip.astype(f32)
    slabs = [skip[16 * i : 16 * (i + 1)] for i in range(8)]
    while len(slabs) > 1:
        slabs = [slabs[i] + slabs[i + 1] for i in range(0, len(slabs), 2)]
    pooled_all[me] = (slabs[0] * 0.125).astype(bf)

    gather_a = Gather(n, pooled_all, send_a, recv_a)
    gather_b = Gather(n, deep_all, send_b, recv_b)
    gather_c = Gather(n, deeper_all, send_c, recv_c)
    gather_s = Doubling(n, skip_all, send_s, recv_s)
    meet_all()
    gather_a.start()
    gather_s.start()
    w_start(batches[2])
    lanes = Lanes(coarse)
    get_wd.wait()
    get_wdd.wait()
    get_rw.wait()
    gather_a.relay()
    gather_a.finish()
    y = lax.dot_general(
        wd[...], pooled_all[...].reshape(coarse, pooled_all.shape[2]),
        (((1,), (1,)), ((), ())), preferred_element_type=f32,
    )
    deep_all[me] = jnp.maximum(add_taps(lanes, y, part), 0.0).astype(bf)
    gather_b.start()
    gather_s.hop(1)
    w_forward()
    gather_b.relay()
    gather_s.hop(2)
    gather_b.finish()
    y = jnp.dot(
        wdd[...], deep_all[...].reshape(n * part, coarse), preferred_element_type=f32
    )
    deeper_all[me] = jnp.maximum(add_taps(lanes, y, part), 0.0).astype(bf)
    gather_c.start()
    gather_s.hop(3)
    w_finish()
    turn_w()
    gather_s.hop(4)

    def fine(p, values, inner):
        ys[p] = lax.dot_general(
            wt[:, inner], values, (((1,), (1,)), ((), ())), preferred_element_type=f32
        )

    def tap_of(p, tap):
        return ys[p, outs * tap : outs * (tap + 1), :]

    for p in range(8):
        fine(p, skip_all[:, p].reshape(coarse, skip_all.shape[3]), slice(256, 512))
    from_skip = add_fine_taps(lanes, tap_of, outs)
    gather_c.relay()
    gather_c.finish()
    deeper = deeper_all[...].reshape(n * part, coarse).astype(f32).T.astype(bf)
    for p in range(8):
        risen = jnp.dot(deeper, rw[p], preferred_element_type=f32).astype(bf)
        fine(p, risen, slice(0, 256))
    from_risen = add_fine_taps(lanes, tap_of, outs)
    decoded = [jnp.maximum(s + r, 0.0) for s, r in zip(from_skip, from_risen)]
    for half in range(coarse // 128):
        cut = [t[:, 128 * half : 128 * (half + 1)] for t in decoded]
        for j, piece in enumerate(block_transpose(cut, 16)):
            dsend[8 * half + j] = piece.astype(bf)
    d_copies = []
    for k in range(n - 1, 0, -1):
        copy = remote(dsend.at[me ^ k], decoded_all.at[me], send_d.at[k], recv_d.at[k], me ^ k)
        copy.start()
        d_copies.append(copy)
    decoded_all[me] = dsend[me]
    for copy in get_wf:
        copy.wait()
    for k in range(1, n):
        slot = decoded_all.at[me ^ k]
        remote(slot, slot, send_d.at[k], recv_d.at[k], me ^ 1).wait_recv()
    decoded = decoded_all[...].reshape(n * outs, 128).astype(f32).T.astype(bf)
    fine_rows = jnp.dot(decoded, wf[...], preferred_element_type=f32).astype(bf)

    def slab(d, y, x):
        p = 4 * (d // 2) + 2 * (y // 2) + x // 2
        tap = 4 * (d % 2) + 2 * (y % 2) + x % 2
        return fine_rows[16 * p : 16 * (p + 1), chans * tap : chans * (tap + 1)]

    def slabs_of(d):
        return jnp.concatenate([slab(d, y, x) for y in range(4) for x in range(4)], axis=0)

    for d in range(0, depth, 2):
        plane = jnp.concatenate([slabs_of(d), slabs_of(d + 1)], axis=1)
        plane = jnp.dot(order[...], plane, preferred_element_type=f32).astype(bf)
        out_ref[d] = plane[:, 0:chans]
        out_ref[d + 1] = plane[:, chans : 2 * chans]
    for copy in w_copies + d_copies:
        copy.wait_send()
    for gather in (gather_a, gather_b, gather_c, gather_s):
        gather.drain()


def net(
    volume, first_kernel, second_kernel, deep_kernel, deeper_kernel,
    rise_kernel, decode_kernel, final_kernel,
):
    n = lax.axis_size("sp")
    depth, height, width, chans = volume.shape
    mid = second_kernel.shape[4]
    low = rise_kernel.shape[3]
    part = deep_kernel.shape[4]
    block = decode_kernel.shape[3]
    outs = mid // n
    coarse = 16 * n
    area = height * width
    taps = 27 * outs
    wide = -(-taps // LANES) * LANES
    bf = jnp.bfloat16
    vmem = pltpu.VMEM
    dma = pltpu.SemaphoreType.DMA
    hbm = pl.BlockSpec(memory_space=pltpu.HBM)

    def tap_rows(kernel):
        return jnp.transpose(kernel, (0, 1, 2, 4, 3)).reshape(27 * part, kernel.shape[3])

    return pl.pallas_call(
        functools.partial(net_kernel, n),
        out_shape=jax.ShapeDtypeStruct((depth, area, chans), bf),
        in_specs=[hbm] * 8,
        out_specs=pl.BlockSpec(memory_space=pltpu.VMEM),
        scratch_shapes=[
            vmem((depth, area, chans), bf),
            vmem((2, area, chans), bf),
            vmem((36 * 16, area), bf),
            vmem((16 * 16, area // 4), bf),
            vmem((area, area), bf),
            vmem((18 * chans, 2 * chans), bf),
            vmem((3, 9 * chans, mid), bf),
            vmem((27 * part, mid), bf),
            vmem((27 * part, low), bf),
            vmem((8, low, mid), bf),
            vmem((27, block, mid), bf),
            vmem((mid, 8 * chans), bf),
            vmem((depth + 2, 36 * 16, chans), bf),
            vmem((depth // 2 + 2, area // 4, chans), bf),
            vmem((depth // 2 + 2, 16 * 16, chans), bf),
            vmem((n, 16, mid), bf),
            vmem((n, part, coarse), bf),
            vmem((n, part, coarse), bf),
            vmem((n, 8, 16, mid), bf),
            vmem((n, block, wide), bf),
            vmem((n, block, wide), bf),
            vmem((taps, 2 * mid), bf),
            vmem((8, taps, coarse), jnp.float32),
            vmem((n, outs, 128), bf),
            vmem((n, outs, 128), bf),
            dma((24,)),
            dma((2,)), dma((2,)), dma((2,)), dma((2,)),
            dma((2 * n,)), dma((n,)), dma((2 * n,)), dma((n,)),
            dma((2 * n,)), dma((n,)), dma((2 * n,)), dma((n,)),
            dma((n,)), dma((n,)), dma((n,)), dma((n,)), dma((n,)), dma((n,)),
            pltpu.SemaphoreType.REGULAR((2,)),
        ],
        compiler_params=pltpu.CompilerParams(
            collective_id=2, has_side_effects=True, vmem_limit_bytes=107 << 19
        ),
        name="net",
    )(
        volume.reshape(depth, area, chans),
        first_kernel.reshape(3, 9 * chans, chans),
        second_kernel.reshape(3, 9 * chans, mid),
        tap_rows(deep_kernel),
        tap_rows(deeper_kernel),
        rise_kernel.reshape(8, low, mid),
        decode_kernel.reshape(27, block, mid),
        final_kernel.reshape(8, mid, chans),
    ).reshape(volume.shape)


def split_body(
    volume, first_kernel, second_kernel, deep_kernel, deeper_kernel,
    rise_kernel, decode_kernel, final_kernel,
):
    n = lax.axis_size("sp")
    if n != 16 or lax.axis_size("rep") != 2 or decode_kernel.shape[4] % (16 * n):
        return body(
            volume, first_kernel, second_kernel, deep_kernel, deeper_kernel,
            rise_kernel, decode_kernel, final_kernel,
        )
    return net(
        volume, first_kernel, second_kernel, deep_kernel, deeper_kernel,
        rise_kernel, decode_kernel, final_kernel,
    )


def solution(mesh):
    return jax.shard_map(
        split_body,
        mesh=mesh,
        in_specs=(
            P(("rep", "sp"), None, None, None),
            P(),
            P(),
            P(None, None, None, None, "sp"),
            P(None, None, None, None, "sp"),
            P(),
            P(None, None, None, "sp", None),
            P(),
        ),
        out_specs=P(("rep", "sp"), None, None, None),
        check_vma=False,
    )
```

```python
import functools

import jax
import jax.numpy as jnp
from jax import lax
from jax.experimental import pallas as pl
from jax.experimental.pallas import tpu as pltpu
from jax.sharding import PartitionSpec as P

LANES = 128


def remote(src, dst, send_sem, recv_sem, target):
    return pltpu.make_async_remote_copy(
        src_ref=src, dst_ref=dst, send_sem=send_sem, recv_sem=recv_sem,
        device_id={"sp": target}, device_id_type=pl.DeviceIdType.MESH,
    )


def trade_edges(n, first, last, low, high, send_sem, recv_sem):
    me = lax.axis_index("sp")
    upward = remote(last, low, send_sem.at[0], recv_sem.at[0], lax.rem(me + 1, n))
    downward = remote(first, high, send_sem.at[1], recv_sem.at[1], lax.rem(me + n - 1, n))

    @pl.when(me < n - 1)
    def _():
        upward.start()

    @pl.when(me > 0)
    def _():
        downward.start()

    @pl.when(me == 0)
    def _():
        low[...] = jnp.zeros(low.shape, low.dtype)

    @pl.when(me == n - 1)
    def _():
        high[...] = jnp.zeros(high.shape, high.dtype)

    def finish():
        @pl.when(me > 0)
        def _():
            upward.wait_recv()
            downward.wait_send()

        @pl.when(me < n - 1)
        def _():
            downward.wait_recv()
            upward.wait_send()

    return finish


def greet_neighbours(n):
    me = lax.axis_index("sp")
    barrier = pltpu.get_barrier_semaphore()

    @pl.when(me > 0)
    def _():
        pl.semaphore_signal(
            barrier, inc=1, device_id={"sp": lax.rem(me + n - 1, n)},
            device_id_type=pl.DeviceIdType.MESH,
        )

    @pl.when(me < n - 1)
    def _():
        pl.semaphore_signal(
            barrier, inc=1, device_id={"sp": lax.rem(me + 1, n)},
            device_id_type=pl.DeviceIdType.MESH,
        )

    @pl.when((me > 0) & (me < n - 1))
    def _():
        pl.semaphore_wait(barrier, 2)

    @pl.when((me == 0) | (me == n - 1))
    def _():
        pl.semaphore_wait(barrier, 1)


def first_level_kernel(
    n, depth, height, width,
    volume_ref, weight_ref, out_ref,
    ends, taps, sums, send_a, recv_a, send_b, recv_b,
):
    area = height * width
    chans = volume_ref.shape[2]
    greet_neighbours(n)
    finish = trade_edges(
        n, volume_ref.at[0], volume_ref.at[depth - 1], ends.at[0], ends.at[1], send_a, recv_a
    )
    index = lax.broadcasted_iota(jnp.int32, (area, 1), 0) & (width - 1)
    blank = jnp.zeros((depth + 2, width, 3 * chans), jnp.bfloat16)
    taps[:, 0:width] = blank
    taps[:, area + width : area + 2 * width] = blank

    def spread(at, values):
        taps[at, width : area + width, chans : 2 * chans] = values
        values = values.astype(jnp.float32)
        left = jnp.where(index > 0, pltpu.roll(values, 1, 0), 0.0)
        right = jnp.where(index < width - 1, pltpu.roll(values, area - 1, 0), 0.0)
        taps[at, width : area + width, 0:chans] = left.astype(jnp.bfloat16)
        taps[at, width : area + width, 2 * chans : 3 * chans] = right.astype(jnp.bfloat16)

    for d in range(depth):
        spread(d + 1, volume_ref[d])
    finish()
    spread(0, ends[0])
    spread(depth + 1, ends[1])
    for pair in range(depth // 2):
        total = jnp.zeros((2 * area, weight_ref.shape[3]), jnp.float32)
        for a in range(3):
            for b in range(3):
                block = taps[2 * pair + a : 2 * pair + a + 2, b * width : b * width + area]
                total += jnp.dot(
                    block.reshape(2 * area, 3 * chans), weight_ref[a, b],
                    preferred_element_type=jnp.float32,
                )
        total = jnp.maximum(total, 0.0).astype(jnp.bfloat16).astype(jnp.float32)
        total = total[0:area] + total[area : 2 * area]
        total = total.reshape(height // 2, 2, width, total.shape[1]).sum(axis=1)
        sums[...] = total.reshape(area // 2, total.shape[2])
        total = sums[pl.ds(0, area // 4, 2), :] + sums[pl.ds(1, area // 4, 2), :]
        out_ref[1 + pair] = (total * 0.125).astype(jnp.bfloat16)
    halves = depth // 2
    trade_edges(
        n, out_ref.at[1], out_ref.at[halves], out_ref.at[0], out_ref.at[halves + 1],
        send_b, recv_b,
    )()


def first_level(volume, kernel):
    n = lax.axis_size("sp")
    depth, height, width, chans = volume.shape
    outs = kernel.shape[4]
    area = height * width
    vmem = pl.BlockSpec(memory_space=pltpu.VMEM)
    padded = pl.pallas_call(
        functools.partial(first_level_kernel, n, depth, height, width),
        out_shape=jax.ShapeDtypeStruct((depth // 2 + 2, area // 4, outs), jnp.bfloat16),
        in_specs=[vmem] * 2,
        out_specs=vmem,
        scratch_shapes=[
            pltpu.VMEM((2, area, chans), jnp.bfloat16),
            pltpu.VMEM((depth + 2, area + 2 * width, 3 * chans), jnp.bfloat16),
            pltpu.VMEM((area // 2, outs), jnp.float32),
        ]
        + [pltpu.SemaphoreType.DMA((2,))] * 4,
        compiler_params=pltpu.CompilerParams(
            collective_id=1, has_side_effects=True, vmem_limit_bytes=16 << 20
        ),
        name="first_level",
    )(volume.reshape(depth, area, chans), kernel.reshape(3, 3, 3 * chans, outs))
    return padded.reshape(depth // 2 + 2, height // 2, width // 2, outs)


def conv_depth(padded, kernel):
    result = lax.conv_general_dilated(
        padded[None],
        kernel,
        (1, 1, 1),
        ((0, 0), (1, 1), (1, 1)),
        dimension_numbers=("NDHWC", "DHWIO", "NDHWC"),
        preferred_element_type=jnp.float32,
    )
    return result[0]


def pool_mean(values):
    depth, height, width, chans = values.shape
    blocks = values.astype(jnp.float32).reshape(depth // 2, 2, height // 2, 2, width // 2, 2, chans)
    return jnp.mean(blocks, axis=(1, 3, 5)).astype(jnp.bfloat16)


def up_conv(values, kernel):
    depth, height, width, chans = values.shape
    result = jnp.einsum("dhwi,abcio->dahbwco", values, kernel, preferred_element_type=jnp.float32)
    return result.reshape(2 * depth, 2 * height, 2 * width, kernel.shape[4])


def conv_rows(values, weight_ref, height, width):
    rows = values.shape[0]
    index = lax.broadcasted_iota(jnp.int32, (rows, 1), 0)
    w_at = index & (width - 1)
    h_at = (index >> (width.bit_length() - 1)) & (height - 1)
    part, chans = weight_ref.shape[2:]
    blank = jnp.zeros((LANES - 3 * part, chans), weight_ref.dtype)
    total = jnp.zeros((rows, LANES), jnp.float32)
    for b in range(3):
        for c in range(3):
            shift = width * (b - 1) + (c - 1)
            moved = values if shift == 0 else pltpu.roll(values, (-shift) % rows, 0)
            h_to, w_to = h_at + (b - 1), w_at + (c - 1)
            keep = (h_to >= 0) & (h_to < height) & (w_to >= 0) & (w_to < width)
            moved = jnp.where(keep, moved, 0.0).astype(jnp.bfloat16)
            tap = 3 * b + c
            weight = jnp.concatenate([weight_ref[a, tap] for a in range(3)] + [blank], axis=0)
            total += lax.dot_general(
                moved, weight, (((1,), (1,)), ((), ())), preferred_element_type=jnp.float32
            )
    return total


def bottleneck_kernel(
    n, height, width, part,
    pooled_ref, skip_ref, deep_w_ref, deeper_w_ref, out_ref, near_ref,
    whole, deep_mine, deep_all, packed,
    send_a, recv_a, send_b, recv_b, send_c, recv_c, send_d, recv_d,
):
    me = lax.axis_index("sp")
    area = height * width
    voxels = n * area
    partner = me + 1 - 2 * (me % 2)
    half = n // 2

    barrier = pltpu.get_barrier_semaphore()

    def greet(k, carry):
        pl.semaphore_signal(
            barrier, inc=1, device_id={"sp": lax.rem(me + k, n)},
            device_id_type=pl.DeviceIdType.MESH,
        )
        return carry

    lax.fori_loop(1, n, greet, 0)
    pl.semaphore_wait(barrier, n - 1)

    def gather(mine, everyone, send_sem, recv_sem):
        def slot(source):
            return everyone.at[source]

        def direct(k):
            target = lax.rem(me + 2 * k, n)
            return remote(mine, slot(me), send_sem.at[k], recv_sem.at[me], target)

        def relay(k):
            source = lax.rem(me + 2 * (half - k), n)
            return remote(
                slot(source), slot(source), send_sem.at[half + k], recv_sem.at[source], partner
            )

        def arrival(source):
            return remote(mine, slot(source), send_sem.at[0], recv_sem.at[source], partner)

        def start_direct(k, carry):
            direct(k).start()
            return carry

        to_partner = remote(mine, slot(me), send_sem.at[0], recv_sem.at[me], partner)
        lax.fori_loop(1, half, start_direct, 0)
        to_partner.start()
        everyone[me] = mine[...]

        def pass_on(k, carry):
            arrival(lax.rem(me + 2 * (half - k), n)).wait_recv()
            relay(k).start()
            return carry

        lax.fori_loop(1, half, pass_on, 0)

        def from_partner(k, carry):
            arrival(lax.rem(partner + 2 * (half - k), n)).wait_recv()
            return carry

        lax.fori_loop(0, half, from_partner, 0)

        def finish():
            to_partner.wait_send()

            def sent(k, carry):
                direct(k).wait_send()
                relay(k).wait_send()
                return carry

            lax.fori_loop(1, half, sent, 0)

        return finish

    finish_a = gather(pooled_ref, whole, send_a, recv_a)
    depth = skip_ref.shape[0]
    finish_d = trade_edges(
        n, skip_ref.at[0], skip_ref.at[depth - 1], near_ref.at[0], near_ref.at[1], send_d, recv_d
    )
    lanes = lax.broadcasted_iota(jnp.int32, (1, voxels), 1)
    values = whole[...].astype(jnp.float32).reshape(voxels, pooled_ref.shape[1])
    deep = conv_rows(values, deep_w_ref, height, width).T
    below = jnp.where(lanes >= area, pltpu.roll(deep[0:part], area, 1), 0.0)
    above = jnp.where(
        lanes < voxels - area, pltpu.roll(deep[2 * part : 3 * part], voxels - area, 1), 0.0
    )
    deep = below + deep[part : 2 * part] + above
    deep_mine[...] = jnp.maximum(deep, 0.0).astype(jnp.bfloat16)
    finish_b = gather(deep_mine, deep_all, send_b, recv_b)

    values = deep_all[...].astype(jnp.float32).reshape(n * part, voxels).T
    deeper = conv_rows(values, deeper_w_ref, height, width)
    rows = lax.broadcasted_iota(jnp.int32, (voxels, 1), 0)

    def down(block):
        return jnp.where(rows >= area, pltpu.roll(block, area, 0), 0.0)

    def up(block):
        return jnp.where(rows < voxels - area, pltpu.roll(block, voxels - area, 0), 0.0)

    deeper = (
        down(deeper)
        + pltpu.roll(deeper, LANES - part, 1)
        + up(pltpu.roll(deeper, LANES - 2 * part, 1))
    )
    deeper = jnp.maximum(deeper, 0.0)
    lane = lax.broadcasted_iota(jnp.int32, (1, LANES), 1)
    deeper = jnp.where(
        lane < part,
        down(deeper),
        jnp.where(
            lane < 2 * part,
            pltpu.roll(deeper, part, 1),
            up(pltpu.roll(deeper, 2 * part, 1)),
        ),
    )
    packed[...] = deeper.astype(jnp.bfloat16).reshape(n, area, LANES)

    def deal(k):
        target = lax.rem(me + k, n)
        return remote(packed.at[target], out_ref.at[me], send_c.at[k], recv_c.at[me], target)

    def start_deal(k, carry):
        deal(k).start()
        return carry

    lax.fori_loop(1, n, start_deal, 0)
    out_ref[me] = packed[me]

    def receive(k, carry):
        source = lax.rem(me + k, n)
        remote(
            packed.at[source], out_ref.at[source], send_c.at[k], recv_c.at[source], source
        ).wait_recv()
        return carry

    lax.fori_loop(1, n, receive, 0)

    def sent(k, carry):
        deal(k).wait_send()
        return carry

    lax.fori_loop(1, n, sent, 0)
    finish_a()
    finish_b()
    finish_d()


def out_major(kernel):
    chans, part = kernel.shape[3], kernel.shape[4]
    return jnp.transpose(kernel, (0, 1, 2, 4, 3)).reshape(3, 9, part, chans)


def bottleneck(pooled, skip, deep_kernel, deeper_kernel):
    n = lax.axis_size("sp")
    _, height, width, chans = pooled.shape
    part = deep_kernel.shape[4]
    area = height * width
    voxels = n * area
    vmem = pl.BlockSpec(memory_space=pltpu.VMEM)
    received, near = pl.pallas_call(
        functools.partial(bottleneck_kernel, n, height, width, part),
        out_shape=(
            jax.ShapeDtypeStruct((n, area, LANES), jnp.bfloat16),
            jax.ShapeDtypeStruct((2,) + skip.shape[1:], jnp.bfloat16),
        ),
        in_specs=[vmem] * 4,
        out_specs=(vmem, vmem),
        scratch_shapes=[
            pltpu.VMEM((n, area, chans), jnp.bfloat16),
            pltpu.VMEM((part, voxels), jnp.bfloat16),
            pltpu.VMEM((n, part, voxels), jnp.bfloat16),
            pltpu.VMEM((n, area, LANES), jnp.bfloat16),
        ]
        + [pltpu.SemaphoreType.DMA((n,))] * 6
        + [pltpu.SemaphoreType.DMA((2,))] * 2,
        compiler_params=pltpu.CompilerParams(
            collective_id=0, has_side_effects=True, vmem_limit_bytes=24 << 20
        ),
        name="bottleneck",
    )(pooled.reshape(area, chans), skip, out_major(deep_kernel), out_major(deeper_kernel))
    blocks = received[:, :, : 3 * part].reshape(n, area, 3, part)
    return jnp.transpose(blocks, (2, 1, 0, 3)).reshape(3, height, width, n * part), near


def body(
    volume,
    first_kernel,
    second_kernel,
    deep_kernel,
    deeper_kernel,
    rise_kernel,
    decode_kernel,
    final_kernel,
):
    padded_pool = first_level(volume, first_kernel)
    skip = jax.nn.relu(conv_depth(padded_pool, second_kernel)).astype(jnp.bfloat16)
    pooled_two = pool_mean(skip)
    deeper_near, skip_near = bottleneck(pooled_two, skip, deep_kernel, deeper_kernel)
    padded_skip = jnp.concatenate([skip_near[:1], skip, skip_near[1:]], axis=0)
    risen = up_conv(deeper_near, rise_kernel)[1:-1].astype(jnp.bfloat16)
    padded_joined = jnp.concatenate([risen, padded_skip], axis=3)
    whole_decode_kernel = lax.all_gather(decode_kernel, "sp", axis=3, tiled=True)
    decoded = jax.nn.relu(conv_depth(padded_joined, whole_decode_kernel)).astype(jnp.bfloat16)
    return up_conv(decoded, final_kernel).astype(jnp.bfloat16)


def picks(index, columns):
    lane = lax.broadcasted_iota(jnp.int32, (index.shape[0], columns), 1)
    return jnp.where(lane == index, 1.0, 0.0).astype(jnp.bfloat16)


def spread_matrix():
    row = lax.broadcasted_iota(jnp.int32, (36 * 16, 1), 0)
    slab = row >> 4
    eh = (slab * 43) >> 8
    h = ((row >> 2) & 3) * 4 + eh - 1
    w = (row & 3) * 4 + (slab - 6 * eh) - 1
    inside = (h >= 0) & (h < 16) & (w >= 0) & (w < 16)
    return picks(jnp.where(inside, h * 16 + w, -1), 256)


def spread_matrix_two():
    row = lax.broadcasted_iota(jnp.int32, (16 * 16, 1), 0)
    h = ((row >> 2) & 3) * 2 + (row >> 6) - 1
    w = (row & 3) * 2 + ((row >> 4) & 3) - 1
    inside = (h >= 0) & (h < 8) & (w >= 0) & (w < 8)
    at = (h & 1) * 32 + (w & 1) * 16 + (h >> 1) * 4 + (w >> 1)
    return picks(jnp.where(inside, at, -1), 64)


def gather_matrix():
    row = lax.broadcasted_iota(jnp.int32, (256, 1), 0)
    h, w = row >> 4, row & 15
    return picks((h & 3) * 64 + (w & 3) * 16 + (h >> 2) * 4 + (w >> 2), 256)


def block_transpose(pieces, width):
    pieces = list(pieces)
    count = len(pieces)
    block = lax.broadcasted_iota(jnp.int32, pieces[0].shape, 1) // width
    step = 1
    while step < count:
        low = (block & step) == 0
        for i in range(count):
            if i & step:
                continue
            a, b = pieces[i], pieces[i + step]
            pieces[i] = jnp.where(low, a, pltpu.roll(b, width * step, 1))
            pieces[i + step] = jnp.where(low, pltpu.roll(a, 128 - width * step, 1), b)
        step *= 2
    return pieces


def moved(values, by, keep):
    lanes = values.shape[1]
    return jnp.where(keep, pltpu.roll(values, by % lanes, 1), 0.0)


class Lanes:
    def __init__(self, count):
        lane = lax.broadcasted_iota(jnp.int32, (1, count), 1)
        wc, hc, d = lane & 3, (lane >> 2) & 3, lane >> 4
        top = count // 16 - 1
        self.after = {1: wc > 0, 4: hc > 0, 16: d > 0}
        self.before = {1: wc < 3, 4: hc < 3, 16: d < top}

    def back(self, values, by):
        return moved(values, by, self.after[by])

    def ahead(self, values, by):
        return moved(values, -by, self.before[by])


def add_taps(lanes, y, outs):
    def row(a, b, c):
        at = (9 * a + 3 * b + c) * outs
        return y[at : at + outs]

    def tall(c):
        return jnp.concatenate([row(a, b, c) for b in range(3) for a in range(3)], axis=0)

    y = tall(1) + lanes.back(tall(0), 1) + lanes.ahead(tall(2), 1)
    y = [y[i * 3 * outs : (i + 1) * 3 * outs] for i in range(3)]
    y = y[1] + lanes.back(y[0], 4) + lanes.ahead(y[2], 4)
    y = [y[i * outs : (i + 1) * outs] for i in range(3)]
    return y[1] + lanes.back(y[0], 16) + lanes.ahead(y[2], 16)


def add_fine_taps(lanes, load, outs):
    def pair(zero, one, by):
        even = zero[1] + one[2] + lanes.back(one[0], by)
        odd = one[1] + zero[0] + lanes.ahead(zero[2], by)
        return even, odd

    planes = {}
    for pd in range(2):
        rows = {}
        for ph in range(2):
            def taps(pw):
                p = 4 * pd + 2 * ph + pw
                return [
                    jnp.concatenate(
                        [load(p, 9 * a + 3 * b + c) for b in range(3) for a in range(3)], axis=0
                    )
                    for c in range(3)
                ]

            rows[ph] = pair(taps(0), taps(1), 1)
        for qw in range(2):
            def cut(ph):
                return [rows[ph][qw][i * 3 * outs : (i + 1) * 3 * outs] for i in range(3)]

            planes[pd, qw] = pair(cut(0), cut(1), 4)
    result = [None] * 8
    for qw in range(2):
        for qh in range(2):
            def cut(pd):
                return [planes[pd, qw][qh][i * outs : (i + 1) * outs] for i in range(3)]

            low, high = pair(cut(0), cut(1), 16)
            result[2 * qh + qw] = low
            result[4 + 2 * qh + qw] = high
    return result


class Gather:
    def __init__(self, n, slots, send_sem, recv_sem):
        self.n, self.slots, self.send_sem, self.recv_sem = n, slots, send_sem, recv_sem
        self.me = lax.axis_index("sp")
        self.sent = []
        self.others = list(range(n - 2, 0, -2))

    def send(self, source, target):
        slot = self.slots.at[self.me ^ source]
        copy = remote(
            slot, slot, self.send_sem.at[len(self.sent)], self.recv_sem.at[source ^ target],
            self.me ^ target,
        )
        copy.start()
        self.sent.append(copy)

    def wait(self, source):
        slot = self.slots.at[self.me ^ source]
        remote(slot, slot, self.send_sem.at[0], self.recv_sem.at[source], self.me ^ 1).wait_recv()

    def start(self):
        for k in self.others:
            self.send(0, k)
        self.send(0, 1)

    def relay(self):
        for k in reversed(self.others):
            self.wait(k)
            self.send(k, 1)

    def finish(self):
        for k in range(1, self.n, 2):
            self.wait(k)

    def pass_on(self, source, *targets):
        self.wait(source)
        for target in targets:
            self.send(source, target)

    def drain(self):
        for copy in self.sent:
            copy.wait_send()


class Doubling(Gather):
    def steps(self):
        bits = [1 << i for i in range(self.n.bit_length() - 1)]
        known = [[0]]
        for _ in bits:
            known.append([k | bit for k in known[-1] for bit in bits if bit < (k & -k or self.n)])
        return bits, known

    def start(self):
        bits, _ = self.steps()
        for bit in reversed(bits):
            self.send(0, bit)

    def hop(self, step):
        bits, known = self.steps()
        for k in known[step]:
            self.pass_on(k, *[bit for bit in reversed(bits) if bit < (k & -k)])


def net_kernel(
    n,
    volume_hbm, first_hbm, second_hbm, deep_hbm, deeper_hbm, rise_hbm, decode_hbm, final_hbm,
    out_ref,
    vol, vhalo, pp, pp2, order, wpair, w2, wd, wdd, rw, kloc, wf,
    ex, pool, ex2, pooled_all, deep_all, deeper_all, skip_all,
    wsend, wall, wt, ys, dsend, decoded_all,
    load_sem, send_v, recv_v, send_p, recv_p,
    send_a, recv_a, send_b, recv_b, send_c, recv_c, send_s, recv_s,
    send_w, recv_w, send_f, recv_f, send_d, recv_d, ready,
):
    me = lax.axis_index("sp")
    bf = jnp.bfloat16
    f32 = jnp.float32
    depth = vol.shape[0]
    k1 = first_hbm.shape[1]
    part = wd.shape[0] // 27
    outs = 256 // n
    coarse = 16 * n

    loads = []

    def load(src, dst):
        copy = pltpu.make_async_copy(src, dst, load_sem.at[len(loads)])
        copy.start()
        loads.append(copy)
        return copy

    get_vol = load(volume_hbm, vol)
    get_k = load(decode_hbm, kloc)
    get_w1 = [
        load(first_hbm.at[1], wpair.at[0:k1, 0:128]),
        load(first_hbm.at[0], wpair.at[0:k1, 128:256]),
        load(first_hbm.at[2], wpair.at[k1 : 2 * k1, 0:128]),
        load(first_hbm.at[1], wpair.at[k1 : 2 * k1, 128:256]),
    ]
    get_w2 = load(second_hbm, w2)
    get_wd = load(deep_hbm, wd)
    get_wdd = load(deeper_hbm, wdd)
    get_rw = load(rise_hbm, rw)
    chans = final_hbm.shape[2]
    get_wf = [load(final_hbm.at[i], wf.at[:, chans * i : chans * (i + 1)]) for i in range(8)]

    twin = lax.axis_index("rep")
    barrier = pltpu.get_barrier_semaphore()
    plane, columns = (1, 2, 3), (4, 8)

    def say(sem, target):
        pl.semaphore_signal(
            sem, inc=1, device_id={"sp": target}, device_id_type=pl.DeviceIdType.MESH
        )

    corner = ((me % 4 == 0) & (me > 0)) | ((me % 4 == 3) & (me < n - 1))
    beyond = jnp.where(me % 4 == 0, me + n - 1, me + 1) % n
    pl.when(corner)(lambda: say(barrier, beyond))
    for k in columns[::-1] + plane:
        say(barrier, me ^ k)
    pl.semaphore_signal(
        barrier, inc=1, device_id={"rep": 1 - twin, "sp": me},
        device_id_type=pl.DeviceIdType.MESH,
    )

    def meet_near():
        near = len(plane) + len(columns) + 1

        @pl.when(corner)
        def _():
            pl.semaphore_wait(barrier, near + 1)

        @pl.when(jnp.logical_not(corner))
        def _():
            pl.semaphore_wait(barrier, near)

        for k in plane:
            say(ready.at[0], me ^ k)

    def meet_planes():
        pl.semaphore_wait(ready.at[0], len(plane))
        for k in columns:
            say(ready.at[1], me ^ k)

    def meet_all():
        pl.semaphore_wait(ready.at[1], len(columns))

    def spread(planes, to):
        get = jnp.concatenate(planes, axis=1)
        result = jnp.dot(pp[...], get, preferred_element_type=f32).astype(bf)
        for i, at in enumerate(to):
            ex[at] = result[:, 128 * i : 128 * (i + 1)]

    pp[...] = spread_matrix()
    get_vol.wait()
    for d in range(0, depth, 2):
        spread([vol[d], vol[d + 1]], [d + 1, d + 2])

    meet_near()
    finish_v = trade_edges(
        n, vol.at[0], vol.at[depth - 1], vhalo.at[0], vhalo.at[1], send_v, recv_v
    )
    pp2[...] = spread_matrix_two()
    order[...] = gather_matrix()

    get_k.wait()
    per = 128 // outs
    for half in range(256 // 128):
        for group in range(wsend.shape[2] // 128):
            taps = []
            for i in range(per):
                tap = per * group + i
                if tap < 27:
                    taps.append(kloc[tap, :, 128 * half : 128 * (half + 1)].astype(f32))
                else:
                    taps.append(jnp.zeros((kloc.shape[1], 128), f32))
            for j, piece in enumerate(block_transpose(taps, outs)):
                wsend[per * half + j, :, 128 * group : 128 * (group + 1)] = piece.astype(bf)

    w_copies = []

    def w_piece(k):
        return remote(wsend.at[me ^ k], wall.at[me], send_w.at[k], recv_w.at[k], me ^ k)

    def w_arrived(k):
        slot = wall.at[me ^ k]
        remote(slot, slot, send_w.at[k], recv_w.at[k], me ^ 1).wait_recv()

    def w_start(batch):
        for k in [2 * i + twin for i in batch] if batch else [1]:
            copy = w_piece(k)
            copy.start()
            w_copies.append(copy)

    def w_forward():
        for i in range(1, n // 2):
            k = 2 * i + twin
            w_arrived(k)
            slot = wall.at[me ^ k]
            copy = pltpu.make_async_remote_copy(
                src_ref=slot, dst_ref=slot, send_sem=send_f.at[i], recv_sem=recv_f.at[i],
                device_id={"rep": 1 - twin, "sp": me}, device_id_type=pl.DeviceIdType.MESH,
            )
            copy.start()
            w_copies.append(copy)

    def w_finish():
        w_arrived(1)
        for i in range(1, n // 2):
            slot = wall.at[me ^ (2 * i + 1 - twin)]
            pltpu.make_async_remote_copy(
                src_ref=slot, dst_ref=slot, send_sem=send_f.at[i], recv_sem=recv_f.at[i],
                device_id={"rep": 1 - twin, "sp": me}, device_id_type=pl.DeviceIdType.MESH,
            ).wait_recv()

    batches = [[5], [4, 3, 2, 1], [7, 6]]
    w_start([])
    wall[me] = wsend[me]

    def taken(at, b):
        columns = []
        for c in range(3):
            columns.append(
                jnp.concatenate(
                    [ex[at, pl.ds(((b + hm) * 6 + c) * 16, 64), :] for hm in range(4)], axis=0
                )
            )
        return columns

    def rows_of(at):
        return jnp.concatenate(sum([taken(at, b) for b in range(3)], []), axis=1)

    for copy in get_w1:
        copy.wait()

    def both(at):
        left = jnp.concatenate([rows_of(at), rows_of(at + 1)], axis=1)
        return jnp.dot(left, wpair[...], preferred_element_type=f32)

    pairs = [both(1), both(3)]
    own_low = jnp.dot(rows_of(2), wpair[0:k1, 128:256], preferred_element_type=f32)
    own_high = jnp.dot(rows_of(3), wpair[k1 : 2 * k1, 0:128], preferred_element_type=f32)
    def turn_w():
        for at in range(0, wt.shape[1], 128):
            block = wall[pl.ds(at // part, 128 // part)].reshape(128, wall.shape[2])
            wt[:, at : at + 128] = block.astype(f32).T.astype(bf)[0 : wt.shape[0]]

    meet_planes()
    w_start(batches[0])
    finish_v()
    spread([vhalo[0], vhalo[1]], [0, depth + 1])
    far_low = jnp.dot(rows_of(0), wpair[0:k1, 128:256], preferred_element_type=f32)
    far_high = jnp.dot(rows_of(5), wpair[k1 : 2 * k1, 0:128], preferred_element_type=f32)
    planes = [
        pairs[0][:, 0:128] + far_low,
        pairs[0][:, 128:256] + own_high,
        pairs[1][:, 0:128] + own_low,
        pairs[1][:, 128:256] + far_high,
    ]
    planes = [jnp.maximum(t, 0.0).astype(bf).astype(f32) for t in planes]
    for i in range(2):
        total = planes[2 * i] + planes[2 * i + 1]
        for ph in range(2):
            for pw in range(2):
                slabs = [
                    total[((2 * ph + y) * 4 + 2 * pw + x) * 16 :][:16]
                    for y in range(2) for x in range(2)
                ]
                slab = (slabs[0] + slabs[1]) + (slabs[2] + slabs[3])
                pool[1 + i, pl.ds((2 * ph + pw) * 16, 16), :] = (slab * 0.125).astype(bf)

    finish_p = trade_edges(n, pool.at[1], pool.at[2], pool.at[0], pool.at[3], send_p, recv_p)
    w_start(batches[1])
    get_w2.wait()

    def spread_two(at):
        ex2[at] = jnp.dot(pp2[...], pool[at], preferred_element_type=f32).astype(bf)

    def rows_two(a):
        columns = []
        for b in range(3):
            for c in range(3):
                columns.append(
                    jnp.concatenate(
                        [
                            ex2[a + i, pl.ds(((b + ph) * 4 + c) * 16, 32), :]
                            for i in range(2) for ph in range(2)
                        ],
                        axis=0,
                    )
                )
        return jnp.concatenate(columns, axis=1)

    spread_two(1)
    spread_two(2)
    skip = jnp.dot(rows_two(1), w2[1], preferred_element_type=f32)
    finish_p()
    spread_two(0)
    spread_two(3)
    skip += jnp.dot(rows_two(0), w2[0], preferred_element_type=f32)
    skip += jnp.dot(rows_two(2), w2[2], preferred_element_type=f32)
    skip = jnp.maximum(skip, 0.0).astype(bf)
    skip_all[me] = skip.reshape(skip_all.shape[1:])
    skip = skip.astype(f32)
    slabs = [skip[16 * i : 16 * (i + 1)] for i in range(8)]
    while len(slabs) > 1:
        slabs = [slabs[i] + slabs[i + 1] for i in range(0, len(slabs), 2)]
    pooled_all[me] = (slabs[0] * 0.125).astype(bf)

    gather_a = Gather(n, pooled_all, send_a, recv_a)
    gather_b = Gather(n, deep_all, send_b, recv_b)
    gather_c = Gather(n, deeper_all, send_c, recv_c)
    gather_s = Doubling(n, skip_all, send_s, recv_s)
    meet_all()
    gather_a.start()
    gather_s.start()
    w_start(batches[2])
    lanes = Lanes(coarse)
    get_wd.wait()
    get_wdd.wait()
    get_rw.wait()
    gather_a.relay()
    gather_a.finish()
    y = lax.dot_general(
        wd[...], pooled_all[...].reshape(coarse, pooled_all.shape[2]),
        (((1,), (1,)), ((), ())), preferred_element_type=f32,
    )
    deep_all[me] = jnp.maximum(add_taps(lanes, y, part), 0.0).astype(bf)
    gather_b.start()
    gather_s.hop(1)
    w_forward()
    gather_b.relay()
    gather_s.hop(2)
    gather_b.finish()
    y = jnp.dot(
        wdd[...], deep_all[...].reshape(n * part, coarse), preferred_element_type=f32
    )
    deeper_all[me] = jnp.maximum(add_taps(lanes, y, part), 0.0).astype(bf)
    gather_c.start()
    gather_s.hop(3)
    w_finish()
    turn_w()
    gather_s.hop(4)

    def fine(p, values, inner):
        ys[p] = lax.dot_general(
            wt[:, inner], values, (((1,), (1,)), ((), ())), preferred_element_type=f32
        )

    def tap_of(p, tap):
        return ys[p, outs * tap : outs * (tap + 1), :]

    for p in range(8):
        fine(p, skip_all[:, p].reshape(coarse, skip_all.shape[3]), slice(256, 512))
    from_skip = add_fine_taps(lanes, tap_of, outs)
    gather_c.relay()
    gather_c.finish()
    deeper = deeper_all[...].reshape(n * part, coarse).astype(f32).T.astype(bf)
    for p in range(8):
        risen = jnp.dot(deeper, rw[p], preferred_element_type=f32).astype(bf)
        fine(p, risen, slice(0, 256))
    from_risen = add_fine_taps(lanes, tap_of, outs)
    decoded = [jnp.maximum(s + r, 0.0) for s, r in zip(from_skip, from_risen)]
    for half in range(coarse // 128):
        cut = [t[:, 128 * half : 128 * (half + 1)] for t in decoded]
        for j, piece in enumerate(block_transpose(cut, 16)):
            dsend[8 * half + j] = piece.astype(bf)
    d_copies = []
    for k in range(n - 1, 0, -1):
        copy = remote(dsend.at[me ^ k], decoded_all.at[me], send_d.at[k], recv_d.at[k], me ^ k)
        copy.start()
        d_copies.append(copy)
    decoded_all[me] = dsend[me]
    for copy in w_copies:
        copy.wait_send()
    for gather in (gather_a, gather_b, gather_c, gather_s):
        gather.drain()
    for copy in d_copies:
        copy.wait_send()
    for copy in get_wf:
        copy.wait()
    for k in range(1, n):
        slot = decoded_all.at[me ^ k]
        remote(slot, slot, send_d.at[k], recv_d.at[k], me ^ 1).wait_recv()
    decoded = decoded_all[...].reshape(n * outs, 128).astype(f32).T.astype(bf)
    fine_rows = jnp.dot(decoded, wf[...], preferred_element_type=f32).astype(bf)

    def slab(d, y, x):
        p = 4 * (d // 2) + 2 * (y // 2) + x // 2
        tap = 4 * (d % 2) + 2 * (y % 2) + x % 2
        return fine_rows[16 * p : 16 * (p + 1), chans * tap : chans * (tap + 1)]

    def slabs_of(d):
        return jnp.concatenate([slab(d, y, x) for y in range(4) for x in range(4)], axis=0)

    for d in range(0, depth, 2):
        plane = jnp.concatenate([slabs_of(d), slabs_of(d + 1)], axis=1)
        plane = jnp.dot(order[...], plane, preferred_element_type=f32).astype(bf)
        out_ref[d] = plane[:, 0:chans]
        out_ref[d + 1] = plane[:, chans : 2 * chans]


def net(
    volume, first_kernel, second_kernel, deep_kernel, deeper_kernel,
    rise_kernel, decode_kernel, final_kernel,
):
    n = lax.axis_size("sp")
    depth, height, width, chans = volume.shape
    mid = second_kernel.shape[4]
    low = rise_kernel.shape[3]
    part = deep_kernel.shape[4]
    block = decode_kernel.shape[3]
    outs = mid // n
    coarse = 16 * n
    area = height * width
    taps = 27 * outs
    wide = -(-taps // LANES) * LANES
    bf = jnp.bfloat16
    vmem = pltpu.VMEM
    dma = pltpu.SemaphoreType.DMA
    hbm = pl.BlockSpec(memory_space=pltpu.HBM)

    def tap_rows(kernel):
        return jnp.transpose(kernel, (0, 1, 2, 4, 3)).reshape(27 * part, kernel.shape[3])

    return pl.pallas_call(
        functools.partial(net_kernel, n),
        out_shape=jax.ShapeDtypeStruct((depth, area, chans), bf),
        in_specs=[hbm] * 8,
        out_specs=pl.BlockSpec(memory_space=pltpu.VMEM),
        scratch_shapes=[
            vmem((depth, area, chans), bf),
            vmem((2, area, chans), bf),
            vmem((36 * 16, area), bf),
            vmem((16 * 16, area // 4), bf),
            vmem((area, area), bf),
            vmem((18 * chans, 2 * chans), bf),
            vmem((3, 9 * chans, mid), bf),
            vmem((27 * part, mid), bf),
            vmem((27 * part, low), bf),
            vmem((8, low, mid), bf),
            vmem((27, block, mid), bf),
            vmem((mid, 8 * chans), bf),
            vmem((depth + 2, 36 * 16, chans), bf),
            vmem((depth // 2 + 2, area // 4, chans), bf),
            vmem((depth // 2 + 2, 16 * 16, chans), bf),
            vmem((n, 16, mid), bf),
            vmem((n, part, coarse), bf),
            vmem((n, part, coarse), bf),
            vmem((n, 8, 16, mid), bf),
            vmem((n, block, wide), bf),
            vmem((n, block, wide), bf),
            vmem((taps, 2 * mid), bf),
            vmem((8, taps, coarse), jnp.float32),
            vmem((n, outs, 128), bf),
            vmem((n, outs, 128), bf),
            dma((24,)),
            dma((2,)), dma((2,)), dma((2,)), dma((2,)),
            dma((2 * n,)), dma((n,)), dma((2 * n,)), dma((n,)),
            dma((2 * n,)), dma((n,)), dma((2 * n,)), dma((n,)),
            dma((n,)), dma((n,)), dma((n,)), dma((n,)), dma((n,)), dma((n,)),
            pltpu.SemaphoreType.REGULAR((2,)),
        ],
        compiler_params=pltpu.CompilerParams(
            collective_id=2, has_side_effects=True, vmem_limit_bytes=107 << 19
        ),
        name="net",
    )(
        volume.reshape(depth, area, chans),
        first_kernel.reshape(3, 9 * chans, chans),
        second_kernel.reshape(3, 9 * chans, mid),
        tap_rows(deep_kernel),
        tap_rows(deeper_kernel),
        rise_kernel.reshape(8, low, mid),
        decode_kernel.reshape(27, block, mid),
        final_kernel.reshape(8, mid, chans),
    ).reshape(volume.shape)


def split_body(
    volume, first_kernel, second_kernel, deep_kernel, deeper_kernel,
    rise_kernel, decode_kernel, final_kernel,
):
    n = lax.axis_size("sp")
    if n != 16 or lax.axis_size("rep") != 2 or decode_kernel.shape[4] % (16 * n):
        return body(
            volume, first_kernel, second_kernel, deep_kernel, deeper_kernel,
            rise_kernel, decode_kernel, final_kernel,
        )
    return net(
        volume, first_kernel, second_kernel, deep_kernel, deeper_kernel,
        rise_kernel, decode_kernel, final_kernel,
    )


def solution(mesh):
    return jax.shard_map(
        split_body,
        mesh=mesh,
        in_specs=(
            P(("rep", "sp"), None, None, None),
            P(),
            P(),
            P(None, None, None, None, "sp"),
            P(None, None, None, None, "sp"),
            P(),
            P(None, None, None, "sp", None),
            P(),
        ),
        out_specs=P(("rep", "sp"), None, None, None),
        check_vma=False,
    )
```

```python
import functools

import jax
import jax.numpy as jnp
from jax import lax
from jax.experimental import pallas as pl
from jax.experimental.pallas import tpu as pltpu
from jax.sharding import PartitionSpec as P

LANES = 128


def remote(src, dst, send_sem, recv_sem, target):
    return pltpu.make_async_remote_copy(
        src_ref=src, dst_ref=dst, send_sem=send_sem, recv_sem=recv_sem,
        device_id={"sp": target}, device_id_type=pl.DeviceIdType.MESH,
    )


def trade_edges(n, first, last, low, high, send_sem, recv_sem):
    me = lax.axis_index("sp")
    upward = remote(last, low, send_sem.at[0], recv_sem.at[0], lax.rem(me + 1, n))
    downward = remote(first, high, send_sem.at[1], recv_sem.at[1], lax.rem(me + n - 1, n))

    @pl.when(me < n - 1)
    def _():
        upward.start()

    @pl.when(me > 0)
    def _():
        downward.start()

    @pl.when(me == 0)
    def _():
        low[...] = jnp.zeros(low.shape, low.dtype)

    @pl.when(me == n - 1)
    def _():
        high[...] = jnp.zeros(high.shape, high.dtype)

    def finish():
        @pl.when(me > 0)
        def _():
            upward.wait_recv()
            downward.wait_send()

        @pl.when(me < n - 1)
        def _():
            downward.wait_recv()
            upward.wait_send()

    return finish


def greet_neighbours(n):
    me = lax.axis_index("sp")
    barrier = pltpu.get_barrier_semaphore()

    @pl.when(me > 0)
    def _():
        pl.semaphore_signal(
            barrier, inc=1, device_id={"sp": lax.rem(me + n - 1, n)},
            device_id_type=pl.DeviceIdType.MESH,
        )

    @pl.when(me < n - 1)
    def _():
        pl.semaphore_signal(
            barrier, inc=1, device_id={"sp": lax.rem(me + 1, n)},
            device_id_type=pl.DeviceIdType.MESH,
        )

    @pl.when((me > 0) & (me < n - 1))
    def _():
        pl.semaphore_wait(barrier, 2)

    @pl.when((me == 0) | (me == n - 1))
    def _():
        pl.semaphore_wait(barrier, 1)


def first_level_kernel(
    n, depth, height, width,
    volume_ref, weight_ref, out_ref,
    ends, taps, sums, send_a, recv_a, send_b, recv_b,
):
    area = height * width
    chans = volume_ref.shape[2]
    greet_neighbours(n)
    finish = trade_edges(
        n, volume_ref.at[0], volume_ref.at[depth - 1], ends.at[0], ends.at[1], send_a, recv_a
    )
    index = lax.broadcasted_iota(jnp.int32, (area, 1), 0) & (width - 1)
    blank = jnp.zeros((depth + 2, width, 3 * chans), jnp.bfloat16)
    taps[:, 0:width] = blank
    taps[:, area + width : area + 2 * width] = blank

    def spread(at, values):
        taps[at, width : area + width, chans : 2 * chans] = values
        values = values.astype(jnp.float32)
        left = jnp.where(index > 0, pltpu.roll(values, 1, 0), 0.0)
        right = jnp.where(index < width - 1, pltpu.roll(values, area - 1, 0), 0.0)
        taps[at, width : area + width, 0:chans] = left.astype(jnp.bfloat16)
        taps[at, width : area + width, 2 * chans : 3 * chans] = right.astype(jnp.bfloat16)

    for d in range(depth):
        spread(d + 1, volume_ref[d])
    finish()
    spread(0, ends[0])
    spread(depth + 1, ends[1])
    for pair in range(depth // 2):
        total = jnp.zeros((2 * area, weight_ref.shape[3]), jnp.float32)
        for a in range(3):
            for b in range(3):
                block = taps[2 * pair + a : 2 * pair + a + 2, b * width : b * width + area]
                total += jnp.dot(
                    block.reshape(2 * area, 3 * chans), weight_ref[a, b],
                    preferred_element_type=jnp.float32,
                )
        total = jnp.maximum(total, 0.0).astype(jnp.bfloat16).astype(jnp.float32)
        total = total[0:area] + total[area : 2 * area]
        total = total.reshape(height // 2, 2, width, total.shape[1]).sum(axis=1)
        sums[...] = total.reshape(area // 2, total.shape[2])
        total = sums[pl.ds(0, area // 4, 2), :] + sums[pl.ds(1, area // 4, 2), :]
        out_ref[1 + pair] = (total * 0.125).astype(jnp.bfloat16)
    halves = depth // 2
    trade_edges(
        n, out_ref.at[1], out_ref.at[halves], out_ref.at[0], out_ref.at[halves + 1],
        send_b, recv_b,
    )()


def first_level(volume, kernel):
    n = lax.axis_size("sp")
    depth, height, width, chans = volume.shape
    outs = kernel.shape[4]
    area = height * width
    vmem = pl.BlockSpec(memory_space=pltpu.VMEM)
    padded = pl.pallas_call(
        functools.partial(first_level_kernel, n, depth, height, width),
        out_shape=jax.ShapeDtypeStruct((depth // 2 + 2, area // 4, outs), jnp.bfloat16),
        in_specs=[vmem] * 2,
        out_specs=vmem,
        scratch_shapes=[
            pltpu.VMEM((2, area, chans), jnp.bfloat16),
            pltpu.VMEM((depth + 2, area + 2 * width, 3 * chans), jnp.bfloat16),
            pltpu.VMEM((area // 2, outs), jnp.float32),
        ]
        + [pltpu.SemaphoreType.DMA((2,))] * 4,
        compiler_params=pltpu.CompilerParams(
            collective_id=1, has_side_effects=True, vmem_limit_bytes=16 << 20
        ),
        name="first_level",
    )(volume.reshape(depth, area, chans), kernel.reshape(3, 3, 3 * chans, outs))
    return padded.reshape(depth // 2 + 2, height // 2, width // 2, outs)


def conv_depth(padded, kernel):
    result = lax.conv_general_dilated(
        padded[None],
        kernel,
        (1, 1, 1),
        ((0, 0), (1, 1), (1, 1)),
        dimension_numbers=("NDHWC", "DHWIO", "NDHWC"),
        preferred_element_type=jnp.float32,
    )
    return result[0]


def pool_mean(values):
    depth, height, width, chans = values.shape
    blocks = values.astype(jnp.float32).reshape(depth // 2, 2, height // 2, 2, width // 2, 2, chans)
    return jnp.mean(blocks, axis=(1, 3, 5)).astype(jnp.bfloat16)


def up_conv(values, kernel):
    depth, height, width, chans = values.shape
    result = jnp.einsum("dhwi,abcio->dahbwco", values, kernel, preferred_element_type=jnp.float32)
    return result.reshape(2 * depth, 2 * height, 2 * width, kernel.shape[4])


def conv_rows(values, weight_ref, height, width):
    rows = values.shape[0]
    index = lax.broadcasted_iota(jnp.int32, (rows, 1), 0)
    w_at = index & (width - 1)
    h_at = (index >> (width.bit_length() - 1)) & (height - 1)
    part, chans = weight_ref.shape[2:]
    blank = jnp.zeros((LANES - 3 * part, chans), weight_ref.dtype)
    total = jnp.zeros((rows, LANES), jnp.float32)
    for b in range(3):
        for c in range(3):
            shift = width * (b - 1) + (c - 1)
            moved = values if shift == 0 else pltpu.roll(values, (-shift) % rows, 0)
            h_to, w_to = h_at + (b - 1), w_at + (c - 1)
            keep = (h_to >= 0) & (h_to < height) & (w_to >= 0) & (w_to < width)
            moved = jnp.where(keep, moved, 0.0).astype(jnp.bfloat16)
            tap = 3 * b + c
            weight = jnp.concatenate([weight_ref[a, tap] for a in range(3)] + [blank], axis=0)
            total += lax.dot_general(
                moved, weight, (((1,), (1,)), ((), ())), preferred_element_type=jnp.float32
            )
    return total


def bottleneck_kernel(
    n, height, width, part,
    pooled_ref, skip_ref, deep_w_ref, deeper_w_ref, out_ref, near_ref,
    whole, deep_mine, deep_all, packed,
    send_a, recv_a, send_b, recv_b, send_c, recv_c, send_d, recv_d,
):
    me = lax.axis_index("sp")
    area = height * width
    voxels = n * area
    partner = me + 1 - 2 * (me % 2)
    half = n // 2

    barrier = pltpu.get_barrier_semaphore()

    def greet(k, carry):
        pl.semaphore_signal(
            barrier, inc=1, device_id={"sp": lax.rem(me + k, n)},
            device_id_type=pl.DeviceIdType.MESH,
        )
        return carry

    lax.fori_loop(1, n, greet, 0)
    pl.semaphore_wait(barrier, n - 1)

    def gather(mine, everyone, send_sem, recv_sem):
        def slot(source):
            return everyone.at[source]

        def direct(k):
            target = lax.rem(me + 2 * k, n)
            return remote(mine, slot(me), send_sem.at[k], recv_sem.at[me], target)

        def relay(k):
            source = lax.rem(me + 2 * (half - k), n)
            return remote(
                slot(source), slot(source), send_sem.at[half + k], recv_sem.at[source], partner
            )

        def arrival(source):
            return remote(mine, slot(source), send_sem.at[0], recv_sem.at[source], partner)

        def start_direct(k, carry):
            direct(k).start()
            return carry

        to_partner = remote(mine, slot(me), send_sem.at[0], recv_sem.at[me], partner)
        lax.fori_loop(1, half, start_direct, 0)
        to_partner.start()
        everyone[me] = mine[...]

        def pass_on(k, carry):
            arrival(lax.rem(me + 2 * (half - k), n)).wait_recv()
            relay(k).start()
            return carry

        lax.fori_loop(1, half, pass_on, 0)

        def from_partner(k, carry):
            arrival(lax.rem(partner + 2 * (half - k), n)).wait_recv()
            return carry

        lax.fori_loop(0, half, from_partner, 0)

        def finish():
            to_partner.wait_send()

            def sent(k, carry):
                direct(k).wait_send()
                relay(k).wait_send()
                return carry

            lax.fori_loop(1, half, sent, 0)

        return finish

    finish_a = gather(pooled_ref, whole, send_a, recv_a)
    depth = skip_ref.shape[0]
    finish_d = trade_edges(
        n, skip_ref.at[0], skip_ref.at[depth - 1], near_ref.at[0], near_ref.at[1], send_d, recv_d
    )
    lanes = lax.broadcasted_iota(jnp.int32, (1, voxels), 1)
    values = whole[...].astype(jnp.float32).reshape(voxels, pooled_ref.shape[1])
    deep = conv_rows(values, deep_w_ref, height, width).T
    below = jnp.where(lanes >= area, pltpu.roll(deep[0:part], area, 1), 0.0)
    above = jnp.where(
        lanes < voxels - area, pltpu.roll(deep[2 * part : 3 * part], voxels - area, 1), 0.0
    )
    deep = below + deep[part : 2 * part] + above
    deep_mine[...] = jnp.maximum(deep, 0.0).astype(jnp.bfloat16)
    finish_b = gather(deep_mine, deep_all, send_b, recv_b)

    values = deep_all[...].astype(jnp.float32).reshape(n * part, voxels).T
    deeper = conv_rows(values, deeper_w_ref, height, width)
    rows = lax.broadcasted_iota(jnp.int32, (voxels, 1), 0)

    def down(block):
        return jnp.where(rows >= area, pltpu.roll(block, area, 0), 0.0)

    def up(block):
        return jnp.where(rows < voxels - area, pltpu.roll(block, voxels - area, 0), 0.0)

    deeper = (
        down(deeper)
        + pltpu.roll(deeper, LANES - part, 1)
        + up(pltpu.roll(deeper, LANES - 2 * part, 1))
    )
    deeper = jnp.maximum(deeper, 0.0)
    lane = lax.broadcasted_iota(jnp.int32, (1, LANES), 1)
    deeper = jnp.where(
        lane < part,
        down(deeper),
        jnp.where(
            lane < 2 * part,
            pltpu.roll(deeper, part, 1),
            up(pltpu.roll(deeper, 2 * part, 1)),
        ),
    )
    packed[...] = deeper.astype(jnp.bfloat16).reshape(n, area, LANES)

    def deal(k):
        target = lax.rem(me + k, n)
        return remote(packed.at[target], out_ref.at[me], send_c.at[k], recv_c.at[me], target)

    def start_deal(k, carry):
        deal(k).start()
        return carry

    lax.fori_loop(1, n, start_deal, 0)
    out_ref[me] = packed[me]

    def receive(k, carry):
        source = lax.rem(me + k, n)
        remote(
            packed.at[source], out_ref.at[source], send_c.at[k], recv_c.at[source], source
        ).wait_recv()
        return carry

    lax.fori_loop(1, n, receive, 0)

    def sent(k, carry):
        deal(k).wait_send()
        return carry

    lax.fori_loop(1, n, sent, 0)
    finish_a()
    finish_b()
    finish_d()


def out_major(kernel):
    chans, part = kernel.shape[3], kernel.shape[4]
    return jnp.transpose(kernel, (0, 1, 2, 4, 3)).reshape(3, 9, part, chans)


def bottleneck(pooled, skip, deep_kernel, deeper_kernel):
    n = lax.axis_size("sp")
    _, height, width, chans = pooled.shape
    part = deep_kernel.shape[4]
    area = height * width
    voxels = n * area
    vmem = pl.BlockSpec(memory_space=pltpu.VMEM)
    received, near = pl.pallas_call(
        functools.partial(bottleneck_kernel, n, height, width, part),
        out_shape=(
            jax.ShapeDtypeStruct((n, area, LANES), jnp.bfloat16),
            jax.ShapeDtypeStruct((2,) + skip.shape[1:], jnp.bfloat16),
        ),
        in_specs=[vmem] * 4,
        out_specs=(vmem, vmem),
        scratch_shapes=[
            pltpu.VMEM((n, area, chans), jnp.bfloat16),
            pltpu.VMEM((part, voxels), jnp.bfloat16),
            pltpu.VMEM((n, part, voxels), jnp.bfloat16),
            pltpu.VMEM((n, area, LANES), jnp.bfloat16),
        ]
        + [pltpu.SemaphoreType.DMA((n,))] * 6
        + [pltpu.SemaphoreType.DMA((2,))] * 2,
        compiler_params=pltpu.CompilerParams(
            collective_id=0, has_side_effects=True, vmem_limit_bytes=24 << 20
        ),
        name="bottleneck",
    )(pooled.reshape(area, chans), skip, out_major(deep_kernel), out_major(deeper_kernel))
    blocks = received[:, :, : 3 * part].reshape(n, area, 3, part)
    return jnp.transpose(blocks, (2, 1, 0, 3)).reshape(3, height, width, n * part), near


def body(
    volume,
    first_kernel,
    second_kernel,
    deep_kernel,
    deeper_kernel,
    rise_kernel,
    decode_kernel,
    final_kernel,
):
    padded_pool = first_level(volume, first_kernel)
    skip = jax.nn.relu(conv_depth(padded_pool, second_kernel)).astype(jnp.bfloat16)
    pooled_two = pool_mean(skip)
    deeper_near, skip_near = bottleneck(pooled_two, skip, deep_kernel, deeper_kernel)
    padded_skip = jnp.concatenate([skip_near[:1], skip, skip_near[1:]], axis=0)
    risen = up_conv(deeper_near, rise_kernel)[1:-1].astype(jnp.bfloat16)
    padded_joined = jnp.concatenate([risen, padded_skip], axis=3)
    whole_decode_kernel = lax.all_gather(decode_kernel, "sp", axis=3, tiled=True)
    decoded = jax.nn.relu(conv_depth(padded_joined, whole_decode_kernel)).astype(jnp.bfloat16)
    return up_conv(decoded, final_kernel).astype(jnp.bfloat16)


def picks(index, columns):
    lane = lax.broadcasted_iota(jnp.int32, (index.shape[0], columns), 1)
    return jnp.where(lane == index, 1.0, 0.0).astype(jnp.bfloat16)


def spread_matrix():
    row = lax.broadcasted_iota(jnp.int32, (36 * 16, 1), 0)
    slab = row >> 4
    eh = (slab * 43) >> 8
    h = ((row >> 2) & 3) * 4 + eh - 1
    w = (row & 3) * 4 + (slab - 6 * eh) - 1
    inside = (h >= 0) & (h < 16) & (w >= 0) & (w < 16)
    return picks(jnp.where(inside, h * 16 + w, -1), 256)


def spread_matrix_two():
    row = lax.broadcasted_iota(jnp.int32, (16 * 16, 1), 0)
    h = ((row >> 2) & 3) * 2 + (row >> 6) - 1
    w = (row & 3) * 2 + ((row >> 4) & 3) - 1
    inside = (h >= 0) & (h < 8) & (w >= 0) & (w < 8)
    at = (h & 1) * 32 + (w & 1) * 16 + (h >> 1) * 4 + (w >> 1)
    return picks(jnp.where(inside, at, -1), 64)


def gather_matrix():
    row = lax.broadcasted_iota(jnp.int32, (256, 1), 0)
    h, w = row >> 4, row & 15
    return picks((h & 3) * 64 + (w & 3) * 16 + (h >> 2) * 4 + (w >> 2), 256)


def block_transpose(pieces, width):
    pieces = list(pieces)
    count = len(pieces)
    block = lax.broadcasted_iota(jnp.int32, pieces[0].shape, 1) // width
    step = 1
    while step < count:
        low = (block & step) == 0
        for i in range(count):
            if i & step:
                continue
            a, b = pieces[i], pieces[i + step]
            pieces[i] = jnp.where(low, a, pltpu.roll(b, width * step, 1))
            pieces[i + step] = jnp.where(low, pltpu.roll(a, 128 - width * step, 1), b)
        step *= 2
    return pieces


def moved(values, by, keep):
    lanes = values.shape[1]
    return jnp.where(keep, pltpu.roll(values, by % lanes, 1), 0.0)


class Lanes:
    def __init__(self, count):
        lane = lax.broadcasted_iota(jnp.int32, (1, count), 1)
        wc, hc, d = lane & 3, (lane >> 2) & 3, lane >> 4
        top = count // 16 - 1
        self.after = {1: wc > 0, 4: hc > 0, 16: d > 0}
        self.before = {1: wc < 3, 4: hc < 3, 16: d < top}

    def back(self, values, by):
        return moved(values, by, self.after[by])

    def ahead(self, values, by):
        return moved(values, -by, self.before[by])


def add_taps(lanes, y, outs):
    def row(a, b, c):
        at = (9 * a + 3 * b + c) * outs
        return y[at : at + outs]

    def tall(c):
        return jnp.concatenate([row(a, b, c) for b in range(3) for a in range(3)], axis=0)

    y = tall(1) + lanes.back(tall(0), 1) + lanes.ahead(tall(2), 1)
    y = [y[i * 3 * outs : (i + 1) * 3 * outs] for i in range(3)]
    y = y[1] + lanes.back(y[0], 4) + lanes.ahead(y[2], 4)
    y = [y[i * outs : (i + 1) * outs] for i in range(3)]
    return y[1] + lanes.back(y[0], 16) + lanes.ahead(y[2], 16)


def add_fine_taps(lanes, load, outs):
    def pair(zero, one, by):
        even = zero[1] + one[2] + lanes.back(one[0], by)
        odd = one[1] + zero[0] + lanes.ahead(zero[2], by)
        return even, odd

    planes = {}
    for pd in range(2):
        rows = {}
        for ph in range(2):
            def taps(pw):
                p = 4 * pd + 2 * ph + pw
                return [
                    jnp.concatenate(
                        [load(p, 9 * a + 3 * b + c) for b in range(3) for a in range(3)], axis=0
                    )
                    for c in range(3)
                ]

            rows[ph] = pair(taps(0), taps(1), 1)
        for qw in range(2):
            def cut(ph):
                return [rows[ph][qw][i * 3 * outs : (i + 1) * 3 * outs] for i in range(3)]

            planes[pd, qw] = pair(cut(0), cut(1), 4)
    result = [None] * 8
    for qw in range(2):
        for qh in range(2):
            def cut(pd):
                return [planes[pd, qw][qh][i * outs : (i + 1) * outs] for i in range(3)]

            low, high = pair(cut(0), cut(1), 16)
            result[2 * qh + qw] = low
            result[4 + 2 * qh + qw] = high
    return result


class Gather:
    def __init__(self, n, slots, send_sem, recv_sem):
        self.n, self.slots, self.send_sem, self.recv_sem = n, slots, send_sem, recv_sem
        self.me = lax.axis_index("sp")
        self.sent = []
        self.others = list(range(n - 2, 0, -2))

    def send(self, source, target):
        slot = self.slots.at[self.me ^ source]
        copy = remote(
            slot, slot, self.send_sem.at[len(self.sent)], self.recv_sem.at[source ^ target],
            self.me ^ target,
        )
        copy.start()
        self.sent.append(copy)

    def wait(self, source):
        slot = self.slots.at[self.me ^ source]
        remote(slot, slot, self.send_sem.at[0], self.recv_sem.at[source], self.me ^ 1).wait_recv()

    def start(self):
        for k in self.others:
            self.send(0, k)
        self.send(0, 1)

    def relay(self):
        for k in reversed(self.others):
            self.wait(k)
            self.send(k, 1)

    def finish(self):
        for k in range(1, self.n, 2):
            self.wait(k)

    def pass_on(self, source, *targets):
        self.wait(source)
        for target in targets:
            self.send(source, target)

    def drain(self):
        for copy in self.sent:
            copy.wait_send()


class Doubling(Gather):
    def steps(self):
        bits = [1 << i for i in range(self.n.bit_length() - 1)]
        known = [[0]]
        for _ in bits:
            known.append([k | bit for k in known[-1] for bit in bits if bit < (k & -k or self.n)])
        return bits, known

    def start(self):
        bits, _ = self.steps()
        for bit in reversed(bits):
            self.send(0, bit)

    def hop(self, step):
        bits, known = self.steps()
        for k in known[step]:
            self.pass_on(k, *[bit for bit in reversed(bits) if bit < (k & -k)])


def net_kernel(
    n,
    volume_hbm, first_hbm, second_hbm, deep_hbm, deeper_hbm, rise_hbm, decode_hbm, final_hbm,
    out_ref,
    vol, vhalo, pp, pp2, order, wpair, w2, wd, wdd, rw, kloc, wf,
    ex, pool, ex2, pooled_all, deep_all, deeper_all, skip_all,
    wsend, wall, wt, ys, dsend, decoded_all,
    load_sem, send_v, recv_v, send_p, recv_p,
    send_a, recv_a, send_b, recv_b, send_c, recv_c, send_s, recv_s,
    send_w, recv_w, send_f, recv_f, send_d, recv_d, ready,
):
    me = lax.axis_index("sp")
    bf = jnp.bfloat16
    f32 = jnp.float32
    depth = vol.shape[0]
    k1 = first_hbm.shape[1]
    part = wd.shape[0] // 27
    outs = 256 // n
    coarse = 16 * n

    loads = []

    def load(src, dst):
        copy = pltpu.make_async_copy(src, dst, load_sem.at[len(loads)])
        copy.start()
        loads.append(copy)
        return copy

    get_vol = load(volume_hbm, vol)
    get_k = load(decode_hbm, kloc)
    get_w1 = [
        load(first_hbm.at[1], wpair.at[0:k1, 0:128]),
        load(first_hbm.at[0], wpair.at[0:k1, 128:256]),
        load(first_hbm.at[2], wpair.at[k1 : 2 * k1, 0:128]),
        load(first_hbm.at[1], wpair.at[k1 : 2 * k1, 128:256]),
    ]
    get_w2 = load(second_hbm, w2)
    get_wd = load(deep_hbm, wd)
    get_wdd = load(deeper_hbm, wdd)
    get_rw = load(rise_hbm, rw)
    chans = final_hbm.shape[2]
    get_wf = [load(final_hbm.at[i], wf.at[:, chans * i : chans * (i + 1)]) for i in range(8)]

    twin = lax.axis_index("rep")
    barrier = pltpu.get_barrier_semaphore()
    plane, columns = (1, 2, 3), (4, 8)

    def say(sem, target):
        pl.semaphore_signal(
            sem, inc=1, device_id={"sp": target}, device_id_type=pl.DeviceIdType.MESH
        )

    corner = ((me % 4 == 0) & (me > 0)) | ((me % 4 == 3) & (me < n - 1))
    beyond = jnp.where(me % 4 == 0, me + n - 1, me + 1) % n
    pl.when(corner)(lambda: say(barrier, beyond))
    for k in columns[::-1] + plane:
        say(barrier, me ^ k)
    pl.semaphore_signal(
        barrier, inc=1, device_id={"rep": 1 - twin, "sp": me},
        device_id_type=pl.DeviceIdType.MESH,
    )

    def meet_near():
        near = len(plane) + len(columns) + 1

        @pl.when(corner)
        def _():
            pl.semaphore_wait(barrier, near + 1)

        @pl.when(jnp.logical_not(corner))
        def _():
            pl.semaphore_wait(barrier, near)

        for k in plane:
            say(ready.at[0], me ^ k)

    def meet_planes():
        pl.semaphore_wait(ready.at[0], len(plane))
        for k in columns:
            say(ready.at[1], me ^ k)

    def meet_all():
        pl.semaphore_wait(ready.at[1], len(columns))

    def spread(planes, to):
        get = jnp.concatenate(planes, axis=1)
        result = jnp.dot(pp[...], get, preferred_element_type=f32).astype(bf)
        for i, at in enumerate(to):
            ex[at] = result[:, 128 * i : 128 * (i + 1)]

    pp[...] = spread_matrix()
    get_vol.wait()
    for d in range(0, depth, 2):
        spread([vol[d], vol[d + 1]], [d + 1, d + 2])

    meet_near()
    finish_v = trade_edges(
        n, vol.at[0], vol.at[depth - 1], vhalo.at[0], vhalo.at[1], send_v, recv_v
    )
    pp2[...] = spread_matrix_two()
    order[...] = gather_matrix()

    get_k.wait()
    per = 128 // outs
    for half in range(256 // 128):
        for group in range(wsend.shape[2] // 128):
            taps = []
            for i in range(per):
                tap = per * group + i
                if tap < 27:
                    taps.append(kloc[tap, :, 128 * half : 128 * (half + 1)].astype(f32))
                else:
                    taps.append(jnp.zeros((kloc.shape[1], 128), f32))
            for j, piece in enumerate(block_transpose(taps, outs)):
                wsend[per * half + j, :, 128 * group : 128 * (group + 1)] = piece.astype(bf)

    w_copies = []

    def w_piece(k):
        return remote(wsend.at[me ^ k], wall.at[me], send_w.at[k], recv_w.at[k], me ^ k)

    def w_arrived(k):
        slot = wall.at[me ^ k]
        remote(slot, slot, send_w.at[k], recv_w.at[k], me ^ 1).wait_recv()

    def w_start(batch):
        for k in [2 * i + twin for i in batch] if batch else [1]:
            copy = w_piece(k)
            copy.start()
            w_copies.append(copy)

    def w_forward():
        for i in range(1, n // 2):
            k = 2 * i + twin
            w_arrived(k)
            slot = wall.at[me ^ k]
            copy = pltpu.make_async_remote_copy(
                src_ref=slot, dst_ref=slot, send_sem=send_f.at[i], recv_sem=recv_f.at[i],
                device_id={"rep": 1 - twin, "sp": me}, device_id_type=pl.DeviceIdType.MESH,
            )
            copy.start()
            w_copies.append(copy)

    def w_finish():
        w_arrived(1)
        for i in range(1, n // 2):
            slot = wall.at[me ^ (2 * i + 1 - twin)]
            pltpu.make_async_remote_copy(
                src_ref=slot, dst_ref=slot, send_sem=send_f.at[i], recv_sem=recv_f.at[i],
                device_id={"rep": 1 - twin, "sp": me}, device_id_type=pl.DeviceIdType.MESH,
            ).wait_recv()

    batches = [[5], [4, 3, 2, 1], [7, 6]]
    w_start([])
    wall[me] = wsend[me]

    def taken(at, b):
        columns = []
        for c in range(3):
            columns.append(
                jnp.concatenate(
                    [ex[at, pl.ds(((b + hm) * 6 + c) * 16, 64), :] for hm in range(4)], axis=0
                )
            )
        return columns

    def rows_of(at):
        return jnp.concatenate(sum([taken(at, b) for b in range(3)], []), axis=1)

    for copy in get_w1:
        copy.wait()

    def both(at):
        left = jnp.concatenate([rows_of(at), rows_of(at + 1)], axis=1)
        return jnp.dot(left, wpair[...], preferred_element_type=f32)

    pairs = [both(1), both(3)]
    own_low = jnp.dot(rows_of(2), wpair[0:k1, 128:256], preferred_element_type=f32)
    own_high = jnp.dot(rows_of(3), wpair[k1 : 2 * k1, 0:128], preferred_element_type=f32)
    def turn_w():
        for at in range(0, wt.shape[1], 128):
            block = wall[pl.ds(at // part, 128 // part)].reshape(128, wall.shape[2])
            wt[:, at : at + 128] = block.astype(f32).T.astype(bf)[0 : wt.shape[0]]

    meet_planes()
    w_start(batches[0])
    finish_v()
    spread([vhalo[0], vhalo[1]], [0, depth + 1])
    far_low = jnp.dot(rows_of(0), wpair[0:k1, 128:256], preferred_element_type=f32)
    far_high = jnp.dot(rows_of(5), wpair[k1 : 2 * k1, 0:128], preferred_element_type=f32)
    planes = [
        pairs[0][:, 0:128] + far_low,
        pairs[0][:, 128:256] + own_high,
        pairs[1][:, 0:128] + own_low,
        pairs[1][:, 128:256] + far_high,
    ]
    planes = [jnp.maximum(t, 0.0).astype(bf).astype(f32) for t in planes]
    for i in range(2):
        total = planes[2 * i] + planes[2 * i + 1]
        for ph in range(2):
            for pw in range(2):
                slabs = [
                    total[((2 * ph + y) * 4 + 2 * pw + x) * 16 :][:16]
                    for y in range(2) for x in range(2)
                ]
                slab = (slabs[0] + slabs[1]) + (slabs[2] + slabs[3])
                pool[1 + i, pl.ds((2 * ph + pw) * 16, 16), :] = (slab * 0.125).astype(bf)

    finish_p = trade_edges(n, pool.at[1], pool.at[2], pool.at[0], pool.at[3], send_p, recv_p)
    w_start(batches[1])
    get_w2.wait()

    def spread_two(at):
        ex2[at] = jnp.dot(pp2[...], pool[at], preferred_element_type=f32).astype(bf)

    def rows_two(at):
        columns = []
        for b in range(3):
            for c in range(3):
                columns.append(
                    jnp.concatenate(
                        [ex2[at, pl.ds(((b + ph) * 4 + c) * 16, 32), :] for ph in range(2)], axis=0
                    )
                )
        return jnp.concatenate(columns, axis=1)

    def taps_two(at, a):
        return jnp.dot(rows_two(at), w2[a], preferred_element_type=f32)

    spread_two(1)
    spread_two(2)
    both_rows = jnp.concatenate([rows_two(1), rows_two(2)], axis=0)
    skip = jnp.dot(both_rows, w2[1], preferred_element_type=f32)
    inner = [taps_two(2, 2), taps_two(1, 0)]
    finish_p()
    spread_two(0)
    spread_two(3)
    outer = [taps_two(0, 0), taps_two(3, 2)]
    skip += jnp.concatenate([x + y for x, y in zip(inner, outer)], axis=0)
    skip = jnp.maximum(skip, 0.0).astype(bf)
    skip_all[me] = skip.reshape(skip_all.shape[1:])
    skip = skip.astype(f32)
    slabs = [skip[16 * i : 16 * (i + 1)] for i in range(8)]
    while len(slabs) > 1:
        slabs = [slabs[i] + slabs[i + 1] for i in range(0, len(slabs), 2)]
    pooled_all[me] = (slabs[0] * 0.125).astype(bf)

    gather_a = Gather(n, pooled_all, send_a, recv_a)
    gather_b = Gather(n, deep_all, send_b, recv_b)
    gather_c = Gather(n, deeper_all, send_c, recv_c)
    gather_s = Doubling(n, skip_all, send_s, recv_s)
    meet_all()
    gather_a.start()
    gather_s.start()
    w_start(batches[2])
    lanes = Lanes(coarse)
    get_wd.wait()
    get_wdd.wait()
    get_rw.wait()
    gather_a.relay()
    gather_a.finish()
    y = lax.dot_general(
        wd[...], pooled_all[...].reshape(coarse, pooled_all.shape[2]),
        (((1,), (1,)), ((), ())), preferred_element_type=f32,
    )
    deep_all[me] = jnp.maximum(add_taps(lanes, y, part), 0.0).astype(bf)
    gather_b.start()
    gather_s.hop(1)
    w_forward()
    gather_b.relay()
    gather_s.hop(2)
    gather_b.finish()
    y = jnp.dot(
        wdd[...], deep_all[...].reshape(n * part, coarse), preferred_element_type=f32
    )
    deeper_all[me] = jnp.maximum(add_taps(lanes, y, part), 0.0).astype(bf)
    gather_c.start()
    w_finish()
    turn_w()
    gather_s.hop(3)
    gather_c.relay()
    gather_s.hop(4)

    def fine(p, values, inner):
        ys[p] = lax.dot_general(
            wt[:, inner], values, (((1,), (1,)), ((), ())), preferred_element_type=f32
        )

    def tap_of(p, tap):
        return ys[p, outs * tap : outs * (tap + 1), :]

    for p in range(8):
        fine(p, skip_all[:, p].reshape(coarse, skip_all.shape[3]), slice(256, 512))
    from_skip = add_fine_taps(lanes, tap_of, outs)
    gather_c.finish()
    deeper = deeper_all[...].reshape(n * part, coarse).astype(f32).T.astype(bf)
    for p in range(8):
        risen = jnp.dot(deeper, rw[p], preferred_element_type=f32).astype(bf)
        fine(p, risen, slice(0, 256))
    from_risen = add_fine_taps(lanes, tap_of, outs)
    decoded = [jnp.maximum(s + r, 0.0) for s, r in zip(from_skip, from_risen)]
    for half in range(coarse // 128):
        cut = [t[:, 128 * half : 128 * (half + 1)] for t in decoded]
        for j, piece in enumerate(block_transpose(cut, 16)):
            dsend[8 * half + j] = piece.astype(bf)
    d_copies = []
    for k in range(n - 1, 0, -1):
        copy = remote(dsend.at[me ^ k], decoded_all.at[me], send_d.at[k], recv_d.at[k], me ^ k)
        copy.start()
        d_copies.append(copy)
    decoded_all[me] = dsend[me]
    for copy in w_copies:
        copy.wait_send()
    for gather in (gather_a, gather_b, gather_c, gather_s):
        gather.drain()
    for copy in d_copies:
        copy.wait_send()
    for copy in get_wf:
        copy.wait()
    for k in range(1, n):
        slot = decoded_all.at[me ^ k]
        remote(slot, slot, send_d.at[k], recv_d.at[k], me ^ 1).wait_recv()
    decoded = decoded_all[...].reshape(n * outs, 128).astype(f32).T.astype(bf)
    fine_rows = jnp.dot(decoded, wf[...], preferred_element_type=f32).astype(bf)

    def slab(d, y, x):
        p = 4 * (d // 2) + 2 * (y // 2) + x // 2
        tap = 4 * (d % 2) + 2 * (y % 2) + x % 2
        return fine_rows[16 * p : 16 * (p + 1), chans * tap : chans * (tap + 1)]

    def slabs_of(d):
        return jnp.concatenate([slab(d, y, x) for y in range(4) for x in range(4)], axis=0)

    for d in range(0, depth, 2):
        plane = jnp.concatenate([slabs_of(d), slabs_of(d + 1)], axis=1)
        plane = jnp.dot(order[...], plane, preferred_element_type=f32).astype(bf)
        out_ref[d] = plane[:, 0:chans]
        out_ref[d + 1] = plane[:, chans : 2 * chans]


def net(
    volume, first_kernel, second_kernel, deep_kernel, deeper_kernel,
    rise_kernel, decode_kernel, final_kernel,
):
    n = lax.axis_size("sp")
    depth, height, width, chans = volume.shape
    mid = second_kernel.shape[4]
    low = rise_kernel.shape[3]
    part = deep_kernel.shape[4]
    block = decode_kernel.shape[3]
    outs = mid // n
    coarse = 16 * n
    area = height * width
    taps = 27 * outs
    wide = -(-taps // LANES) * LANES
    bf = jnp.bfloat16
    vmem = pltpu.VMEM
    dma = pltpu.SemaphoreType.DMA
    hbm = pl.BlockSpec(memory_space=pltpu.HBM)

    def tap_rows(kernel):
        return jnp.transpose(kernel, (0, 1, 2, 4, 3)).reshape(27 * part, kernel.shape[3])

    return pl.pallas_call(
        functools.partial(net_kernel, n),
        out_shape=jax.ShapeDtypeStruct((depth, area, chans), bf),
        in_specs=[hbm] * 8,
        out_specs=pl.BlockSpec(memory_space=pltpu.VMEM),
        scratch_shapes=[
            vmem((depth, area, chans), bf),
            vmem((2, area, chans), bf),
            vmem((36 * 16, area), bf),
            vmem((16 * 16, area // 4), bf),
            vmem((area, area), bf),
            vmem((18 * chans, 2 * chans), bf),
            vmem((3, 9 * chans, mid), bf),
            vmem((27 * part, mid), bf),
            vmem((27 * part, low), bf),
            vmem((8, low, mid), bf),
            vmem((27, block, mid), bf),
            vmem((mid, 8 * chans), bf),
            vmem((depth + 2, 36 * 16, chans), bf),
            vmem((depth // 2 + 2, area // 4, chans), bf),
            vmem((depth // 2 + 2, 16 * 16, chans), bf),
            vmem((n, 16, mid), bf),
            vmem((n, part, coarse), bf),
            vmem((n, part, coarse), bf),
            vmem((n, 8, 16, mid), bf),
            vmem((n, block, wide), bf),
            vmem((n, block, wide), bf),
            vmem((taps, 2 * mid), bf),
            vmem((8, taps, coarse), jnp.float32),
            vmem((n, outs, 128), bf),
            vmem((n, outs, 128), bf),
            dma((24,)),
            dma((2,)), dma((2,)), dma((2,)), dma((2,)),
            dma((2 * n,)), dma((n,)), dma((2 * n,)), dma((n,)),
            dma((2 * n,)), dma((n,)), dma((2 * n,)), dma((n,)),
            dma((n,)), dma((n,)), dma((n,)), dma((n,)), dma((n,)), dma((n,)),
            pltpu.SemaphoreType.REGULAR((2,)),
        ],
        compiler_params=pltpu.CompilerParams(
            collective_id=2, has_side_effects=True, vmem_limit_bytes=107 << 19
        ),
        name="net",
    )(
        volume.reshape(depth, area, chans),
        first_kernel.reshape(3, 9 * chans, chans),
        second_kernel.reshape(3, 9 * chans, mid),
        tap_rows(deep_kernel),
        tap_rows(deeper_kernel),
        rise_kernel.reshape(8, low, mid),
        decode_kernel.reshape(27, block, mid),
        final_kernel.reshape(8, mid, chans),
    ).reshape(volume.shape)


def split_body(
    volume, first_kernel, second_kernel, deep_kernel, deeper_kernel,
    rise_kernel, decode_kernel, final_kernel,
):
    n = lax.axis_size("sp")
    if n != 16 or lax.axis_size("rep") != 2 or decode_kernel.shape[4] % (16 * n):
        return body(
            volume, first_kernel, second_kernel, deep_kernel, deeper_kernel,
            rise_kernel, decode_kernel, final_kernel,
        )
    return net(
        volume, first_kernel, second_kernel, deep_kernel, deeper_kernel,
        rise_kernel, decode_kernel, final_kernel,
    )


def solution(mesh):
    return jax.shard_map(
        split_body,
        mesh=mesh,
        in_specs=(
            P(("rep", "sp"), None, None, None),
            P(),
            P(),
            P(None, None, None, None, "sp"),
            P(None, None, None, None, "sp"),
            P(),
            P(None, None, None, "sp", None),
            P(),
        ),
        out_specs=P(("rep", "sp"), None, None, None),
        check_vma=False,
    )
```

```python
import functools

import jax
import jax.numpy as jnp
from jax import lax
from jax.experimental import pallas as pl
from jax.experimental.pallas import tpu as pltpu
from jax.sharding import PartitionSpec as P

LANES = 128


def remote(src, dst, send_sem, recv_sem, target):
    return pltpu.make_async_remote_copy(
        src_ref=src, dst_ref=dst, send_sem=send_sem, recv_sem=recv_sem,
        device_id={"sp": target}, device_id_type=pl.DeviceIdType.MESH,
    )


def trade_edges(n, first, last, low, high, send_sem, recv_sem):
    me = lax.axis_index("sp")
    upward = remote(last, low, send_sem.at[0], recv_sem.at[0], lax.rem(me + 1, n))
    downward = remote(first, high, send_sem.at[1], recv_sem.at[1], lax.rem(me + n - 1, n))

    @pl.when(me < n - 1)
    def _():
        upward.start()

    @pl.when(me > 0)
    def _():
        downward.start()

    @pl.when(me == 0)
    def _():
        low[...] = jnp.zeros(low.shape, low.dtype)

    @pl.when(me == n - 1)
    def _():
        high[...] = jnp.zeros(high.shape, high.dtype)

    def finish():
        @pl.when(me > 0)
        def _():
            upward.wait_recv()
            downward.wait_send()

        @pl.when(me < n - 1)
        def _():
            downward.wait_recv()
            upward.wait_send()

    return finish


def greet_neighbours(n):
    me = lax.axis_index("sp")
    barrier = pltpu.get_barrier_semaphore()

    @pl.when(me > 0)
    def _():
        pl.semaphore_signal(
            barrier, inc=1, device_id={"sp": lax.rem(me + n - 1, n)},
            device_id_type=pl.DeviceIdType.MESH,
        )

    @pl.when(me < n - 1)
    def _():
        pl.semaphore_signal(
            barrier, inc=1, device_id={"sp": lax.rem(me + 1, n)},
            device_id_type=pl.DeviceIdType.MESH,
        )

    @pl.when((me > 0) & (me < n - 1))
    def _():
        pl.semaphore_wait(barrier, 2)

    @pl.when((me == 0) | (me == n - 1))
    def _():
        pl.semaphore_wait(barrier, 1)


def first_level_kernel(
    n, depth, height, width,
    volume_ref, weight_ref, out_ref,
    ends, taps, sums, send_a, recv_a, send_b, recv_b,
):
    area = height * width
    chans = volume_ref.shape[2]
    greet_neighbours(n)
    finish = trade_edges(
        n, volume_ref.at[0], volume_ref.at[depth - 1], ends.at[0], ends.at[1], send_a, recv_a
    )
    index = lax.broadcasted_iota(jnp.int32, (area, 1), 0) & (width - 1)
    blank = jnp.zeros((depth + 2, width, 3 * chans), jnp.bfloat16)
    taps[:, 0:width] = blank
    taps[:, area + width : area + 2 * width] = blank

    def spread(at, values):
        taps[at, width : area + width, chans : 2 * chans] = values
        values = values.astype(jnp.float32)
        left = jnp.where(index > 0, pltpu.roll(values, 1, 0), 0.0)
        right = jnp.where(index < width - 1, pltpu.roll(values, area - 1, 0), 0.0)
        taps[at, width : area + width, 0:chans] = left.astype(jnp.bfloat16)
        taps[at, width : area + width, 2 * chans : 3 * chans] = right.astype(jnp.bfloat16)

    for d in range(depth):
        spread(d + 1, volume_ref[d])
    finish()
    spread(0, ends[0])
    spread(depth + 1, ends[1])
    for pair in range(depth // 2):
        total = jnp.zeros((2 * area, weight_ref.shape[3]), jnp.float32)
        for a in range(3):
            for b in range(3):
                block = taps[2 * pair + a : 2 * pair + a + 2, b * width : b * width + area]
                total += jnp.dot(
                    block.reshape(2 * area, 3 * chans), weight_ref[a, b],
                    preferred_element_type=jnp.float32,
                )
        total = jnp.maximum(total, 0.0).astype(jnp.bfloat16).astype(jnp.float32)
        total = total[0:area] + total[area : 2 * area]
        total = total.reshape(height // 2, 2, width, total.shape[1]).sum(axis=1)
        sums[...] = total.reshape(area // 2, total.shape[2])
        total = sums[pl.ds(0, area // 4, 2), :] + sums[pl.ds(1, area // 4, 2), :]
        out_ref[1 + pair] = (total * 0.125).astype(jnp.bfloat16)
    halves = depth // 2
    trade_edges(
        n, out_ref.at[1], out_ref.at[halves], out_ref.at[0], out_ref.at[halves + 1],
        send_b, recv_b,
    )()


def first_level(volume, kernel):
    n = lax.axis_size("sp")
    depth, height, width, chans = volume.shape
    outs = kernel.shape[4]
    area = height * width
    vmem = pl.BlockSpec(memory_space=pltpu.VMEM)
    padded = pl.pallas_call(
        functools.partial(first_level_kernel, n, depth, height, width),
        out_shape=jax.ShapeDtypeStruct((depth // 2 + 2, area // 4, outs), jnp.bfloat16),
        in_specs=[vmem] * 2,
        out_specs=vmem,
        scratch_shapes=[
            pltpu.VMEM((2, area, chans), jnp.bfloat16),
            pltpu.VMEM((depth + 2, area + 2 * width, 3 * chans), jnp.bfloat16),
            pltpu.VMEM((area // 2, outs), jnp.float32),
        ]
        + [pltpu.SemaphoreType.DMA((2,))] * 4,
        compiler_params=pltpu.CompilerParams(
            collective_id=1, has_side_effects=True, vmem_limit_bytes=16 << 20
        ),
        name="first_level",
    )(volume.reshape(depth, area, chans), kernel.reshape(3, 3, 3 * chans, outs))
    return padded.reshape(depth // 2 + 2, height // 2, width // 2, outs)


def conv_depth(padded, kernel):
    result = lax.conv_general_dilated(
        padded[None],
        kernel,
        (1, 1, 1),
        ((0, 0), (1, 1), (1, 1)),
        dimension_numbers=("NDHWC", "DHWIO", "NDHWC"),
        preferred_element_type=jnp.float32,
    )
    return result[0]


def pool_mean(values):
    depth, height, width, chans = values.shape
    blocks = values.astype(jnp.float32).reshape(depth // 2, 2, height // 2, 2, width // 2, 2, chans)
    return jnp.mean(blocks, axis=(1, 3, 5)).astype(jnp.bfloat16)


def up_conv(values, kernel):
    depth, height, width, chans = values.shape
    result = jnp.einsum("dhwi,abcio->dahbwco", values, kernel, preferred_element_type=jnp.float32)
    return result.reshape(2 * depth, 2 * height, 2 * width, kernel.shape[4])


def conv_rows(values, weight_ref, height, width):
    rows = values.shape[0]
    index = lax.broadcasted_iota(jnp.int32, (rows, 1), 0)
    w_at = index & (width - 1)
    h_at = (index >> (width.bit_length() - 1)) & (height - 1)
    part, chans = weight_ref.shape[2:]
    blank = jnp.zeros((LANES - 3 * part, chans), weight_ref.dtype)
    total = jnp.zeros((rows, LANES), jnp.float32)
    for b in range(3):
        for c in range(3):
            shift = width * (b - 1) + (c - 1)
            moved = values if shift == 0 else pltpu.roll(values, (-shift) % rows, 0)
            h_to, w_to = h_at + (b - 1), w_at + (c - 1)
            keep = (h_to >= 0) & (h_to < height) & (w_to >= 0) & (w_to < width)
            moved = jnp.where(keep, moved, 0.0).astype(jnp.bfloat16)
            tap = 3 * b + c
            weight = jnp.concatenate([weight_ref[a, tap] for a in range(3)] + [blank], axis=0)
            total += lax.dot_general(
                moved, weight, (((1,), (1,)), ((), ())), preferred_element_type=jnp.float32
            )
    return total


def bottleneck_kernel(
    n, height, width, part,
    pooled_ref, skip_ref, deep_w_ref, deeper_w_ref, out_ref, near_ref,
    whole, deep_mine, deep_all, packed,
    send_a, recv_a, send_b, recv_b, send_c, recv_c, send_d, recv_d,
):
    me = lax.axis_index("sp")
    area = height * width
    voxels = n * area
    partner = me + 1 - 2 * (me % 2)
    half = n // 2

    barrier = pltpu.get_barrier_semaphore()

    def greet(k, carry):
        pl.semaphore_signal(
            barrier, inc=1, device_id={"sp": lax.rem(me + k, n)},
            device_id_type=pl.DeviceIdType.MESH,
        )
        return carry

    lax.fori_loop(1, n, greet, 0)
    pl.semaphore_wait(barrier, n - 1)

    def gather(mine, everyone, send_sem, recv_sem):
        def slot(source):
            return everyone.at[source]

        def direct(k):
            target = lax.rem(me + 2 * k, n)
            return remote(mine, slot(me), send_sem.at[k], recv_sem.at[me], target)

        def relay(k):
            source = lax.rem(me + 2 * (half - k), n)
            return remote(
                slot(source), slot(source), send_sem.at[half + k], recv_sem.at[source], partner
            )

        def arrival(source):
            return remote(mine, slot(source), send_sem.at[0], recv_sem.at[source], partner)

        def start_direct(k, carry):
            direct(k).start()
            return carry

        to_partner = remote(mine, slot(me), send_sem.at[0], recv_sem.at[me], partner)
        lax.fori_loop(1, half, start_direct, 0)
        to_partner.start()
        everyone[me] = mine[...]

        def pass_on(k, carry):
            arrival(lax.rem(me + 2 * (half - k), n)).wait_recv()
            relay(k).start()
            return carry

        lax.fori_loop(1, half, pass_on, 0)

        def from_partner(k, carry):
            arrival(lax.rem(partner + 2 * (half - k), n)).wait_recv()
            return carry

        lax.fori_loop(0, half, from_partner, 0)

        def finish():
            to_partner.wait_send()

            def sent(k, carry):
                direct(k).wait_send()
                relay(k).wait_send()
                return carry

            lax.fori_loop(1, half, sent, 0)

        return finish

    finish_a = gather(pooled_ref, whole, send_a, recv_a)
    depth = skip_ref.shape[0]
    finish_d = trade_edges(
        n, skip_ref.at[0], skip_ref.at[depth - 1], near_ref.at[0], near_ref.at[1], send_d, recv_d
    )
    lanes = lax.broadcasted_iota(jnp.int32, (1, voxels), 1)
    values = whole[...].astype(jnp.float32).reshape(voxels, pooled_ref.shape[1])
    deep = conv_rows(values, deep_w_ref, height, width).T
    below = jnp.where(lanes >= area, pltpu.roll(deep[0:part], area, 1), 0.0)
    above = jnp.where(
        lanes < voxels - area, pltpu.roll(deep[2 * part : 3 * part], voxels - area, 1), 0.0
    )
    deep = below + deep[part : 2 * part] + above
    deep_mine[...] = jnp.maximum(deep, 0.0).astype(jnp.bfloat16)
    finish_b = gather(deep_mine, deep_all, send_b, recv_b)

    values = deep_all[...].astype(jnp.float32).reshape(n * part, voxels).T
    deeper = conv_rows(values, deeper_w_ref, height, width)
    rows = lax.broadcasted_iota(jnp.int32, (voxels, 1), 0)

    def down(block):
        return jnp.where(rows >= area, pltpu.roll(block, area, 0), 0.0)

    def up(block):
        return jnp.where(rows < voxels - area, pltpu.roll(block, voxels - area, 0), 0.0)

    deeper = (
        down(deeper)
        + pltpu.roll(deeper, LANES - part, 1)
        + up(pltpu.roll(deeper, LANES - 2 * part, 1))
    )
    deeper = jnp.maximum(deeper, 0.0)
    lane = lax.broadcasted_iota(jnp.int32, (1, LANES), 1)
    deeper = jnp.where(
        lane < part,
        down(deeper),
        jnp.where(
            lane < 2 * part,
            pltpu.roll(deeper, part, 1),
            up(pltpu.roll(deeper, 2 * part, 1)),
        ),
    )
    packed[...] = deeper.astype(jnp.bfloat16).reshape(n, area, LANES)

    def deal(k):
        target = lax.rem(me + k, n)
        return remote(packed.at[target], out_ref.at[me], send_c.at[k], recv_c.at[me], target)

    def start_deal(k, carry):
        deal(k).start()
        return carry

    lax.fori_loop(1, n, start_deal, 0)
    out_ref[me] = packed[me]

    def receive(k, carry):
        source = lax.rem(me + k, n)
        remote(
            packed.at[source], out_ref.at[source], send_c.at[k], recv_c.at[source], source
        ).wait_recv()
        return carry

    lax.fori_loop(1, n, receive, 0)

    def sent(k, carry):
        deal(k).wait_send()
        return carry

    lax.fori_loop(1, n, sent, 0)
    finish_a()
    finish_b()
    finish_d()


def out_major(kernel):
    chans, part = kernel.shape[3], kernel.shape[4]
    return jnp.transpose(kernel, (0, 1, 2, 4, 3)).reshape(3, 9, part, chans)


def bottleneck(pooled, skip, deep_kernel, deeper_kernel):
    n = lax.axis_size("sp")
    _, height, width, chans = pooled.shape
    part = deep_kernel.shape[4]
    area = height * width
    voxels = n * area
    vmem = pl.BlockSpec(memory_space=pltpu.VMEM)
    received, near = pl.pallas_call(
        functools.partial(bottleneck_kernel, n, height, width, part),
        out_shape=(
            jax.ShapeDtypeStruct((n, area, LANES), jnp.bfloat16),
            jax.ShapeDtypeStruct((2,) + skip.shape[1:], jnp.bfloat16),
        ),
        in_specs=[vmem] * 4,
        out_specs=(vmem, vmem),
        scratch_shapes=[
            pltpu.VMEM((n, area, chans), jnp.bfloat16),
            pltpu.VMEM((part, voxels), jnp.bfloat16),
            pltpu.VMEM((n, part, voxels), jnp.bfloat16),
            pltpu.VMEM((n, area, LANES), jnp.bfloat16),
        ]
        + [pltpu.SemaphoreType.DMA((n,))] * 6
        + [pltpu.SemaphoreType.DMA((2,))] * 2,
        compiler_params=pltpu.CompilerParams(
            collective_id=0, has_side_effects=True, vmem_limit_bytes=24 << 20
        ),
        name="bottleneck",
    )(pooled.reshape(area, chans), skip, out_major(deep_kernel), out_major(deeper_kernel))
    blocks = received[:, :, : 3 * part].reshape(n, area, 3, part)
    return jnp.transpose(blocks, (2, 1, 0, 3)).reshape(3, height, width, n * part), near


def body(
    volume,
    first_kernel,
    second_kernel,
    deep_kernel,
    deeper_kernel,
    rise_kernel,
    decode_kernel,
    final_kernel,
):
    padded_pool = first_level(volume, first_kernel)
    skip = jax.nn.relu(conv_depth(padded_pool, second_kernel)).astype(jnp.bfloat16)
    pooled_two = pool_mean(skip)
    deeper_near, skip_near = bottleneck(pooled_two, skip, deep_kernel, deeper_kernel)
    padded_skip = jnp.concatenate([skip_near[:1], skip, skip_near[1:]], axis=0)
    risen = up_conv(deeper_near, rise_kernel)[1:-1].astype(jnp.bfloat16)
    padded_joined = jnp.concatenate([risen, padded_skip], axis=3)
    whole_decode_kernel = lax.all_gather(decode_kernel, "sp", axis=3, tiled=True)
    decoded = jax.nn.relu(conv_depth(padded_joined, whole_decode_kernel)).astype(jnp.bfloat16)
    return up_conv(decoded, final_kernel).astype(jnp.bfloat16)


def picks(index, columns):
    lane = lax.broadcasted_iota(jnp.int32, (index.shape[0], columns), 1)
    return jnp.where(lane == index, 1.0, 0.0).astype(jnp.bfloat16)


def spread_matrix():
    row = lax.broadcasted_iota(jnp.int32, (36 * 16, 1), 0)
    slab = row >> 4
    eh = (slab * 43) >> 8
    h = ((row >> 2) & 3) * 4 + eh - 1
    w = (row & 3) * 4 + (slab - 6 * eh) - 1
    inside = (h >= 0) & (h < 16) & (w >= 0) & (w < 16)
    return picks(jnp.where(inside, h * 16 + w, -1), 256)


def spread_matrix_two():
    row = lax.broadcasted_iota(jnp.int32, (16 * 16, 1), 0)
    h = ((row >> 2) & 3) * 2 + (row >> 6) - 1
    w = (row & 3) * 2 + ((row >> 4) & 3) - 1
    inside = (h >= 0) & (h < 8) & (w >= 0) & (w < 8)
    at = (h & 1) * 32 + (w & 1) * 16 + (h >> 1) * 4 + (w >> 1)
    return picks(jnp.where(inside, at, -1), 64)


def gather_matrix():
    row = lax.broadcasted_iota(jnp.int32, (256, 1), 0)
    h, w = row >> 4, row & 15
    return picks((h & 3) * 64 + (w & 3) * 16 + (h >> 2) * 4 + (w >> 2), 256)


def block_transpose(pieces, width):
    pieces = list(pieces)
    count = len(pieces)
    block = lax.broadcasted_iota(jnp.int32, pieces[0].shape, 1) // width
    step = 1
    while step < count:
        low = (block & step) == 0
        for i in range(count):
            if i & step:
                continue
            a, b = pieces[i], pieces[i + step]
            pieces[i] = jnp.where(low, a, pltpu.roll(b, width * step, 1))
            pieces[i + step] = jnp.where(low, pltpu.roll(a, 128 - width * step, 1), b)
        step *= 2
    return pieces


def moved(values, by, keep):
    lanes = values.shape[1]
    return jnp.where(keep, pltpu.roll(values, by % lanes, 1), 0.0)


class Lanes:
    def __init__(self, count):
        lane = lax.broadcasted_iota(jnp.int32, (1, count), 1)
        wc, hc, d = lane & 3, (lane >> 2) & 3, lane >> 4
        top = count // 16 - 1
        self.after = {1: wc > 0, 4: hc > 0, 16: d > 0}
        self.before = {1: wc < 3, 4: hc < 3, 16: d < top}

    def back(self, values, by):
        return moved(values, by, self.after[by])

    def ahead(self, values, by):
        return moved(values, -by, self.before[by])


def add_taps(lanes, y, outs):
    def row(a, b, c):
        at = (9 * a + 3 * b + c) * outs
        return y[at : at + outs]

    def tall(c):
        return jnp.concatenate([row(a, b, c) for b in range(3) for a in range(3)], axis=0)

    y = tall(1) + lanes.back(tall(0), 1) + lanes.ahead(tall(2), 1)
    y = [y[i * 3 * outs : (i + 1) * 3 * outs] for i in range(3)]
    y = y[1] + lanes.back(y[0], 4) + lanes.ahead(y[2], 4)
    y = [y[i * outs : (i + 1) * outs] for i in range(3)]
    return y[1] + lanes.back(y[0], 16) + lanes.ahead(y[2], 16)


def add_fine_taps(lanes, load, outs):
    def pair(zero, one, by):
        even = zero[1] + one[2] + lanes.back(one[0], by)
        odd = one[1] + zero[0] + lanes.ahead(zero[2], by)
        return even, odd

    planes = {}
    for pd in range(2):
        rows = {}
        for ph in range(2):
            def taps(pw):
                p = 4 * pd + 2 * ph + pw
                return [
                    jnp.concatenate(
                        [load(p, 9 * a + 3 * b + c) for b in range(3) for a in range(3)], axis=0
                    )
                    for c in range(3)
                ]

            rows[ph] = pair(taps(0), taps(1), 1)
        for qw in range(2):
            def cut(ph):
                return [rows[ph][qw][i * 3 * outs : (i + 1) * 3 * outs] for i in range(3)]

            planes[pd, qw] = pair(cut(0), cut(1), 4)
    result = [None] * 8
    for qw in range(2):
        for qh in range(2):
            def cut(pd):
                return [planes[pd, qw][qh][i * outs : (i + 1) * outs] for i in range(3)]

            low, high = pair(cut(0), cut(1), 16)
            result[2 * qh + qw] = low
            result[4 + 2 * qh + qw] = high
    return result


class Gather:
    def __init__(self, n, slots, send_sem, recv_sem):
        self.n, self.slots, self.send_sem, self.recv_sem = n, slots, send_sem, recv_sem
        self.me = lax.axis_index("sp")
        self.sent = []
        self.others = list(range(n - 2, 0, -2))

    def send(self, source, target):
        slot = self.slots.at[self.me ^ source]
        copy = remote(
            slot, slot, self.send_sem.at[len(self.sent)], self.recv_sem.at[source ^ target],
            self.me ^ target,
        )
        copy.start()
        self.sent.append(copy)

    def wait(self, source):
        slot = self.slots.at[self.me ^ source]
        remote(slot, slot, self.send_sem.at[0], self.recv_sem.at[source], self.me ^ 1).wait_recv()

    def start(self):
        for k in self.others:
            self.send(0, k)
        self.send(0, 1)

    def relay(self):
        for k in reversed(self.others):
            self.wait(k)
            self.send(k, 1)

    def finish(self):
        for k in range(1, self.n, 2):
            self.wait(k)

    def pass_on(self, source, *targets):
        self.wait(source)
        for target in targets:
            self.send(source, target)

    def drain(self):
        for copy in self.sent:
            copy.wait_send()


class Doubling(Gather):
    def steps(self):
        bits = [1 << i for i in range(self.n.bit_length() - 1)]
        known = [[0]]
        for _ in bits:
            known.append([k | bit for k in known[-1] for bit in bits if bit < (k & -k or self.n)])
        return bits, known

    def start(self):
        bits, _ = self.steps()
        for bit in reversed(bits):
            self.send(0, bit)

    def hop(self, step):
        bits, known = self.steps()
        for k in known[step]:
            self.pass_on(k, *[bit for bit in reversed(bits) if bit < (k & -k)])


def net_kernel(
    n,
    volume_hbm, first_hbm, second_hbm, deep_hbm, deeper_hbm, rise_hbm, decode_hbm, final_hbm,
    out_ref,
    vol, vhalo, pp, pp2, order, wpair, w2, wd, wdd, rw, kloc, wf,
    ex, pool, ex2, pooled_all, deep_all, deeper_all, skip_all,
    wsend, wall, wt, ys, dsend, decoded_all,
    load_sem, send_v, recv_v, send_p, recv_p,
    send_a, recv_a, send_b, recv_b, send_c, recv_c, send_s, recv_s,
    send_w, recv_w, send_f, recv_f, send_d, recv_d, ready,
):
    me = lax.axis_index("sp")
    bf = jnp.bfloat16
    f32 = jnp.float32
    depth = vol.shape[0]
    k1 = first_hbm.shape[1]
    part = wd.shape[0] // 27
    outs = 256 // n
    coarse = 16 * n

    twin = lax.axis_index("rep")
    barrier = pltpu.get_barrier_semaphore()
    plane, columns = (1, 2, 3), (4, 8)

    def say(sem, target):
        pl.semaphore_signal(
            sem, inc=1, device_id={"sp": target}, device_id_type=pl.DeviceIdType.MESH
        )

    corner = ((me % 4 == 0) & (me > 0)) | ((me % 4 == 3) & (me < n - 1))
    beyond = jnp.where(me % 4 == 0, me + n - 1, me + 1) % n
    pl.when(corner)(lambda: say(barrier, beyond))
    for k in columns[::-1] + plane:
        say(barrier, me ^ k)
    pl.semaphore_signal(
        barrier, inc=1, device_id={"rep": 1 - twin, "sp": me},
        device_id_type=pl.DeviceIdType.MESH,
    )

    def meet_near():
        near = len(plane) + len(columns) + 1

        @pl.when(corner)
        def _():
            pl.semaphore_wait(barrier, near + 1)

        @pl.when(jnp.logical_not(corner))
        def _():
            pl.semaphore_wait(barrier, near)

        for k in plane:
            say(ready.at[0], me ^ k)

    def meet_planes():
        pl.semaphore_wait(ready.at[0], len(plane))
        for k in columns:
            say(ready.at[1], me ^ k)

    def meet_all():
        pl.semaphore_wait(ready.at[1], len(columns))

    loads = []

    def load(src, dst):
        copy = pltpu.make_async_copy(src, dst, load_sem.at[len(loads)])
        copy.start()
        loads.append(copy)
        return copy

    get_vol = load(volume_hbm, vol)
    get_k = load(decode_hbm, kloc)
    get_w1 = [
        load(first_hbm.at[1], wpair.at[0:k1, 0:128]),
        load(first_hbm.at[0], wpair.at[0:k1, 128:256]),
        load(first_hbm.at[2], wpair.at[k1 : 2 * k1, 0:128]),
        load(first_hbm.at[1], wpair.at[k1 : 2 * k1, 128:256]),
    ]
    get_w2 = load(second_hbm, w2)
    get_wd = load(deep_hbm, wd)
    get_wdd = load(deeper_hbm, wdd)
    get_rw = load(rise_hbm, rw)
    chans = final_hbm.shape[2]
    get_wf = [load(final_hbm.at[i], wf.at[:, chans * i : chans * (i + 1)]) for i in range(8)]

    def spread(planes, to):
        get = jnp.concatenate(planes, axis=1)
        result = jnp.dot(pp[...], get, preferred_element_type=f32).astype(bf)
        for i, at in enumerate(to):
            ex[at] = result[:, 128 * i : 128 * (i + 1)]

    pp[...] = spread_matrix()
    get_vol.wait()
    for d in range(0, depth, 2):
        spread([vol[d], vol[d + 1]], [d + 1, d + 2])

    meet_near()
    finish_v = trade_edges(
        n, vol.at[0], vol.at[depth - 1], vhalo.at[0], vhalo.at[1], send_v, recv_v
    )
    pp2[...] = spread_matrix_two()
    order[...] = gather_matrix()

    get_k.wait()
    per = 128 // outs
    for half in range(256 // 128):
        for group in range(wsend.shape[2] // 128):
            taps = []
            for i in range(per):
                tap = per * group + i
                if tap < 27:
                    taps.append(kloc[tap, :, 128 * half : 128 * (half + 1)].astype(f32))
                else:
                    taps.append(jnp.zeros((kloc.shape[1], 128), f32))
            for j, piece in enumerate(block_transpose(taps, outs)):
                wsend[per * half + j, :, 128 * group : 128 * (group + 1)] = piece.astype(bf)

    w_copies = []

    def w_piece(k):
        return remote(wsend.at[me ^ k], wall.at[me], send_w.at[k], recv_w.at[k], me ^ k)

    def w_arrived(k):
        slot = wall.at[me ^ k]
        remote(slot, slot, send_w.at[k], recv_w.at[k], me ^ 1).wait_recv()

    def w_start(batch):
        for k in [2 * i + twin for i in batch] if batch else [1]:
            copy = w_piece(k)
            copy.start()
            w_copies.append(copy)

    def w_forward():
        for i in range(1, n // 2):
            k = 2 * i + twin
            w_arrived(k)
            slot = wall.at[me ^ k]
            copy = pltpu.make_async_remote_copy(
                src_ref=slot, dst_ref=slot, send_sem=send_f.at[i], recv_sem=recv_f.at[i],
                device_id={"rep": 1 - twin, "sp": me}, device_id_type=pl.DeviceIdType.MESH,
            )
            copy.start()
            w_copies.append(copy)

    def w_finish():
        w_arrived(1)
        for i in range(1, n // 2):
            slot = wall.at[me ^ (2 * i + 1 - twin)]
            pltpu.make_async_remote_copy(
                src_ref=slot, dst_ref=slot, send_sem=send_f.at[i], recv_sem=recv_f.at[i],
                device_id={"rep": 1 - twin, "sp": me}, device_id_type=pl.DeviceIdType.MESH,
            ).wait_recv()

    batches = [[5], [4, 3, 2, 1], [7, 6]]
    w_start([])
    wall[me] = wsend[me]

    def taken(at, b):
        columns = []
        for c in range(3):
            columns.append(
                jnp.concatenate(
                    [ex[at, pl.ds(((b + hm) * 6 + c) * 16, 64), :] for hm in range(4)], axis=0
                )
            )
        return columns

    def rows_of(at):
        return jnp.concatenate(sum([taken(at, b) for b in range(3)], []), axis=1)

    for copy in get_w1:
        copy.wait()

    def both(at):
        left = jnp.concatenate([rows_of(at), rows_of(at + 1)], axis=1)
        return jnp.dot(left, wpair[...], preferred_element_type=f32)

    pairs = [both(1), both(3)]
    own_low = jnp.dot(rows_of(2), wpair[0:k1, 128:256], preferred_element_type=f32)
    own_high = jnp.dot(rows_of(3), wpair[k1 : 2 * k1, 0:128], preferred_element_type=f32)
    def turn_w():
        for at in range(0, wt.shape[1], 128):
            block = wall[pl.ds(at // part, 128 // part)].reshape(128, wall.shape[2])
            wt[:, at : at + 128] = block.astype(f32).T.astype(bf)[0 : wt.shape[0]]

    meet_planes()
    w_start(batches[0])
    finish_v()
    spread([vhalo[0], vhalo[1]], [0, depth + 1])
    far_low = jnp.dot(rows_of(0), wpair[0:k1, 128:256], preferred_element_type=f32)
    far_high = jnp.dot(rows_of(5), wpair[k1 : 2 * k1, 0:128], preferred_element_type=f32)
    planes = [
        pairs[0][:, 0:128] + far_low,
        pairs[0][:, 128:256] + own_high,
        pairs[1][:, 0:128] + own_low,
        pairs[1][:, 128:256] + far_high,
    ]
    planes = [jnp.maximum(t, 0.0).astype(bf).astype(f32) for t in planes]
    for i in range(2):
        total = planes[2 * i] + planes[2 * i + 1]
        for ph in range(2):
            for pw in range(2):
                slabs = [
                    total[((2 * ph + y) * 4 + 2 * pw + x) * 16 :][:16]
                    for y in range(2) for x in range(2)
                ]
                slab = (slabs[0] + slabs[1]) + (slabs[2] + slabs[3])
                pool[1 + i, pl.ds((2 * ph + pw) * 16, 16), :] = (slab * 0.125).astype(bf)

    finish_p = trade_edges(n, pool.at[1], pool.at[2], pool.at[0], pool.at[3], send_p, recv_p)
    w_start(batches[1])
    get_w2.wait()

    def spread_two(at):
        ex2[at] = jnp.dot(pp2[...], pool[at], preferred_element_type=f32).astype(bf)

    def rows_two(at):
        columns = []
        for b in range(3):
            for c in range(3):
                columns.append(
                    jnp.concatenate(
                        [ex2[at, pl.ds(((b + ph) * 4 + c) * 16, 32), :] for ph in range(2)], axis=0
                    )
                )
        return jnp.concatenate(columns, axis=1)

    def taps_two(at, a):
        return jnp.dot(rows_two(at), w2[a], preferred_element_type=f32)

    spread_two(1)
    spread_two(2)
    both_rows = jnp.concatenate([rows_two(1), rows_two(2)], axis=0)
    skip = jnp.dot(both_rows, w2[1], preferred_element_type=f32)
    inner = [taps_two(2, 2), taps_two(1, 0)]
    finish_p()
    spread_two(0)
    spread_two(3)
    outer = [taps_two(0, 0), taps_two(3, 2)]
    skip += jnp.concatenate([x + y for x, y in zip(inner, outer)], axis=0)
    skip = jnp.maximum(skip, 0.0).astype(bf)
    skip_all[me] = skip.reshape(skip_all.shape[1:])
    skip = skip.astype(f32)
    slabs = [skip[16 * i : 16 * (i + 1)] for i in range(8)]
    while len(slabs) > 1:
        slabs = [slabs[i] + slabs[i + 1] for i in range(0, len(slabs), 2)]
    pooled_all[me] = (slabs[0] * 0.125).astype(bf)

    gather_a = Gather(n, pooled_all, send_a, recv_a)
    gather_b = Gather(n, deep_all, send_b, recv_b)
    gather_c = Gather(n, deeper_all, send_c, recv_c)
    gather_s = Doubling(n, skip_all, send_s, recv_s)
    meet_all()
    gather_a.start()
    gather_s.start()
    w_start(batches[2])
    lanes = Lanes(coarse)
    get_wd.wait()
    get_wdd.wait()
    get_rw.wait()
    gather_a.relay()
    gather_a.finish()
    y = lax.dot_general(
        wd[...], pooled_all[...].reshape(coarse, pooled_all.shape[2]),
        (((1,), (1,)), ((), ())), preferred_element_type=f32,
    )
    deep_all[me] = jnp.maximum(add_taps(lanes, y, part), 0.0).astype(bf)
    gather_b.start()
    gather_s.hop(1)
    w_forward()
    gather_b.relay()
    gather_s.hop(2)
    gather_b.finish()
    y = jnp.dot(
        wdd[...], deep_all[...].reshape(n * part, coarse), preferred_element_type=f32
    )
    deeper_all[me] = jnp.maximum(add_taps(lanes, y, part), 0.0).astype(bf)
    gather_c.start()
    w_finish()
    turn_w()
    gather_s.hop(3)
    gather_c.relay()
    gather_s.hop(4)

    def fine(p, values, inner):
        ys[p] = lax.dot_general(
            wt[:, inner], values, (((1,), (1,)), ((), ())), preferred_element_type=f32
        )

    def tap_of(p, tap):
        return ys[p, outs * tap : outs * (tap + 1), :]

    for p in range(8):
        fine(p, skip_all[:, p].reshape(coarse, skip_all.shape[3]), slice(256, 512))
    from_skip = add_fine_taps(lanes, tap_of, outs)
    gather_c.finish()
    deeper = deeper_all[...].reshape(n * part, coarse).astype(f32).T.astype(bf)
    for p in range(8):
        risen = jnp.dot(deeper, rw[p], preferred_element_type=f32).astype(bf)
        fine(p, risen, slice(0, 256))
    from_risen = add_fine_taps(lanes, tap_of, outs)
    decoded = [jnp.maximum(s + r, 0.0) for s, r in zip(from_skip, from_risen)]
    for half in range(coarse // 128):
        cut = [t[:, 128 * half : 128 * (half + 1)] for t in decoded]
        for j, piece in enumerate(block_transpose(cut, 16)):
            dsend[8 * half + j] = piece.astype(bf)
    d_copies = []
    for k in range(n - 1, 0, -1):
        copy = remote(dsend.at[me ^ k], decoded_all.at[me], send_d.at[k], recv_d.at[k], me ^ k)
        copy.start()
        d_copies.append(copy)
    decoded_all[me] = dsend[me]
    for copy in w_copies:
        copy.wait_send()
    for gather in (gather_a, gather_b, gather_c, gather_s):
        gather.drain()
    for copy in d_copies:
        copy.wait_send()
    for copy in get_wf:
        copy.wait()
    for k in range(1, n):
        slot = decoded_all.at[me ^ k]
        remote(slot, slot, send_d.at[k], recv_d.at[k], me ^ 1).wait_recv()
    decoded = decoded_all[...].reshape(n * outs, 128).astype(f32).T.astype(bf)
    fine_rows = jnp.dot(decoded, wf[...], preferred_element_type=f32).astype(bf)

    def slab(d, y, x):
        p = 4 * (d // 2) + 2 * (y // 2) + x // 2
        tap = 4 * (d % 2) + 2 * (y % 2) + x % 2
        return fine_rows[16 * p : 16 * (p + 1), chans * tap : chans * (tap + 1)]

    def slabs_of(d):
        return jnp.concatenate([slab(d, y, x) for y in range(4) for x in range(4)], axis=0)

    for d in range(0, depth, 2):
        plane = jnp.concatenate([slabs_of(d), slabs_of(d + 1)], axis=1)
        plane = jnp.dot(order[...], plane, preferred_element_type=f32).astype(bf)
        out_ref[d] = plane[:, 0:chans]
        out_ref[d + 1] = plane[:, chans : 2 * chans]


def net(
    volume, first_kernel, second_kernel, deep_kernel, deeper_kernel,
    rise_kernel, decode_kernel, final_kernel,
):
    n = lax.axis_size("sp")
    depth, height, width, chans = volume.shape
    mid = second_kernel.shape[4]
    low = rise_kernel.shape[3]
    part = deep_kernel.shape[4]
    block = decode_kernel.shape[3]
    outs = mid // n
    coarse = 16 * n
    area = height * width
    taps = 27 * outs
    wide = -(-taps // LANES) * LANES
    bf = jnp.bfloat16
    vmem = pltpu.VMEM
    dma = pltpu.SemaphoreType.DMA
    hbm = pl.BlockSpec(memory_space=pltpu.HBM)

    def tap_rows(kernel):
        return jnp.transpose(kernel, (0, 1, 2, 4, 3)).reshape(27 * part, kernel.shape[3])

    return pl.pallas_call(
        functools.partial(net_kernel, n),
        out_shape=jax.ShapeDtypeStruct((depth, area, chans), bf),
        in_specs=[hbm] * 8,
        out_specs=pl.BlockSpec(memory_space=pltpu.VMEM),
        scratch_shapes=[
            vmem((depth, area, chans), bf),
            vmem((2, area, chans), bf),
            vmem((36 * 16, area), bf),
            vmem((16 * 16, area // 4), bf),
            vmem((area, area), bf),
            vmem((18 * chans, 2 * chans), bf),
            vmem((3, 9 * chans, mid), bf),
            vmem((27 * part, mid), bf),
            vmem((27 * part, low), bf),
            vmem((8, low, mid), bf),
            vmem((27, block, mid), bf),
            vmem((mid, 8 * chans), bf),
            vmem((depth + 2, 36 * 16, chans), bf),
            vmem((depth // 2 + 2, area // 4, chans), bf),
            vmem((depth // 2 + 2, 16 * 16, chans), bf),
            vmem((n, 16, mid), bf),
            vmem((n, part, coarse), bf),
            vmem((n, part, coarse), bf),
            vmem((n, 8, 16, mid), bf),
            vmem((n, block, wide), bf),
            vmem((n, block, wide), bf),
            vmem((taps, 2 * mid), bf),
            vmem((8, taps, coarse), jnp.float32),
            vmem((n, outs, 128), bf),
            vmem((n, outs, 128), bf),
            dma((24,)),
            dma((2,)), dma((2,)), dma((2,)), dma((2,)),
            dma((2 * n,)), dma((n,)), dma((2 * n,)), dma((n,)),
            dma((2 * n,)), dma((n,)), dma((2 * n,)), dma((n,)),
            dma((n,)), dma((n,)), dma((n,)), dma((n,)), dma((n,)), dma((n,)),
            pltpu.SemaphoreType.REGULAR((2,)),
        ],
        compiler_params=pltpu.CompilerParams(
            collective_id=2, has_side_effects=True, vmem_limit_bytes=107 << 19
        ),
        name="net",
    )(
        volume.reshape(depth, area, chans),
        first_kernel.reshape(3, 9 * chans, chans),
        second_kernel.reshape(3, 9 * chans, mid),
        tap_rows(deep_kernel),
        tap_rows(deeper_kernel),
        rise_kernel.reshape(8, low, mid),
        decode_kernel.reshape(27, block, mid),
        final_kernel.reshape(8, mid, chans),
    ).reshape(volume.shape)


def split_body(
    volume, first_kernel, second_kernel, deep_kernel, deeper_kernel,
    rise_kernel, decode_kernel, final_kernel,
):
    n = lax.axis_size("sp")
    if n != 16 or lax.axis_size("rep") != 2 or decode_kernel.shape[4] % (16 * n):
        return body(
            volume, first_kernel, second_kernel, deep_kernel, deeper_kernel,
            rise_kernel, decode_kernel, final_kernel,
        )
    return net(
        volume, first_kernel, second_kernel, deep_kernel, deeper_kernel,
        rise_kernel, decode_kernel, final_kernel,
    )


def solution(mesh):
    return jax.shard_map(
        split_body,
        mesh=mesh,
        in_specs=(
            P(("rep", "sp"), None, None, None),
            P(),
            P(),
            P(None, None, None, None, "sp"),
            P(None, None, None, None, "sp"),
            P(),
            P(None, None, None, "sp", None),
            P(),
        ),
        out_specs=P(("rep", "sp"), None, None, None),
        check_vma=False,
    )
```

```python
import functools

import jax
import jax.numpy as jnp
from jax import lax
from jax.experimental import pallas as pl
from jax.experimental.pallas import tpu as pltpu
from jax.sharding import PartitionSpec as P

LANES = 128


def remote(src, dst, send_sem, recv_sem, target):
    return pltpu.make_async_remote_copy(
        src_ref=src, dst_ref=dst, send_sem=send_sem, recv_sem=recv_sem,
        device_id={"sp": target}, device_id_type=pl.DeviceIdType.MESH,
    )


def trade_edges(n, first, last, low, high, send_sem, recv_sem):
    me = lax.axis_index("sp")
    upward = remote(last, low, send_sem.at[0], recv_sem.at[0], lax.rem(me + 1, n))
    downward = remote(first, high, send_sem.at[1], recv_sem.at[1], lax.rem(me + n - 1, n))

    @pl.when(me < n - 1)
    def _():
        upward.start()

    @pl.when(me > 0)
    def _():
        downward.start()

    @pl.when(me == 0)
    def _():
        low[...] = jnp.zeros(low.shape, low.dtype)

    @pl.when(me == n - 1)
    def _():
        high[...] = jnp.zeros(high.shape, high.dtype)

    def finish():
        @pl.when(me > 0)
        def _():
            upward.wait_recv()
            downward.wait_send()

        @pl.when(me < n - 1)
        def _():
            downward.wait_recv()
            upward.wait_send()

    return finish


def greet_neighbours(n):
    me = lax.axis_index("sp")
    barrier = pltpu.get_barrier_semaphore()

    @pl.when(me > 0)
    def _():
        pl.semaphore_signal(
            barrier, inc=1, device_id={"sp": lax.rem(me + n - 1, n)},
            device_id_type=pl.DeviceIdType.MESH,
        )

    @pl.when(me < n - 1)
    def _():
        pl.semaphore_signal(
            barrier, inc=1, device_id={"sp": lax.rem(me + 1, n)},
            device_id_type=pl.DeviceIdType.MESH,
        )

    @pl.when((me > 0) & (me < n - 1))
    def _():
        pl.semaphore_wait(barrier, 2)

    @pl.when((me == 0) | (me == n - 1))
    def _():
        pl.semaphore_wait(barrier, 1)


def first_level_kernel(
    n, depth, height, width,
    volume_ref, weight_ref, out_ref,
    ends, taps, sums, send_a, recv_a, send_b, recv_b,
):
    area = height * width
    chans = volume_ref.shape[2]
    greet_neighbours(n)
    finish = trade_edges(
        n, volume_ref.at[0], volume_ref.at[depth - 1], ends.at[0], ends.at[1], send_a, recv_a
    )
    index = lax.broadcasted_iota(jnp.int32, (area, 1), 0) & (width - 1)
    blank = jnp.zeros((depth + 2, width, 3 * chans), jnp.bfloat16)
    taps[:, 0:width] = blank
    taps[:, area + width : area + 2 * width] = blank

    def spread(at, values):
        taps[at, width : area + width, chans : 2 * chans] = values
        values = values.astype(jnp.float32)
        left = jnp.where(index > 0, pltpu.roll(values, 1, 0), 0.0)
        right = jnp.where(index < width - 1, pltpu.roll(values, area - 1, 0), 0.0)
        taps[at, width : area + width, 0:chans] = left.astype(jnp.bfloat16)
        taps[at, width : area + width, 2 * chans : 3 * chans] = right.astype(jnp.bfloat16)

    for d in range(depth):
        spread(d + 1, volume_ref[d])
    finish()
    spread(0, ends[0])
    spread(depth + 1, ends[1])
    for pair in range(depth // 2):
        total = jnp.zeros((2 * area, weight_ref.shape[3]), jnp.float32)
        for a in range(3):
            for b in range(3):
                block = taps[2 * pair + a : 2 * pair + a + 2, b * width : b * width + area]
                total += jnp.dot(
                    block.reshape(2 * area, 3 * chans), weight_ref[a, b],
                    preferred_element_type=jnp.float32,
                )
        total = jnp.maximum(total, 0.0).astype(jnp.bfloat16).astype(jnp.float32)
        total = total[0:area] + total[area : 2 * area]
        total = total.reshape(height // 2, 2, width, total.shape[1]).sum(axis=1)
        sums[...] = total.reshape(area // 2, total.shape[2])
        total = sums[pl.ds(0, area // 4, 2), :] + sums[pl.ds(1, area // 4, 2), :]
        out_ref[1 + pair] = (total * 0.125).astype(jnp.bfloat16)
    halves = depth // 2
    trade_edges(
        n, out_ref.at[1], out_ref.at[halves], out_ref.at[0], out_ref.at[halves + 1],
        send_b, recv_b,
    )()


def first_level(volume, kernel):
    n = lax.axis_size("sp")
    depth, height, width, chans = volume.shape
    outs = kernel.shape[4]
    area = height * width
    vmem = pl.BlockSpec(memory_space=pltpu.VMEM)
    padded = pl.pallas_call(
        functools.partial(first_level_kernel, n, depth, height, width),
        out_shape=jax.ShapeDtypeStruct((depth // 2 + 2, area // 4, outs), jnp.bfloat16),
        in_specs=[vmem] * 2,
        out_specs=vmem,
        scratch_shapes=[
            pltpu.VMEM((2, area, chans), jnp.bfloat16),
            pltpu.VMEM((depth + 2, area + 2 * width, 3 * chans), jnp.bfloat16),
            pltpu.VMEM((area // 2, outs), jnp.float32),
        ]
        + [pltpu.SemaphoreType.DMA((2,))] * 4,
        compiler_params=pltpu.CompilerParams(
            collective_id=1, has_side_effects=True, vmem_limit_bytes=16 << 20
        ),
        name="first_level",
    )(volume.reshape(depth, area, chans), kernel.reshape(3, 3, 3 * chans, outs))
    return padded.reshape(depth // 2 + 2, height // 2, width // 2, outs)


def conv_depth(padded, kernel):
    result = lax.conv_general_dilated(
        padded[None],
        kernel,
        (1, 1, 1),
        ((0, 0), (1, 1), (1, 1)),
        dimension_numbers=("NDHWC", "DHWIO", "NDHWC"),
        preferred_element_type=jnp.float32,
    )
    return result[0]


def pool_mean(values):
    depth, height, width, chans = values.shape
    blocks = values.astype(jnp.float32).reshape(depth // 2, 2, height // 2, 2, width // 2, 2, chans)
    return jnp.mean(blocks, axis=(1, 3, 5)).astype(jnp.bfloat16)


def up_conv(values, kernel):
    depth, height, width, chans = values.shape
    result = jnp.einsum("dhwi,abcio->dahbwco", values, kernel, preferred_element_type=jnp.float32)
    return result.reshape(2 * depth, 2 * height, 2 * width, kernel.shape[4])


def conv_rows(values, weight_ref, height, width):
    rows = values.shape[0]
    index = lax.broadcasted_iota(jnp.int32, (rows, 1), 0)
    w_at = index & (width - 1)
    h_at = (index >> (width.bit_length() - 1)) & (height - 1)
    part, chans = weight_ref.shape[2:]
    blank = jnp.zeros((LANES - 3 * part, chans), weight_ref.dtype)
    total = jnp.zeros((rows, LANES), jnp.float32)
    for b in range(3):
        for c in range(3):
            shift = width * (b - 1) + (c - 1)
            moved = values if shift == 0 else pltpu.roll(values, (-shift) % rows, 0)
            h_to, w_to = h_at + (b - 1), w_at + (c - 1)
            keep = (h_to >= 0) & (h_to < height) & (w_to >= 0) & (w_to < width)
            moved = jnp.where(keep, moved, 0.0).astype(jnp.bfloat16)
            tap = 3 * b + c
            weight = jnp.concatenate([weight_ref[a, tap] for a in range(3)] + [blank], axis=0)
            total += lax.dot_general(
                moved, weight, (((1,), (1,)), ((), ())), preferred_element_type=jnp.float32
            )
    return total


def bottleneck_kernel(
    n, height, width, part,
    pooled_ref, skip_ref, deep_w_ref, deeper_w_ref, out_ref, near_ref,
    whole, deep_mine, deep_all, packed,
    send_a, recv_a, send_b, recv_b, send_c, recv_c, send_d, recv_d,
):
    me = lax.axis_index("sp")
    area = height * width
    voxels = n * area
    partner = me + 1 - 2 * (me % 2)
    half = n // 2

    barrier = pltpu.get_barrier_semaphore()

    def greet(k, carry):
        pl.semaphore_signal(
            barrier, inc=1, device_id={"sp": lax.rem(me + k, n)},
            device_id_type=pl.DeviceIdType.MESH,
        )
        return carry

    lax.fori_loop(1, n, greet, 0)
    pl.semaphore_wait(barrier, n - 1)

    def gather(mine, everyone, send_sem, recv_sem):
        def slot(source):
            return everyone.at[source]

        def direct(k):
            target = lax.rem(me + 2 * k, n)
            return remote(mine, slot(me), send_sem.at[k], recv_sem.at[me], target)

        def relay(k):
            source = lax.rem(me + 2 * (half - k), n)
            return remote(
                slot(source), slot(source), send_sem.at[half + k], recv_sem.at[source], partner
            )

        def arrival(source):
            return remote(mine, slot(source), send_sem.at[0], recv_sem.at[source], partner)

        def start_direct(k, carry):
            direct(k).start()
            return carry

        to_partner = remote(mine, slot(me), send_sem.at[0], recv_sem.at[me], partner)
        lax.fori_loop(1, half, start_direct, 0)
        to_partner.start()
        everyone[me] = mine[...]

        def pass_on(k, carry):
            arrival(lax.rem(me + 2 * (half - k), n)).wait_recv()
            relay(k).start()
            return carry

        lax.fori_loop(1, half, pass_on, 0)

        def from_partner(k, carry):
            arrival(lax.rem(partner + 2 * (half - k), n)).wait_recv()
            return carry

        lax.fori_loop(0, half, from_partner, 0)

        def finish():
            to_partner.wait_send()

            def sent(k, carry):
                direct(k).wait_send()
                relay(k).wait_send()
                return carry

            lax.fori_loop(1, half, sent, 0)

        return finish

    finish_a = gather(pooled_ref, whole, send_a, recv_a)
    depth = skip_ref.shape[0]
    finish_d = trade_edges(
        n, skip_ref.at[0], skip_ref.at[depth - 1], near_ref.at[0], near_ref.at[1], send_d, recv_d
    )
    lanes = lax.broadcasted_iota(jnp.int32, (1, voxels), 1)
    values = whole[...].astype(jnp.float32).reshape(voxels, pooled_ref.shape[1])
    deep = conv_rows(values, deep_w_ref, height, width).T
    below = jnp.where(lanes >= area, pltpu.roll(deep[0:part], area, 1), 0.0)
    above = jnp.where(
        lanes < voxels - area, pltpu.roll(deep[2 * part : 3 * part], voxels - area, 1), 0.0
    )
    deep = below + deep[part : 2 * part] + above
    deep_mine[...] = jnp.maximum(deep, 0.0).astype(jnp.bfloat16)
    finish_b = gather(deep_mine, deep_all, send_b, recv_b)

    values = deep_all[...].astype(jnp.float32).reshape(n * part, voxels).T
    deeper = conv_rows(values, deeper_w_ref, height, width)
    rows = lax.broadcasted_iota(jnp.int32, (voxels, 1), 0)

    def down(block):
        return jnp.where(rows >= area, pltpu.roll(block, area, 0), 0.0)

    def up(block):
        return jnp.where(rows < voxels - area, pltpu.roll(block, voxels - area, 0), 0.0)

    deeper = (
        down(deeper)
        + pltpu.roll(deeper, LANES - part, 1)
        + up(pltpu.roll(deeper, LANES - 2 * part, 1))
    )
    deeper = jnp.maximum(deeper, 0.0)
    lane = lax.broadcasted_iota(jnp.int32, (1, LANES), 1)
    deeper = jnp.where(
        lane < part,
        down(deeper),
        jnp.where(
            lane < 2 * part,
            pltpu.roll(deeper, part, 1),
            up(pltpu.roll(deeper, 2 * part, 1)),
        ),
    )
    packed[...] = deeper.astype(jnp.bfloat16).reshape(n, area, LANES)

    def deal(k):
        target = lax.rem(me + k, n)
        return remote(packed.at[target], out_ref.at[me], send_c.at[k], recv_c.at[me], target)

    def start_deal(k, carry):
        deal(k).start()
        return carry

    lax.fori_loop(1, n, start_deal, 0)
    out_ref[me] = packed[me]

    def receive(k, carry):
        source = lax.rem(me + k, n)
        remote(
            packed.at[source], out_ref.at[source], send_c.at[k], recv_c.at[source], source
        ).wait_recv()
        return carry

    lax.fori_loop(1, n, receive, 0)

    def sent(k, carry):
        deal(k).wait_send()
        return carry

    lax.fori_loop(1, n, sent, 0)
    finish_a()
    finish_b()
    finish_d()


def out_major(kernel):
    chans, part = kernel.shape[3], kernel.shape[4]
    return jnp.transpose(kernel, (0, 1, 2, 4, 3)).reshape(3, 9, part, chans)


def bottleneck(pooled, skip, deep_kernel, deeper_kernel):
    n = lax.axis_size("sp")
    _, height, width, chans = pooled.shape
    part = deep_kernel.shape[4]
    area = height * width
    voxels = n * area
    vmem = pl.BlockSpec(memory_space=pltpu.VMEM)
    received, near = pl.pallas_call(
        functools.partial(bottleneck_kernel, n, height, width, part),
        out_shape=(
            jax.ShapeDtypeStruct((n, area, LANES), jnp.bfloat16),
            jax.ShapeDtypeStruct((2,) + skip.shape[1:], jnp.bfloat16),
        ),
        in_specs=[vmem] * 4,
        out_specs=(vmem, vmem),
        scratch_shapes=[
            pltpu.VMEM((n, area, chans), jnp.bfloat16),
            pltpu.VMEM((part, voxels), jnp.bfloat16),
            pltpu.VMEM((n, part, voxels), jnp.bfloat16),
            pltpu.VMEM((n, area, LANES), jnp.bfloat16),
        ]
        + [pltpu.SemaphoreType.DMA((n,))] * 6
        + [pltpu.SemaphoreType.DMA((2,))] * 2,
        compiler_params=pltpu.CompilerParams(
            collective_id=0, has_side_effects=True, vmem_limit_bytes=24 << 20
        ),
        name="bottleneck",
    )(pooled.reshape(area, chans), skip, out_major(deep_kernel), out_major(deeper_kernel))
    blocks = received[:, :, : 3 * part].reshape(n, area, 3, part)
    return jnp.transpose(blocks, (2, 1, 0, 3)).reshape(3, height, width, n * part), near


def body(
    volume,
    first_kernel,
    second_kernel,
    deep_kernel,
    deeper_kernel,
    rise_kernel,
    decode_kernel,
    final_kernel,
):
    padded_pool = first_level(volume, first_kernel)
    skip = jax.nn.relu(conv_depth(padded_pool, second_kernel)).astype(jnp.bfloat16)
    pooled_two = pool_mean(skip)
    deeper_near, skip_near = bottleneck(pooled_two, skip, deep_kernel, deeper_kernel)
    padded_skip = jnp.concatenate([skip_near[:1], skip, skip_near[1:]], axis=0)
    risen = up_conv(deeper_near, rise_kernel)[1:-1].astype(jnp.bfloat16)
    padded_joined = jnp.concatenate([risen, padded_skip], axis=3)
    whole_decode_kernel = lax.all_gather(decode_kernel, "sp", axis=3, tiled=True)
    decoded = jax.nn.relu(conv_depth(padded_joined, whole_decode_kernel)).astype(jnp.bfloat16)
    return up_conv(decoded, final_kernel).astype(jnp.bfloat16)


def picks(index, columns):
    lane = lax.broadcasted_iota(jnp.int32, (index.shape[0], columns), 1)
    return jnp.where(lane == index, 1.0, 0.0).astype(jnp.bfloat16)


def spread_matrix():
    row = lax.broadcasted_iota(jnp.int32, (36 * 16, 1), 0)
    slab = row >> 4
    eh = (slab * 43) >> 8
    h = ((row >> 2) & 3) * 4 + eh - 1
    w = (row & 3) * 4 + (slab - 6 * eh) - 1
    inside = (h >= 0) & (h < 16) & (w >= 0) & (w < 16)
    return picks(jnp.where(inside, h * 16 + w, -1), 256)


def spread_matrix_two():
    row = lax.broadcasted_iota(jnp.int32, (16 * 16, 1), 0)
    h = ((row >> 2) & 3) * 2 + (row >> 6) - 1
    w = (row & 3) * 2 + ((row >> 4) & 3) - 1
    inside = (h >= 0) & (h < 8) & (w >= 0) & (w < 8)
    at = (h & 1) * 32 + (w & 1) * 16 + (h >> 1) * 4 + (w >> 1)
    return picks(jnp.where(inside, at, -1), 64)


def gather_matrix():
    row = lax.broadcasted_iota(jnp.int32, (256, 1), 0)
    h, w = row >> 4, row & 15
    return picks((h & 3) * 64 + (w & 3) * 16 + (h >> 2) * 4 + (w >> 2), 256)


def block_transpose(pieces, width):
    pieces = list(pieces)
    count = len(pieces)
    block = lax.broadcasted_iota(jnp.int32, pieces[0].shape, 1) // width
    step = 1
    while step < count:
        low = (block & step) == 0
        for i in range(count):
            if i & step:
                continue
            a, b = pieces[i], pieces[i + step]
            pieces[i] = jnp.where(low, a, pltpu.roll(b, width * step, 1))
            pieces[i + step] = jnp.where(low, pltpu.roll(a, 128 - width * step, 1), b)
        step *= 2
    return pieces


def moved(values, by, keep):
    lanes = values.shape[1]
    return jnp.where(keep, pltpu.roll(values, by % lanes, 1), 0.0)


class Lanes:
    def __init__(self, count):
        lane = lax.broadcasted_iota(jnp.int32, (1, count), 1)
        wc, hc, d = lane & 3, (lane >> 2) & 3, lane >> 4
        top = count // 16 - 1
        self.after = {1: wc > 0, 4: hc > 0, 16: d > 0}
        self.before = {1: wc < 3, 4: hc < 3, 16: d < top}

    def back(self, values, by):
        return moved(values, by, self.after[by])

    def ahead(self, values, by):
        return moved(values, -by, self.before[by])


def add_taps(lanes, y, outs):
    def row(a, b, c):
        at = (9 * a + 3 * b + c) * outs
        return y[at : at + outs]

    def tall(c):
        return jnp.concatenate([row(a, b, c) for b in range(3) for a in range(3)], axis=0)

    y = tall(1) + lanes.back(tall(0), 1) + lanes.ahead(tall(2), 1)
    y = [y[i * 3 * outs : (i + 1) * 3 * outs] for i in range(3)]
    y = y[1] + lanes.back(y[0], 4) + lanes.ahead(y[2], 4)
    y = [y[i * outs : (i + 1) * outs] for i in range(3)]
    return y[1] + lanes.back(y[0], 16) + lanes.ahead(y[2], 16)


def add_fine_taps(lanes, load, outs):
    def pair(zero, one, by):
        even = zero[1] + one[2] + lanes.back(one[0], by)
        odd = one[1] + zero[0] + lanes.ahead(zero[2], by)
        return even, odd

    planes = {}
    for pd in range(2):
        rows = {}
        for ph in range(2):
            def taps(pw):
                p = 4 * pd + 2 * ph + pw
                return [
                    jnp.concatenate(
                        [load(p, 9 * a + 3 * b + c) for b in range(3) for a in range(3)], axis=0
                    )
                    for c in range(3)
                ]

            rows[ph] = pair(taps(0), taps(1), 1)
        for qw in range(2):
            def cut(ph):
                return [rows[ph][qw][i * 3 * outs : (i + 1) * 3 * outs] for i in range(3)]

            planes[pd, qw] = pair(cut(0), cut(1), 4)
    result = [None] * 8
    for qw in range(2):
        for qh in range(2):
            def cut(pd):
                return [planes[pd, qw][qh][i * outs : (i + 1) * outs] for i in range(3)]

            low, high = pair(cut(0), cut(1), 16)
            result[2 * qh + qw] = low
            result[4 + 2 * qh + qw] = high
    return result


class Gather:
    def __init__(self, n, slots, send_sem, recv_sem):
        self.n, self.slots, self.send_sem, self.recv_sem = n, slots, send_sem, recv_sem
        self.me = lax.axis_index("sp")
        self.sent = []
        self.others = list(range(n - 2, 0, -2))

    def send(self, source, target):
        slot = self.slots.at[self.me ^ source]
        copy = remote(
            slot, slot, self.send_sem.at[len(self.sent)], self.recv_sem.at[source ^ target],
            self.me ^ target,
        )
        copy.start()
        self.sent.append(copy)

    def wait(self, source):
        slot = self.slots.at[self.me ^ source]
        remote(slot, slot, self.send_sem.at[0], self.recv_sem.at[source], self.me ^ 1).wait_recv()

    def start(self):
        for k in self.others:
            self.send(0, k)
        self.send(0, 1)

    def relay(self):
        for k in reversed(self.others):
            self.wait(k)
            self.send(k, 1)

    def finish(self):
        for k in range(1, self.n, 2):
            self.wait(k)

    def pass_on(self, source, *targets):
        self.wait(source)
        for target in targets:
            self.send(source, target)

    def drain(self):
        for copy in self.sent:
            copy.wait_send()


class Doubling(Gather):
    def steps(self):
        bits = [1 << i for i in range(self.n.bit_length() - 1)]
        known = [[0]]
        for _ in bits:
            known.append([k | bit for k in known[-1] for bit in bits if bit < (k & -k or self.n)])
        return bits, known

    def start(self):
        bits, _ = self.steps()
        for bit in reversed(bits):
            self.send(0, bit)

    def hop(self, step):
        bits, known = self.steps()
        for k in known[step]:
            self.pass_on(k, *[bit for bit in reversed(bits) if bit < (k & -k)])


def net_kernel(
    n,
    volume_hbm, first_hbm, second_hbm, deep_hbm, deeper_hbm, rise_hbm, decode_hbm, final_hbm,
    out_ref,
    vol, vhalo, pp, pp2, order, wpair, w2, wd, wdd, rw, kloc, wf,
    ex, pool, ex2, pooled_all, deep_all, deeper_all, skip_all,
    wsend, wall, wt, ys, dsend, decoded_all,
    load_sem, send_v, recv_v, send_p, recv_p,
    send_a, recv_a, send_b, recv_b, send_c, recv_c, send_s, recv_s,
    send_w, recv_w, send_f, recv_f, send_d, recv_d, ready,
):
    me = lax.axis_index("sp")
    bf = jnp.bfloat16
    f32 = jnp.float32
    depth = vol.shape[0]
    k1 = first_hbm.shape[1]
    part = wd.shape[0] // 27
    outs = 256 // n
    coarse = 16 * n

    twin = lax.axis_index("rep")
    barrier = pltpu.get_barrier_semaphore()
    plane, columns = (1, 2, 3), (4, 8)

    def say(sem, target):
        pl.semaphore_signal(
            sem, inc=1, device_id={"sp": target}, device_id_type=pl.DeviceIdType.MESH
        )

    corner = ((me % 4 == 0) & (me > 0)) | ((me % 4 == 3) & (me < n - 1))
    beyond = jnp.where(me % 4 == 0, me + n - 1, me + 1) % n
    pl.when(corner)(lambda: say(barrier, beyond))
    for k in columns[::-1] + plane:
        say(barrier, me ^ k)
    pl.semaphore_signal(
        barrier, inc=1, device_id={"rep": 1 - twin, "sp": me},
        device_id_type=pl.DeviceIdType.MESH,
    )

    def meet_near():
        near = len(plane) + len(columns) + 1

        @pl.when(corner)
        def _():
            pl.semaphore_wait(barrier, near + 1)

        @pl.when(jnp.logical_not(corner))
        def _():
            pl.semaphore_wait(barrier, near)

        for k in plane:
            say(ready.at[0], me ^ k)

    def meet_planes():
        pl.semaphore_wait(ready.at[0], len(plane))
        for k in columns:
            say(ready.at[1], me ^ k)

    def meet_all():
        pl.semaphore_wait(ready.at[1], len(columns))

    loads = []

    def load(src, dst):
        copy = pltpu.make_async_copy(src, dst, load_sem.at[len(loads)])
        copy.start()
        loads.append(copy)
        return copy

    get_vol = load(volume_hbm, vol)
    get_k = load(decode_hbm, kloc)
    get_w1 = [
        load(first_hbm.at[1], wpair.at[0:k1, 0:128]),
        load(first_hbm.at[0], wpair.at[0:k1, 128:256]),
        load(first_hbm.at[2], wpair.at[k1 : 2 * k1, 0:128]),
        load(first_hbm.at[1], wpair.at[k1 : 2 * k1, 128:256]),
    ]
    get_w2 = load(second_hbm, w2)
    get_wd = load(deep_hbm, wd)
    get_wdd = load(deeper_hbm, wdd)
    get_rw = load(rise_hbm, rw)
    chans = final_hbm.shape[2]
    get_wf = [load(final_hbm.at[i], wf.at[:, chans * i : chans * (i + 1)]) for i in range(8)]

    def spread(planes, to):
        get = jnp.concatenate(planes, axis=1)
        result = jnp.dot(pp[...], get, preferred_element_type=f32).astype(bf)
        for i, at in enumerate(to):
            ex[at] = result[:, 128 * i : 128 * (i + 1)]

    pp[...] = spread_matrix()
    get_vol.wait()
    for d in range(0, depth, 2):
        spread([vol[d], vol[d + 1]], [d + 1, d + 2])

    meet_near()
    finish_v = trade_edges(
        n, vol.at[0], vol.at[depth - 1], vhalo.at[0], vhalo.at[1], send_v, recv_v
    )
    pp2[...] = spread_matrix_two()
    order[...] = gather_matrix()

    get_k.wait()
    per = 128 // outs
    for half in range(256 // 128):
        for group in range(wsend.shape[2] // 128):
            taps = []
            for i in range(per):
                tap = per * group + i
                if tap < 27:
                    taps.append(kloc[tap, :, 128 * half : 128 * (half + 1)].astype(f32))
                else:
                    taps.append(jnp.zeros((kloc.shape[1], 128), f32))
            for j, piece in enumerate(block_transpose(taps, outs)):
                wsend[per * half + j, :, 128 * group : 128 * (group + 1)] = piece.astype(bf)

    w_copies = []

    def w_piece(k):
        return remote(wsend.at[me ^ k], wall.at[me], send_w.at[k], recv_w.at[k], me ^ k)

    def w_arrived(k):
        slot = wall.at[me ^ k]
        remote(slot, slot, send_w.at[k], recv_w.at[k], me ^ 1).wait_recv()

    def w_start(batch):
        for k in [2 * i + twin for i in batch] if batch else [1]:
            copy = w_piece(k)
            copy.start()
            w_copies.append(copy)

    def w_forward():
        for i in range(1, n // 2):
            k = 2 * i + twin
            w_arrived(k)
            slot = wall.at[me ^ k]
            copy = pltpu.make_async_remote_copy(
                src_ref=slot, dst_ref=slot, send_sem=send_f.at[i], recv_sem=recv_f.at[i],
                device_id={"rep": 1 - twin, "sp": me}, device_id_type=pl.DeviceIdType.MESH,
            )
            copy.start()
            w_copies.append(copy)

    def w_finish():
        w_arrived(1)
        for i in range(1, n // 2):
            slot = wall.at[me ^ (2 * i + 1 - twin)]
            pltpu.make_async_remote_copy(
                src_ref=slot, dst_ref=slot, send_sem=send_f.at[i], recv_sem=recv_f.at[i],
                device_id={"rep": 1 - twin, "sp": me}, device_id_type=pl.DeviceIdType.MESH,
            ).wait_recv()

    batches = [[5], [4, 3, 2, 1], [7, 6]]
    w_start([])
    wall[me] = wsend[me]

    def taken(at, b):
        columns = []
        for c in range(3):
            columns.append(
                jnp.concatenate(
                    [ex[at, pl.ds(((b + hm) * 6 + c) * 16, 64), :] for hm in range(4)], axis=0
                )
            )
        return columns

    def rows_of(at):
        return jnp.concatenate(sum([taken(at, b) for b in range(3)], []), axis=1)

    for copy in get_w1:
        copy.wait()

    def both(at):
        left = jnp.concatenate([rows_of(at), rows_of(at + 1)], axis=1)
        return jnp.dot(left, wpair[...], preferred_element_type=f32)

    pairs = [both(1), both(3)]
    own_low = jnp.dot(rows_of(2), wpair[0:k1, 128:256], preferred_element_type=f32)
    own_high = jnp.dot(rows_of(3), wpair[k1 : 2 * k1, 0:128], preferred_element_type=f32)
    def turn_w():
        for at in range(0, wt.shape[1], 128):
            block = wall[pl.ds(at // part, 128 // part)].reshape(128, wall.shape[2])
            wt[:, at : at + 128] = block.astype(f32).T.astype(bf)[0 : wt.shape[0]]

    meet_planes()
    w_start(batches[0])
    finish_v()
    spread([vhalo[0], vhalo[1]], [0, depth + 1])
    far_low = jnp.dot(rows_of(0), wpair[0:k1, 128:256], preferred_element_type=f32)
    far_high = jnp.dot(rows_of(5), wpair[k1 : 2 * k1, 0:128], preferred_element_type=f32)
    planes = [
        pairs[0][:, 0:128] + far_low,
        pairs[0][:, 128:256] + own_high,
        pairs[1][:, 0:128] + own_low,
        pairs[1][:, 128:256] + far_high,
    ]
    planes = [jnp.maximum(t, 0.0).astype(bf).astype(f32) for t in planes]
    for i in range(2):
        total = planes[2 * i] + planes[2 * i + 1]
        for ph in range(2):
            for pw in range(2):
                slabs = [
                    total[((2 * ph + y) * 4 + 2 * pw + x) * 16 :][:16]
                    for y in range(2) for x in range(2)
                ]
                slab = (slabs[0] + slabs[1]) + (slabs[2] + slabs[3])
                pool[1 + i, pl.ds((2 * ph + pw) * 16, 16), :] = (slab * 0.125).astype(bf)

    finish_p = trade_edges(n, pool.at[1], pool.at[2], pool.at[0], pool.at[3], send_p, recv_p)
    w_start(batches[1])
    get_w2.wait()

    def spread_two(at):
        ex2[at] = jnp.dot(pp2[...], pool[at], preferred_element_type=f32).astype(bf)

    def rows_two(a):
        columns = []
        for b in range(3):
            for c in range(3):
                columns.append(
                    jnp.concatenate(
                        [
                            ex2[a + i, pl.ds(((b + ph) * 4 + c) * 16, 32), :]
                            for i in range(2) for ph in range(2)
                        ],
                        axis=0,
                    )
                )
        return jnp.concatenate(columns, axis=1)

    spread_two(1)
    spread_two(2)
    skip = jnp.dot(rows_two(1), w2[1], preferred_element_type=f32)
    finish_p()
    spread_two(0)
    spread_two(3)
    skip += jnp.dot(rows_two(0), w2[0], preferred_element_type=f32)
    skip += jnp.dot(rows_two(2), w2[2], preferred_element_type=f32)
    skip = jnp.maximum(skip, 0.0).astype(bf)
    skip_all[me] = skip.reshape(skip_all.shape[1:])
    skip = skip.astype(f32)
    slabs = [skip[16 * i : 16 * (i + 1)] for i in range(8)]
    while len(slabs) > 1:
        slabs = [slabs[i] + slabs[i + 1] for i in range(0, len(slabs), 2)]
    pooled_all[me] = (slabs[0] * 0.125).astype(bf)

    gather_a = Gather(n, pooled_all, send_a, recv_a)
    gather_b = Gather(n, deep_all, send_b, recv_b)
    gather_c = Gather(n, deeper_all, send_c, recv_c)
    gather_s = Doubling(n, skip_all, send_s, recv_s)
    meet_all()
    gather_a.start()
    gather_s.start()
    w_start(batches[2])
    lanes = Lanes(coarse)
    get_wd.wait()
    get_wdd.wait()
    get_rw.wait()
    gather_a.relay()
    gather_a.finish()
    y = lax.dot_general(
        wd[...], pooled_all[...].reshape(coarse, pooled_all.shape[2]),
        (((1,), (1,)), ((), ())), preferred_element_type=f32,
    )
    deep_all[me] = jnp.maximum(add_taps(lanes, y, part), 0.0).astype(bf)
    gather_b.start()
    gather_s.hop(1)
    w_forward()
    gather_b.relay()
    gather_s.hop(2)
    gather_b.finish()
    y = jnp.dot(
        wdd[...], deep_all[...].reshape(n * part, coarse), preferred_element_type=f32
    )
    deeper_all[me] = jnp.maximum(add_taps(lanes, y, part), 0.0).astype(bf)
    gather_c.start()
    w_finish()
    turn_w()
    gather_s.hop(3)
    gather_c.relay()
    gather_s.hop(4)

    def fine(p, values, inner):
        ys[p] = lax.dot_general(
            wt[:, inner], values, (((1,), (1,)), ((), ())), preferred_element_type=f32
        )

    def tap_of(p, tap):
        return ys[p, outs * tap : outs * (tap + 1), :]

    for p in range(8):
        fine(p, skip_all[:, p].reshape(coarse, skip_all.shape[3]), slice(256, 512))
    from_skip = add_fine_taps(lanes, tap_of, outs)
    gather_c.finish()
    deeper = deeper_all[...].reshape(n * part, coarse).astype(f32).T.astype(bf)
    for p in range(8):
        risen = jnp.dot(deeper, rw[p], preferred_element_type=f32).astype(bf)
        fine(p, risen, slice(0, 256))
    from_risen = add_fine_taps(lanes, tap_of, outs)
    decoded = [jnp.maximum(s + r, 0.0) for s, r in zip(from_skip, from_risen)]
    for half in range(coarse // 128):
        cut = [t[:, 128 * half : 128 * (half + 1)] for t in decoded]
        for j, piece in enumerate(block_transpose(cut, 16)):
            dsend[8 * half + j] = piece.astype(bf)
    d_copies = []
    for k in range(n - 1, 0, -1):
        copy = remote(dsend.at[me ^ k], decoded_all.at[me], send_d.at[k], recv_d.at[k], me ^ k)
        copy.start()
        d_copies.append(copy)
    decoded_all[me] = dsend[me]
    for copy in w_copies:
        copy.wait_send()
    for gather in (gather_a, gather_b, gather_c, gather_s):
        gather.drain()
    for copy in d_copies:
        copy.wait_send()
    for copy in get_wf:
        copy.wait()
    for k in range(1, n):
        slot = decoded_all.at[me ^ k]
        remote(slot, slot, send_d.at[k], recv_d.at[k], me ^ 1).wait_recv()
    decoded = decoded_all[...].reshape(n * outs, 128).astype(f32).T.astype(bf)
    fine_rows = jnp.dot(decoded, wf[...], preferred_element_type=f32).astype(bf)

    def slab(d, y, x):
        p = 4 * (d // 2) + 2 * (y // 2) + x // 2
        tap = 4 * (d % 2) + 2 * (y % 2) + x % 2
        return fine_rows[16 * p : 16 * (p + 1), chans * tap : chans * (tap + 1)]

    def slabs_of(d):
        return jnp.concatenate([slab(d, y, x) for y in range(4) for x in range(4)], axis=0)

    for d in range(0, depth, 2):
        plane = jnp.concatenate([slabs_of(d), slabs_of(d + 1)], axis=1)
        plane = jnp.dot(order[...], plane, preferred_element_type=f32).astype(bf)
        out_ref[d] = plane[:, 0:chans]
        out_ref[d + 1] = plane[:, chans : 2 * chans]


def net(
    volume, first_kernel, second_kernel, deep_kernel, deeper_kernel,
    rise_kernel, decode_kernel, final_kernel,
):
    n = lax.axis_size("sp")
    depth, height, width, chans = volume.shape
    mid = second_kernel.shape[4]
    low = rise_kernel.shape[3]
    part = deep_kernel.shape[4]
    block = decode_kernel.shape[3]
    outs = mid // n
    coarse = 16 * n
    area = height * width
    taps = 27 * outs
    wide = -(-taps // LANES) * LANES
    bf = jnp.bfloat16
    vmem = pltpu.VMEM
    dma = pltpu.SemaphoreType.DMA
    hbm = pl.BlockSpec(memory_space=pltpu.HBM)

    def tap_rows(kernel):
        return jnp.transpose(kernel, (0, 1, 2, 4, 3)).reshape(27 * part, kernel.shape[3])

    return pl.pallas_call(
        functools.partial(net_kernel, n),
        out_shape=jax.ShapeDtypeStruct((depth, area, chans), bf),
        in_specs=[hbm] * 8,
        out_specs=pl.BlockSpec(memory_space=pltpu.VMEM),
        scratch_shapes=[
            vmem((depth, area, chans), bf),
            vmem((2, area, chans), bf),
            vmem((36 * 16, area), bf),
            vmem((16 * 16, area // 4), bf),
            vmem((area, area), bf),
            vmem((18 * chans, 2 * chans), bf),
            vmem((3, 9 * chans, mid), bf),
            vmem((27 * part, mid), bf),
            vmem((27 * part, low), bf),
            vmem((8, low, mid), bf),
            vmem((27, block, mid), bf),
            vmem((mid, 8 * chans), bf),
            vmem((depth + 2, 36 * 16, chans), bf),
            vmem((depth // 2 + 2, area // 4, chans), bf),
            vmem((depth // 2 + 2, 16 * 16, chans), bf),
            vmem((n, 16, mid), bf),
            vmem((n, part, coarse), bf),
            vmem((n, part, coarse), bf),
            vmem((n, 8, 16, mid), bf),
            vmem((n, block, wide), bf),
            vmem((n, block, wide), bf),
            vmem((taps, 2 * mid), bf),
            vmem((8, taps, coarse), jnp.float32),
            vmem((n, outs, 128), bf),
            vmem((n, outs, 128), bf),
            dma((24,)),
            dma((2,)), dma((2,)), dma((2,)), dma((2,)),
            dma((2 * n,)), dma((n,)), dma((2 * n,)), dma((n,)),
            dma((2 * n,)), dma((n,)), dma((2 * n,)), dma((n,)),
            dma((n,)), dma((n,)), dma((n,)), dma((n,)), dma((n,)), dma((n,)),
            pltpu.SemaphoreType.REGULAR((2,)),
        ],
        compiler_params=pltpu.CompilerParams(
            collective_id=2, has_side_effects=True, vmem_limit_bytes=107 << 19
        ),
        name="net",
    )(
        volume.reshape(depth, area, chans),
        first_kernel.reshape(3, 9 * chans, chans),
        second_kernel.reshape(3, 9 * chans, mid),
        tap_rows(deep_kernel),
        tap_rows(deeper_kernel),
        rise_kernel.reshape(8, low, mid),
        decode_kernel.reshape(27, block, mid),
        final_kernel.reshape(8, mid, chans),
    ).reshape(volume.shape)


def split_body(
    volume, first_kernel, second_kernel, deep_kernel, deeper_kernel,
    rise_kernel, decode_kernel, final_kernel,
):
    n = lax.axis_size("sp")
    if n != 16 or lax.axis_size("rep") != 2 or decode_kernel.shape[4] % (16 * n):
        return body(
            volume, first_kernel, second_kernel, deep_kernel, deeper_kernel,
            rise_kernel, decode_kernel, final_kernel,
        )
    return net(
        volume, first_kernel, second_kernel, deep_kernel, deeper_kernel,
        rise_kernel, decode_kernel, final_kernel,
    )


def solution(mesh):
    return jax.shard_map(
        split_body,
        mesh=mesh,
        in_specs=(
            P(("rep", "sp"), None, None, None),
            P(),
            P(),
            P(None, None, None, None, "sp"),
            P(None, None, None, None, "sp"),
            P(),
            P(None, None, None, "sp", None),
            P(),
        ),
        out_specs=P(("rep", "sp"), None, None, None),
        check_vma=False,
    )
```
